32 devices in a mesh: ctx: 8 (over z, x), ch: 4 (over y, core).
Axes of the slice: x: 2, y: 2, z: 4, core: 2. Of those that a mesh axis runs over, the one named last changes fastest.
Arguments:
- short_conv_input: bfloat16 [1024, 1024], P('ctx', 'ch'), may hold values from -6 to 6
- out_gate: bfloat16 [1024, 1024], P('ctx', 'ch'), may hold values from -6 to 6
- in_gate: bfloat16 [1024, 1024], P('ctx', 'ch'), may hold values from -6 to 6
- out_cotangent: bfloat16 [1024, 1024], P('ctx', 'ch'), may hold values from -6 to 6
- mr_filter: bfloat16 [128, 64], P(None, 'ch'), may hold values from -0.5 to 0.5
- residues: float32 [16, 1024], P(None, ('ch', 'ctx')), may hold values from -5 to 5
- rates: float32 [16, 1024], P(None, ('ch', 'ctx')), may hold values from 0.0009765625 to 0.03
Outputs:
- input_grad: bfloat16 [1024, 1024], P('ctx', 'ch')
- out_gate_grad: bfloat16 [1024, 1024], P('ctx', 'ch')
- in_gate_grad: bfloat16 [1024, 1024], P('ctx', 'ch')
- filter_grad: float32 [128, 64], P(None, 'ch')
- residue_grad: float32 [16, 1024], P(None, ('ch', 'ctx'))
- rate_grad: float32 [16, 1024], P(None, ('ch', 'ctx'))
The draws below stay inside these ranges and needn't reach their ends.
All inputs are finite; a program needn't handle non-finite values.
Results may differ from the reference program's by a relative error of at most 0.013.
Values may be sent and summed in bfloat16 or wider, within the bound.
A program may use at most 64 MiB of HBM per device.

```python
import math
import jax
import jax.numpy as jnp
from jax import lax

CHANNELS = 1024
FILTER_TAPS = 128
GROUP = 16
MODES = 16
TOKENS = 1024
GROUPS = 64


def level_of(stream_key, extent, shards, smallest, high):
    gain, own = 1.0, jax.random.fold_in(stream_key, 6)
    for axis_at, blocks in shards:
        heights = jnp.exp(jax.random.uniform(jax.random.fold_in(own, axis_at), (blocks,), jnp.float32, smallest / len(shards), high / len(shards)))
        gain = gain * jnp.repeat(heights, extent[axis_at] // blocks).reshape([-1 if axis == axis_at else 1 for axis in range(len(extent))])
    return gain


def centred(own_key, dims, spread, bound, pieces=(), kind=jnp.bfloat16):
    drawn = spread * jax.random.normal(own_key, dims, jnp.float32)
    if pieces:
        drawn = drawn * level_of(own_key, dims, pieces, -0.22, 0.18)
    return jnp.clip(drawn, -bound, bound).astype(kind)


def setup_inputs(seed: int = 0) -> dict:
    key_of = jax.random.split(jax.random.key(seed), 8)
    short_conv_input = centred(key_of[0], (TOKENS, CHANNELS), 1.0, 6.0, ((0, 8), (1, 4)))
    out_gate = centred(key_of[1], (TOKENS, CHANNELS), 1.0, 6.0, ((0, 8), (1, 4)))
    in_gate = centred(key_of[2], (TOKENS, CHANNELS), 1.0, 6.0, ((0, 8), (1, 4)))
    out_cotangent = centred(key_of[3], (TOKENS, CHANNELS), 1.0, 6.0, ((0, 8), (1, 4)))
    mr_filter = centred(key_of[4], (FILTER_TAPS, GROUPS), FILTER_TAPS ** -0.5, 0.5, ((1, 4),))
    residues = centred(key_of[5], (MODES, CHANNELS), 1.0, 5.0, ((1, 32),), jnp.float32)
    rates = jnp.clip(jnp.exp(math.log(0.03) - 3.424914 * jax.random.uniform(key_of[6], (MODES, CHANNELS), jnp.float32) ** level_of(key_of[6], (MODES, CHANNELS), ((1, 32),), -0.2, 0.2)), 0.0009765625, 0.03)
    return dict(short_conv_input=short_conv_input, out_gate=out_gate, in_gate=in_gate, out_cotangent=out_cotangent, mr_filter=mr_filter, residues=residues, rates=rates)


def reference(short_conv_input, out_gate, in_gate, out_cotangent, mr_filter, residues, rates):
    single_float = jnp.float32
    bf16 = jnp.bfloat16
    length = short_conv_input.shape[0]
    xf = short_conv_input.astype(single_float)
    gfull = jnp.repeat(mr_filter.astype(single_float), GROUP, axis=1)
    xpad = jnp.concatenate([jnp.zeros((FILTER_TAPS, short_conv_input.shape[1]), single_float), xf], axis=0)

    def add_tap(j, total):
        segment_part = lax.dynamic_slice_in_dim(xpad, (FILTER_TAPS - j).astype(jnp.int32), length, 0)
        return total + gfull[j][None, :] * segment_part
    v = lax.fori_loop(jnp.int32(0), jnp.int32(FILTER_TAPS), add_tap, jnp.zeros(short_conv_input.shape, single_float)).astype(bf16)
    u = (in_gate.astype(single_float) * v.astype(single_float)).astype(bf16)
    dz = (out_gate.astype(single_float) * out_cotangent.astype(single_float)).astype(bf16)
    norm = jnp.sqrt(2.0 * rates / MODES)
    weights = residues * norm
    tau = jnp.arange(length).astype(single_float)

    def add_mode(total, pair):
        weight, rate = pair
        return (total + weight[None, :] * jnp.exp(-rate[None, :] * tau[:, None]), None)
    h, _ = lax.scan(add_mode, jnp.zeros(short_conv_input.shape, single_float), (weights, rates))
    size = 2 * length
    hf = jnp.fft.rfft(h, n=size, axis=0)
    uf = jnp.fft.rfft(u.astype(single_float), n=size, axis=0)
    df = jnp.fft.rfft(dz.astype(single_float), n=size, axis=0)
    z = jnp.fft.irfft(hf * uf, n=size, axis=0)[:length].astype(bf16)
    du = jnp.fft.irfft(jnp.conj(hf) * df, n=size, axis=0)[:length].astype(bf16)
    dh = jnp.fft.irfft(jnp.conj(uf) * df, n=size, axis=0)[:length]
    out_gate_grad = (out_cotangent.astype(single_float) * z.astype(single_float)).astype(bf16)
    in_gate_grad = (du.astype(single_float) * v.astype(single_float)).astype(bf16)
    value_grad = (du.astype(single_float) * in_gate.astype(single_float)).astype(bf16)
    value_grad_full = value_grad.astype(single_float)
    value_grad_padded = jnp.concatenate([value_grad_full, jnp.zeros((FILTER_TAPS, short_conv_input.shape[1]), single_float)], axis=0)

    def add_back(j, total):
        segment_part = lax.dynamic_slice_in_dim(value_grad_padded, j.astype(jnp.int32), length, 0)
        return total + gfull[j][None, :] * segment_part
    input_grad = lax.fori_loop(jnp.int32(0), jnp.int32(FILTER_TAPS), add_back, jnp.zeros(short_conv_input.shape, single_float)).astype(bf16)
    scale = 1.0 / jnp.sqrt(jnp.asarray(length, single_float))

    def tap_sum(j):
        segment_part = lax.dynamic_slice_in_dim(xpad, (FILTER_TAPS - j).astype(jnp.int32), length, 0)
        channel_wise = lax.optimization_barrier(jnp.sum(value_grad_full * segment_part, axis=0))
        return lax.optimization_barrier(jnp.sum(channel_wise.reshape(-1, GROUP), axis=1))
    filter_grad = lax.map(tap_sum, jnp.arange(FILTER_TAPS, dtype=jnp.int32)) * scale

    def mode_sums(rate):
        decay = jnp.exp(-rate[None, :] * tau[:, None])
        first = lax.optimization_barrier(jnp.sum(dh * decay, axis=0))
        second = lax.optimization_barrier(jnp.sum(dh * decay * tau[:, None], axis=0))
        return (first, second)
    s1, s2 = lax.map(mode_sums, rates)
    residue_grad = norm * s1 * scale
    rate_grad = weights * (0.5 * s1 - rates * s2) * scale
    return (input_grad, out_gate_grad, in_gate_grad, filter_grad, residue_grad, rate_grad)
```

```python
import functools
import math

import jax
import jax.numpy as jnp
import numpy as np
from jax import lax
from jax.experimental import pallas as pl
from jax.experimental.pallas import tpu as pltpu
from jax.sharding import PartitionSpec as P

MESH = pl.DeviceIdType.MESH
F32, BF16 = jnp.float32, jnp.bfloat16
AXIS = "ctx"
GRANT = 60 * 1024 * 1024


def dft_tables(half):
    size = 2 * half
    k = np.arange(half)[:, None]
    t = np.arange(half)[None, :]
    angle = 2.0 * np.pi * (k * t % size) / size
    real, imag = np.cos(angle), -np.sin(angle)
    imag[0] = np.cos(np.pi * np.arange(half))
    forward = np.concatenate([real, imag], axis=0)
    gain = np.full((size, 1), 2.0 / size)
    gain[0] = gain[half] = 1.0 / size
    inverse = (forward * gain).T

    def split(table):
        table = table.astype(np.float32)
        high = table.astype(BF16)
        return high, (table - high.astype(np.float32)).astype(BF16)

    return np.concatenate(split(forward), axis=1), np.concatenate(split(inverse), axis=0)


def dot(left, right):
    return jnp.dot(left, right, preferred_element_type=F32)


def split(value):
    high = value.astype(BF16)
    return high, (value - high.astype(F32)).astype(BF16)


def product(left, right):
    return (left.astype(F32) * right.astype(F32)).astype(BF16)


def kernel(
    n, x_hbm, og_hbm, ig_hbm, oc_hbm, filt_hbm, res_hbm, rate_hbm, fwd_hbm, inv_hbm,
    xg_ref, ogg_ref, igg_ref, fg_ref, rg_ref, tg_ref, rim, rr_all, d_all, u_all, dv, dv_rim, mp_send, mp_all, fg_all,
    rates, resid, decay, decay_rev, coef, h_ref, d_sum, u_sum, m_sum, dz_ref, u_ref, g_ref,
    back_ref, conv_ref, xs_ref, fs_ref, mr_ref,
    x_ref, og_ref, ig_ref, oc_ref, filt_ref, res_ref, rate_ref, fwd_ref, inv_ref, in_sem,
    rim_sem, rr_send, rr_recv, d_send, d_recv, u_send, u_recv, dv_sem, mp_ssem, mp_rsem, fg_send, fg_recv,
):
    order = (
        (rate_hbm, rate_ref), (res_hbm, res_ref), (x_hbm, x_ref), (filt_hbm, filt_ref), (fwd_hbm, fwd_ref),
        (og_hbm, og_ref), (oc_hbm, oc_ref), (ig_hbm, ig_ref), (inv_hbm, inv_ref),
    )
    loads = [pltpu.make_async_copy(src, dst, in_sem.at[i]) for i, (src, dst) in enumerate(order)]
    for load in loads:
        load.start()
    me = lax.axis_index(AXIS)
    rows, chans = x_ref.shape
    modes, own = rate_ref.shape
    groups = filt_ref.shape[0]
    parts = modes // 8

    barrier = pltpu.get_barrier_semaphore()

    def greet(k, carry):
        pl.semaphore_signal(barrier, inc=1, device_id={AXIS: lax.rem(me + k, n)}, device_id_type=MESH)
        return carry

    lax.fori_loop(1, n, greet, 0)
    loads[0].wait()
    loads[1].wait()
    for g in range(parts):
        rr_all[me, :, g * own : (g + 1) * own] = rate_ref[8 * g : 8 * g + 8, :]
        rr_all[me, :, (parts + g) * own : (parts + g + 1) * own] = res_ref[8 * g : 8 * g + 8, :]
    pl.semaphore_wait(barrier, n - 1)

    def remote(src, dst, ssem, rsem, to):
        return pltpu.make_async_remote_copy(
            src_ref=src, dst_ref=dst, send_sem=ssem, recv_sem=rsem, device_id={AXIS: to}, device_id_type=MESH
        )

    def rr_copy(slot, to):
        return remote(rr_all.at[slot], rr_all.at[slot], rr_send.at[to], rr_recv.at[slot], to)

    def fg_copy(slot, to):
        return remote(fg_all.at[slot], fg_all.at[slot], fg_send.at[to], fg_recv.at[slot], to)

    def mp_copy(slot, to):
        return remote(mp_send.at[to], mp_all.at[slot], mp_ssem.at[to], mp_rsem.at[slot], to)

    def d_copy(slot, to):
        return remote(d_all.at[slot], d_all.at[slot], d_send.at[to], d_recv.at[slot], to)

    def u_copy(slot, to):
        return remote(u_all.at[slot], u_all.at[slot], u_send.at[to], u_recv.at[slot], to)

    def rim_copy(to):
        return remote(x_ref, rim, rim_sem.at[0], rim_sem.at[1], to)

    def dv_copy(to):
        return remote(dv, dv_rim, dv_sem.at[0], dv_sem.at[1], to)

    def others(act):
        def step(k, carry):
            act(lax.rem(me + k, n))
            return carry

        lax.fori_loop(1, n, step, 0)

    def span(lo, hi, act):
        def step(j, carry):
            act(j)
            return carry

        lax.fori_loop(lo, hi, step, 0)

    others(lambda j: rr_copy(me, j).start())
    loads[2].wait()

    @pl.when(me < n - 1)
    def _():
        rim_copy(me + 1).start()

    for load in loads[3:]:
        load.wait()
    fwd = fwd_ref[...]
    fwd_hi = fwd[:, :rows]
    inv_hi = inv_ref[:rows, :]
    inv_lo = inv_ref[rows:, :]
    tau = lax.broadcasted_iota(jnp.int32, (rows, chans), 0)
    first_row = tau == 0
    sign = (1 - 2 * lax.rem(lax.broadcasted_iota(jnp.int32, (2 * rows, chans), 0), 2)).astype(F32)

    def spectrum(value):
        return dot(fwd, jnp.concatenate([value, value], axis=0))

    def signal(spec):
        high, low = split(spec)
        return dot(inv_hi, high) + dot(inv_hi, low) + dot(inv_lo, high)

    def times(a, b, conj):
        ar, ai, br, bi = a[:rows], a[rows:], b[:rows], b[rows:]
        pure = ai * bi
        cross = jnp.where(first_row, 0.0, pure)
        if conj:
            return jnp.concatenate([ar * br + cross, jnp.where(first_row, pure, ar * bi - ai * br)], axis=0)
        return jnp.concatenate([ar * br - cross, jnp.where(first_row, pure, ar * bi + ai * br)], axis=0)

    member = (
        lax.broadcasted_iota(jnp.int32, (groups, chans), 1) // (chans // groups)
        == lax.broadcasted_iota(jnp.int32, (groups, chans), 0)
    ).astype(BF16)
    taps = lax.dot_general(
        filt_ref[...], member, (((0,), (0,)), ((), ())), preferred_element_type=F32
    ).astype(BF16)
    fs_ref[...] = spectrum(taps)
    dz = product(og_ref[...], oc_ref[...])
    dz_ref[...] = dz.astype(F32)
    xs_ref[...] = spectrum(x_ref[...])

    others(lambda j: rr_copy(j, j).wait_recv())
    for j in range(n):
        piece = rr_all[j]
        for g in range(parts):
            rates[8 * g : 8 * g + 8, j * own : (j + 1) * own] = piece[:, g * own : (g + 1) * own]
            resid[8 * g : 8 * g + 8, j * own : (j + 1) * own] = piece[:, (parts + g) * own : (parts + g + 1) * own]

    norm = jnp.sqrt(2.0 * rates[...] / modes)
    resid[...] = resid[...] * norm
    tiles = rows // 8
    low = lax.broadcasted_iota(jnp.int32, (8, chans), 0).astype(F32)
    high = 7.0 - low
    batch = 4

    def put_moments(sums, m, first, second):
        sums[pl.ds(m, 1), :] = jnp.sum(first, axis=0, keepdims=True)
        sums[pl.ds(modes + m, 1), :] = jnp.sum(second, axis=0, keepdims=True)

    def build(group, carry):
        for i in range(batch):
            m = group * batch + i
            rate = jnp.broadcast_to(rates[pl.ds(m, 1), :], (8, chans))
            hop = jnp.exp(-8.0 * rate)
            e = jnp.exp(-rate * low)
            e_rev = jnp.exp(-rate * high)
            first = run = jnp.zeros((8, chans), F32)
            for t in range(tiles):
                decay[m, 8 * t : 8 * t + 8, :] = e
                decay_rev[m, rows - 8 * t - 8 : rows - 8 * t, :] = e_rev
                first += e * dz_ref[8 * t : 8 * t + 8, :]
                if t < tiles - 1:
                    run += first
                    e, e_rev = e * hop, e_rev * hop
            put_moments(d_sum, m, first, 8.0 * ((tiles - 1) * first - run) + low * first)
        return carry

    lax.fori_loop(0, modes // batch, build, 0)

    def moments(sums, table, value, back):
        def step(group, carry):
            first = [jnp.zeros((8, chans), F32)] * batch
            run = list(first)
            for t in range(tiles):
                part = value[8 * t : 8 * t + 8, :]
                for i in range(batch):
                    first[i] += table[group * batch + i, 8 * t : 8 * t + 8, :] * part
                    if t < tiles - 1:
                        run[i] += first[i]
            for i in range(batch):
                if back:
                    second = 8.0 * run[i] + high * first[i]
                else:
                    second = 8.0 * ((tiles - 1) * first[i] - run[i]) + low * first[i]
                put_moments(sums, group * batch + i, first[i], second)
            return carry

        lax.fori_loop(0, modes // batch, step, 0)

    def blend(weight, table, at):
        parts = [weight[m : m + 1, :] * table[m, at, :] for m in range(modes)]
        while len(parts) > 1:
            parts = [left + right for left, right in zip(parts[::2], parts[1::2])]
        return parts[0]

    def blocks(act):
        def step(i, carry):
            act(pl.ds(pl.multiple_of(16 * i, 16), 16))
            return carry

        lax.fori_loop(0, rows // 16, step, 0)

    d_all[me] = d_sum[:modes, :].astype(BF16)
    span(0, me, lambda j: d_copy(me, j).start())

    @pl.when(me == 0)
    def _():
        rim[...] = jnp.zeros_like(rim)

    @pl.when(me > 0)
    def _():
        rim_copy(me).wait_recv()

    xs = xs_ref[...] + sign * spectrum(rim[...])
    xs_ref[...] = xs
    mr = signal(times(fs_ref[...], xs, False)).astype(BF16)
    mr_ref[...] = mr
    u = product(ig_ref[...], mr)
    u_ref[...] = u.astype(F32)

    moments(u_sum, decay_rev, u_ref, True)
    u_all[me] = u_sum[:modes, :].astype(BF16)
    span(me + 1, n, lambda j: u_copy(me, j).start())

    def fill(at):
        h_ref[at, :] = blend(resid, decay, at)

    blocks(fill)
    h_hi, h_lo = split(h_ref[...])
    hs = spectrum(h_hi) + dot(fwd_hi, h_lo)
    us = spectrum(u)
    ds = spectrum(dz)
    back_ref[...] = signal(times(hs, ds, True))
    g_ref[...] = signal(times(us, ds, True))
    moments(m_sum, decay, g_ref, False)

    step_decay = jnp.exp(-rates[...])
    jump = jnp.exp(-rates[...] * rows)

    span(me + 1, n, lambda j: d_copy(j, j).wait_recv())
    later = lax.fori_loop(
        0, n - 1 - me, lambda i, b: b * jump + d_all[n - 1 - i].astype(F32), jnp.zeros((modes, chans), F32)
    )
    coef[...] = resid[...] * step_decay * later

    def gates(at):
        back = (back_ref[at, :] + blend(coef, decay_rev, at)).astype(BF16)
        dv[at, :] = product(back, ig_ref[at, :])
        igg_ref[at, :] = product(back, mr_ref[at, :])

    blocks(gates)

    @pl.when(me > 0)
    def _():
        dv_copy(me - 1).start()

    dvs = spectrum(dv[...])
    c_hi, c_lo = split(signal(times(xs_ref[...], dvs, True)))
    nt = (((1,), (1,)), ((), ()))
    fg_all[me] = (
        lax.dot_general(member, c_hi, nt, preferred_element_type=F32)
        + lax.dot_general(member, c_lo, nt, preferred_element_type=F32)
    ).astype(BF16)
    others(lambda j: fg_copy(me, j).start())

    conv_ref[...] = signal(times(hs, us, False))
    span(0, me, lambda j: u_copy(j, j).wait_recv())

    def prior(j, carry):
        s, far = carry
        return s * jump + u_all[j].astype(F32), (far + s) * jump

    zero = jnp.zeros((modes, chans), F32)
    s, far = lax.fori_loop(0, me, prior, (zero, zero))
    s = s * step_decay
    d0, d1 = d_sum[:modes, :], d_sum[modes:, :]
    m_sum[:modes, :] += s * d0
    m_sum[modes:, :] += s * (d0 + d1) + step_decay * (rows * far * d0 + u_sum[modes:, :] * later)
    for j in range(n):
        for g in range(2 * parts):
            mp_send[j, :, g * own : (g + 1) * own] = m_sum[8 * g : 8 * g + 8, j * own : (j + 1) * own]
    mp_all[me] = mp_send[me]
    others(lambda j: mp_copy(me, j).start())

    coef[...] = resid[...] * s

    def emit(at):
        conv = (conv_ref[at, :] + blend(coef, decay, at)).astype(BF16)
        ogg_ref[at, :] = product(oc_ref[at, :], conv)

    blocks(emit)

    @pl.when(me == n - 1)
    def _():
        dv_rim[...] = jnp.zeros_like(dv_rim)

    @pl.when(me < n - 1)
    def _():
        dv_copy(me).wait_recv()

    ws = dvs + sign * spectrum(dv_rim[...])
    xg_ref[...] = signal(times(fs_ref[...], ws, True)).astype(BF16)

    scale = 1.0 / math.sqrt(rows * n)
    others(lambda j: fg_copy(j, j).wait_recv())
    fg_ref[...] = jnp.sum(fg_all[...].astype(F32), axis=0) * scale
    others(lambda j: mp_copy(j, j).wait_recv())
    total = jnp.sum(mp_all[...], axis=0)
    for g in range(parts):
        rate = rate_ref[8 * g : 8 * g + 8, :]
        gain = jnp.sqrt(2.0 * rate / modes)
        first = total[:, g * own : (g + 1) * own]
        second = total[:, (parts + g) * own : (parts + g + 1) * own]
        rg_ref[8 * g : 8 * g + 8, :] = gain * first * scale
        tg_ref[8 * g : 8 * g + 8, :] = res_ref[8 * g : 8 * g + 8, :] * gain * (0.5 * first - rate * second) * scale

    others(lambda j: rr_copy(me, j).wait_send())
    others(lambda j: fg_copy(me, j).wait_send())
    others(lambda j: mp_copy(me, j).wait_send())
    span(0, me, lambda j: d_copy(me, j).wait_send())
    span(me + 1, n, lambda j: u_copy(me, j).wait_send())

    @pl.when(me < n - 1)
    def _():
        rim_copy(me + 1).wait_send()

    @pl.when(me > 0)
    def _():
        dv_copy(me - 1).wait_send()


def store(*refs):
    count = (len(refs) - 1) // 2
    gives = [pltpu.make_async_copy(refs[i], refs[count + i], refs[-1].at[i]) for i in range(count)]
    for give in gives:
        give.start()
    for give in gives:
        give.wait()


def local(x, og, ig, oc, filt, res, rate):
    n = lax.axis_size(AXIS)
    rows, chans = x.shape
    modes, own = rate.shape
    groups = filt.shape[1]
    assert rows == filt.shape[0] and modes & (modes - 1) == 0 and 2 * (modes // 8) * own <= 128 and modes % 8 == 0
    fwd, inv = dft_tables(rows)
    hbm = pl.BlockSpec(memory_space=pltpu.HBM)
    vmem = pl.BlockSpec(memory_space=pltpu.VMEM)
    wide = (rows, chans)
    dma = pltpu.SemaphoreType.DMA
    out = pl.pallas_call(
        functools.partial(kernel, n),
        name="mixer",
        out_shape=(
            pltpu.VMEM(wide, BF16),
            pltpu.VMEM(wide, BF16),
            pltpu.VMEM(wide, BF16),
            pltpu.VMEM((groups, rows), F32),
            pltpu.VMEM((modes, own), F32),
            pltpu.VMEM((modes, own), F32),
        ),
        in_specs=[hbm] * 9,
        out_specs=(vmem,) * 6,
        scratch_shapes=[
            pltpu.VMEM(wide, BF16),
            pltpu.VMEM((n, 8, 128), F32),
            pltpu.VMEM((n, modes, chans), BF16),
            pltpu.VMEM((n, modes, chans), BF16),
            pltpu.VMEM(wide, BF16),
            pltpu.VMEM(wide, BF16),
            pltpu.VMEM((n, 8, 128), F32),
            pltpu.VMEM((n, 8, 128), F32),
            pltpu.VMEM((n, groups, rows), BF16),
            pltpu.VMEM((modes, chans), F32),
            pltpu.VMEM((modes, chans), F32),
            pltpu.VMEM((modes,) + wide, F32),
            pltpu.VMEM((modes,) + wide, F32),
            pltpu.VMEM((modes, chans), F32),
            pltpu.VMEM(wide, F32),
            pltpu.VMEM((2 * modes, chans), F32),
            pltpu.VMEM((2 * modes, chans), F32),
            pltpu.VMEM((2 * modes, chans), F32),
            pltpu.VMEM(wide, F32),
            pltpu.VMEM(wide, F32),
            pltpu.VMEM(wide, F32),
            pltpu.VMEM(wide, F32),
            pltpu.VMEM(wide, F32),
            pltpu.VMEM((2 * rows, chans), F32),
            pltpu.VMEM((2 * rows, chans), F32),
            pltpu.VMEM(wide, BF16),
            pltpu.VMEM(wide, BF16), pltpu.VMEM(wide, BF16), pltpu.VMEM(wide, BF16), pltpu.VMEM(wide, BF16),
            pltpu.VMEM((groups, rows), BF16), pltpu.VMEM((modes, own), F32), pltpu.VMEM((modes, own), F32),
            pltpu.VMEM(fwd.shape, BF16), pltpu.VMEM(inv.shape, BF16), dma((9,)),
            dma((2,)), dma((n,)), dma((n,)), dma((n,)), dma((n,)), dma((n,)), dma((n,)), dma((2,)),
            dma((n,)), dma((n,)), dma((n,)), dma((n,)),
        ],
        compiler_params=pltpu.CompilerParams(
            collective_id=0, has_side_effects=True, vmem_limit_bytes=GRANT
        ),
    )(x, og, ig, oc, filt.T, res, rate, jnp.asarray(fwd), jnp.asarray(inv))
    xg, ogg, igg, fg, rg, tg = pl.pallas_call(
        store,
        name="store",
        out_shape=tuple(jax.ShapeDtypeStruct(o.shape, o.dtype) for o in out),
        in_specs=[vmem] * 6,
        out_specs=(hbm,) * 6,
        scratch_shapes=[dma((6,))],
        compiler_params=pltpu.CompilerParams(vmem_limit_bytes=GRANT),
    )(*[pltpu.with_memory_space_constraint(o, pltpu.VMEM) for o in out])
    return xg, ogg, igg, fg.T, rg, tg


def solution(mesh):
    tokens = P("ctx", "ch")
    shared = P(None, "ch")
    owned = P(None, ("ch", "ctx"))
    return jax.shard_map(
        local,
        mesh=mesh,
        in_specs=(tokens, tokens, tokens, tokens, shared, owned, owned),
        out_specs=(tokens, tokens, tokens, shared, owned, owned),
        check_vma=False,
    )
```

```python
import functools
import math

import jax
import jax.numpy as jnp
import numpy as np
from jax import lax
from jax.experimental import pallas as pl
from jax.experimental.pallas import tpu as pltpu
from jax.sharding import PartitionSpec as P

MESH = pl.DeviceIdType.MESH
F32, BF16 = jnp.float32, jnp.bfloat16
AXIS = "ctx"
GRANT = 60 * 1024 * 1024
RATE_MAX = 0.03


def pair(table):
    table = table.astype(np.float32)
    high = table.astype(BF16)
    return high, (table - high.astype(np.float32)).astype(BF16)


def dft_tables(half):
    size = 2 * half
    k = np.arange(half)[:, None]
    t = np.arange(half)[None, :]
    angle = 2.0 * np.pi * (k * t % size) / size
    real, imag = np.cos(angle), -np.sin(angle)
    imag[0] = np.cos(np.pi * np.arange(half))
    forward = np.concatenate([real, imag], axis=0)
    gain = np.full((size, 1), 2.0 / size)
    gain[0] = gain[half] = 1.0 / size
    inverse = (forward * gain).T
    return (
        np.concatenate(pair(forward), axis=1),
        np.concatenate(pair(inverse), axis=0),
        np.concatenate(pair(inverse.T), axis=1),
    )


def basis(rows):
    t = np.arange(rows)
    probe = np.linspace(0.0, RATE_MAX, 97)[None, :]
    count = 4
    while True:
        j = np.arange(count)
        node = (rows - 1) / 2 * (1.0 - np.cos((2 * j + 1) * np.pi / (2 * count)))
        base = np.ones((rows, count))
        for a in range(count):
            for b in range(count):
                if a != b:
                    base[:, a] *= (t - node[b]) / (node[a] - node[b])
        error = np.abs(base @ np.exp(-probe * node[:, None]) - np.exp(-probe * t[:, None])).max()
        if error < 2.0**-26:
            return node, base
        count += 2


def node_tables(rows):
    node, base = basis(rows)
    count = len(node)
    pad = -count % 16
    moment = np.pad(base.T, ((0, pad), (0, 0)))
    turned = np.pad(base[::-1].T, ((0, pad), (0, 0)))
    lag = np.arange(rows)[:, None] - np.arange(rows)[None, :]
    lower = np.where((lag >= 0)[None], base.T[:, np.abs(lag)], 0.0)
    upper = np.swapaxes(lower, 1, 2)
    wide = np.repeat(np.stack([base, base[::-1]]), 8, axis=2)
    high, low = pair(wide)
    return (
        node,
        np.concatenate(pair(np.concatenate([moment, turned])), axis=1),
        np.concatenate(pair(upper.reshape(count * rows, rows)), axis=1),
        np.concatenate(pair(lower.reshape(count * rows, rows)), axis=1),
        np.concatenate([high, low, high], axis=2),
    )


def dot(left, right):
    return jnp.dot(left, right, preferred_element_type=F32)


def split(value):
    high = value.astype(BF16)
    return high, (value - high.astype(F32)).astype(BF16)


def product(left, right):
    return (left.astype(F32) * right.astype(F32)).astype(BF16)


def twice(value):
    return jnp.concatenate([value, value], axis=0)


def kernel(
    n, node, x_hbm, og_hbm, ig_hbm, oc_hbm, filt_hbm, res_hbm, rate_hbm, dft_hbm, mom_hbm, far_hbm, up_hbm, lo_hbm,
    xg_ref, ogg_ref, igg_ref, fg_ref, rg_ref, tg_ref,
    rim, rr_send, rr_all, du_send, du_all, dv, dv_rim, p_send, p_all, fg_send, fg_all,
    rates, resid, e_ref, h_ref, b_ref, row_ref, far_ref, pb_ref, g_ref,
    back_ref, conv_ref, xs_ref, fs_ref, mr_ref,
    wide_ref, filt_ref, own_ref, dft_ref, mom_ref, ft_ref, up_ref, lo_ref, in_sem,
    rim_sem, dv_sem, all_sem, du_recv,
):
    me = lax.axis_index(AXIS)
    barrier = pltpu.get_barrier_semaphore()

    def others(act):
        def step(k, carry):
            act(lax.rem(me + k, n))
            return carry

        lax.fori_loop(1, n, step, 0)

    def span(lo, hi, act):
        def step(j, carry):
            act(j)
            return carry

        lax.fori_loop(lo, hi, step, 0)

    others(lambda j: pl.semaphore_signal(barrier, inc=1, device_id={AXIS: j}, device_id_type=MESH))

    def load(src, dst, i):
        return pltpu.make_async_copy(src, dst, in_sem.at[i])

    load(rate_hbm, own_ref.at[0], 0).start()
    load(res_hbm, own_ref.at[1], 0).start()
    load(og_hbm, wide_ref.at[0], 1).start()
    load(oc_hbm, wide_ref.at[1], 1).start()
    load(mom_hbm, mom_ref, 2).start()
    load(up_hbm, up_ref, 3).start()
    load(x_hbm, wide_ref.at[2], 4).start()
    load(ig_hbm, wide_ref.at[3], 4).start()
    load(filt_hbm, filt_ref, 5).start()
    load(dft_hbm, dft_ref, 6).start()
    load(far_hbm, ft_ref, 7).start()
    load(lo_hbm, lo_ref, 8).start()
    og_ref, oc_ref, x_ref, ig_ref = (wide_ref.at[i] for i in range(4))
    rate_ref, res_ref = own_ref.at[0], own_ref.at[1]

    rows, chans = x_hbm.shape
    modes, own = rate_hbm.shape
    groups = filt_hbm.shape[0]
    parts = modes // 8
    count = len(node)
    tall = mom_ref.shape[0] // 2

    def remote(src, dst, ssem, rsem, to):
        return pltpu.make_async_remote_copy(
            src_ref=src, dst_ref=dst, send_sem=ssem, recv_sem=rsem, device_id={AXIS: to}, device_id_type=MESH
        )

    def rr_copy(to):
        return remote(rr_send, rr_all.at[me], all_sem.at[0], all_sem.at[1], to)

    def p_copy(to):
        return remote(p_send.at[to], p_all.at[me], all_sem.at[2], all_sem.at[3], to)

    def fg_copy(to):
        return remote(fg_send, fg_all.at[me], all_sem.at[4], all_sem.at[5], to)

    def du_copy(which, slot, to):
        return remote(du_send.at[which], du_all.at[slot], all_sem.at[6], du_recv.at[slot], to)

    def rim_copy(to):
        return remote(x_ref, rim, rim_sem.at[0], rim_sem.at[1], to)

    def dv_copy(to):
        return remote(dv, dv_rim, dv_sem.at[0], dv_sem.at[1], to)

    def take(ref, i):
        part = ref.at[pl.ds(0, n - 1)]
        pltpu.make_async_copy(part, part, all_sem.at[i]).wait()

    p_send[...] = jnp.zeros_like(p_send)
    g_ref[...] = jnp.zeros_like(g_ref)
    load(own_ref, own_ref, 0).wait()
    for g in range(parts):
        rr_send[:, g * own : (g + 1) * own] = rate_ref[8 * g : 8 * g + 8, :]
        rr_send[:, (parts + g) * own : (parts + g + 1) * own] = res_ref[8 * g : 8 * g + 8, :]

    load(wide_ref.at[pl.ds(0, 2)], wide_ref.at[pl.ds(0, 2)], 1).wait()
    load(mom_ref, mom_ref, 2).wait()
    dz2 = twice(product(og_ref[...], oc_ref[...]))
    du_send[0] = dot(mom_ref[:tall, :], dz2).astype(BF16)
    load(up_ref, up_ref, 3).wait()
    for j in range(count):
        b_ref[j] = dot(up_ref[j * rows : (j + 1) * rows, :], dz2)

    load(wide_ref.at[pl.ds(2, 2)], wide_ref.at[pl.ds(2, 2)], 4).wait()
    load(filt_hbm, filt_ref, 5).wait()
    load(dft_hbm, dft_ref, 6).wait()
    load(far_hbm, ft_ref, 7).wait()
    fwd = dft_ref[0]
    inv_hi = dft_ref[1, :rows, :]
    inv_lo = dft_ref[1, rows:, :]
    first_row = lax.broadcasted_iota(jnp.int32, (rows, chans), 0) == 0
    sign = (1 - 2 * lax.rem(lax.broadcasted_iota(jnp.int32, (2 * rows, chans), 0), 2)).astype(F32)

    def spectrum(value):
        return dot(fwd, twice(value))

    def signal(spec):
        high, low = split(spec)
        return dot(inv_hi, high) + dot(inv_hi, low) + dot(inv_lo, high)

    def times(a, b, conj):
        ar, ai, br, bi = a[:rows], a[rows:], b[:rows], b[rows:]
        pure = ai * bi
        cross = jnp.where(first_row, 0.0, pure)
        if conj:
            return jnp.concatenate([ar * br + cross, jnp.where(first_row, pure, ar * bi - ai * br)], axis=0)
        return jnp.concatenate([ar * br - cross, jnp.where(first_row, pure, ar * bi + ai * br)], axis=0)

    member = (
        lax.broadcasted_iota(jnp.int32, (groups, chans), 1) // (chans // groups)
        == lax.broadcasted_iota(jnp.int32, (groups, chans), 0)
    ).astype(BF16)
    taps = lax.dot_general(
        filt_ref[...], member, (((0,), (0,)), ((), ())), preferred_element_type=F32
    ).astype(BF16)
    fs_ref[...] = spectrum(taps)
    xs_ref[...] = spectrum(x_ref[...])

    pl.semaphore_wait(barrier, n - 1)
    others(lambda j: rr_copy(j).start())
    span(0, me, lambda j: du_copy(0, me, j).start())

    @pl.when(me < n - 1)
    def _():
        rim_copy(me + 1).start()

    rr_all[me] = rr_send[...]

    @pl.when(me == 0)
    def _():
        rim[...] = jnp.zeros_like(rim)

    @pl.when(me > 0)
    def _():
        rim_copy(me).wait_recv()

    xs = xs_ref[...] + sign * spectrum(rim[...])
    xs_ref[...] = xs
    mr = signal(times(fs_ref[...], xs, False)).astype(BF16)
    mr_ref[...] = mr
    u = product(ig_ref[...], mr)
    u2 = twice(u)
    state = dot(mom_ref[tall:, :], u2).astype(BF16)
    du_send[1] = state
    span(me + 1, n, lambda j: du_copy(1, me, j).start())
    for j in range(count):
        total = jnp.zeros((8, chans), F32)
        for t in range(rows // 8):
            total += b_ref[j, 8 * t : 8 * t + 8, :] * u[8 * t : 8 * t + 8, :].astype(F32)
        g_ref[j : j + 1, :] = jnp.sum(total, axis=0, keepdims=True)
    lag = g_ref[...].astype(BF16)
    here = du_send[0]
    for j in range(n):
        at = slice(j * own, (j + 1) * own)
        p_send[j, :, :own] = state[:, at]
        p_send[j, :, own : 2 * own] = here[:, at]
        p_send[j, :, 2 * own : 3 * own] = lag[:, at]
    p_all[me] = p_send[me]
    others(lambda j: p_copy(j).start())

    take(rr_all, 1)
    for j in range(n):
        piece = rr_all[j]
        for g in range(parts):
            rates[8 * g : 8 * g + 8, j * own : (j + 1) * own] = piece[:, g * own : (g + 1) * own]
            resid[8 * g : 8 * g + 8, j * own : (j + 1) * own] = piece[:, (parts + g) * own : (parts + g + 1) * own]
    rate = rates[...]
    weight = resid[...] * jnp.sqrt(2.0 * rate / modes)
    resid[...] = weight
    for j in range(count):
        e = jnp.exp(-float(node[j]) * rate)
        e_ref[j] = e
        h_ref[j : j + 1, :] = jnp.sum(weight * e, axis=0, keepdims=True)

    def jump():
        return jnp.exp(-rates[...] * rows)

    def gather(slot, carry):
        row_ref[...] = du_all[slot].astype(F32)
        for j in range(count):
            carry += e_ref[j] * row_ref[j : j + 1, :]
        return carry

    def spread(state, which):
        coef = resid[...] * jnp.exp(-rates[...]) * state
        for j in range(count):
            part = coef * e_ref[j]
            total = part[:8]
            for g in range(1, parts):
                total += part[8 * g : 8 * g + 8]
            pb_ref[8 * j : 8 * j + 8, :] = total
        high, low = split(pb_ref[...])
        far_ref[...] = dot(ft_ref[which], jnp.concatenate([high, high, low], axis=0))

    @pl.when(me == n - 1)
    def _():
        far_ref[...] = jnp.zeros_like(far_ref)

    @pl.when(me < n - 1)
    def _():
        span(me + 1, n, lambda j: du_copy(0, j, j).wait_recv())
        decay = jump()
        spread(
            lax.fori_loop(0, n - 1 - me, lambda i, q: gather(n - 1 - i, q * decay), jnp.zeros((modes, chans), F32)), 1
        )

    def blocks(act):
        step = 32

        def body(i, carry):
            act(pl.ds(pl.multiple_of(step * i, step), step))
            return carry

        lax.fori_loop(0, rows // step, body, 0)

    def gates(at):
        total = far_ref[at, :]
        for j in range(count):
            total += h_ref[j : j + 1, :] * b_ref[j, at, :]
        back = total.astype(BF16)
        dv[at, :] = product(back, ig_ref[at, :])
        igg_ref[at, :] = product(back, mr_ref[at, :])

    blocks(gates)

    @pl.when(me > 0)
    def _():
        dv_copy(me - 1).start()

    dvs = spectrum(dv[...])
    c_hi, c_lo = split(times(xs_ref[...], dvs, True))
    nt = (((1,), (1,)), ((), ()))
    sums = lax.dot_general(member, c_hi, nt, preferred_element_type=F32) + lax.dot_general(
        member, c_lo, nt, preferred_element_type=F32
    )
    both = dot(jnp.concatenate(split(sums), axis=0), dft_ref[2])
    fg_send[...] = (both[:groups, :rows] + both[groups:, :rows] + both[:groups, rows:]).astype(BF16)
    others(lambda j: fg_copy(j).start())
    fg_all[me] = fg_send[...]

    load(lo_hbm, lo_ref, 8).wait()
    conv = jnp.zeros((rows, chans), F32)
    for j in range(count):
        conv += h_ref[j : j + 1, :] * dot(lo_ref[j * rows : (j + 1) * rows, :], u2)
    conv_ref[...] = conv

    @pl.when(me == 0)
    def _():
        far_ref[...] = jnp.zeros_like(far_ref)

    @pl.when(me > 0)
    def _():
        span(0, me, lambda j: du_copy(1, j, j).wait_recv())
        decay = jump()
        spread(lax.fori_loop(0, me, lambda i, s: gather(i, s * decay), jnp.zeros((modes, chans), F32)), 0)

    conv = (conv_ref[...] + far_ref[...]).astype(BF16)
    ogg_ref[...] = product(oc_ref[...], conv)

    take(p_all, 3)
    scale = 1.0 / math.sqrt(rows * n)
    lanes = p_all.shape[2]
    mine = rate_ref[...]
    fold = jnp.concatenate([mine] * (lanes // own), axis=1)
    hop = jnp.exp(-float(rows) * fold)

    def owner(b, carry):
        s, far, first, second, near0, near1 = carry
        row_ref[:, :lanes] = p_all[b].astype(F32)
        zero = one = jnp.zeros((modes, lanes), F32)
        for j in range(count):
            part = jnp.exp(-float(node[j]) * fold) * row_ref[j : j + 1, :lanes]
            zero += part
            one += float(node[j]) * part
        d0 = pltpu.roll(zero, lanes - own, 1)
        d1 = pltpu.roll(one, lanes - own, 1)
        first += d0 * s
        second += (d0 + d1) * s + d0 * far
        return s * hop + zero, (far + rows * s) * hop + one, first, second, near0 + zero, near1 + one

    empty = jnp.zeros((modes, lanes), F32)
    _, _, first, second, near0, near1 = lax.fori_loop(0, n, owner, (empty,) * 6)
    step = jnp.exp(-fold)
    first = (step * first + pltpu.roll(near0, lanes - 2 * own, 1))[:, :own]
    second = (step * second + pltpu.roll(near1, lanes - 2 * own, 1))[:, :own]
    gain = jnp.sqrt(2.0 * mine / modes)
    rg_ref[...] = gain * first * scale
    tg_ref[...] = res_ref[...] * gain * (0.5 * first - mine * second) * scale

    @pl.when(me == n - 1)
    def _():
        dv_rim[...] = jnp.zeros_like(dv_rim)

    @pl.when(me < n - 1)
    def _():
        dv_copy(me).wait_recv()

    ws = dvs + sign * spectrum(dv_rim[...])
    xg_ref[...] = signal(times(fs_ref[...], ws, True)).astype(BF16)

    take(rr_all, 0)
    take(p_all, 2)
    take(du_all, 6)

    @pl.when(me < n - 1)
    def _():
        rim_copy(me + 1).wait_send()

    @pl.when(me > 0)
    def _():
        dv_copy(me - 1).wait_send()

    take(fg_all, 4)
    take(fg_all, 5)
    fg_ref[...] = jnp.sum(fg_all[...].astype(F32), axis=0) * scale


def store(*refs):
    count = (len(refs) - 1) // 2
    gives = [pltpu.make_async_copy(refs[i], refs[count + i], refs[-1].at[i]) for i in range(count)]
    for give in gives:
        give.start()
    for give in gives:
        give.wait()


def local(x, og, ig, oc, filt, res, rate):
    n = lax.axis_size(AXIS)
    rows, chans = x.shape
    modes, own = rate.shape
    groups = filt.shape[1]
    assert rows == filt.shape[0] and modes % 8 == 0 and 2 * (modes // 8) * own <= 128 and 128 % own == 0
    fwd, inv, turn = dft_tables(rows)
    node, mom, up, lo, far = node_tables(rows)
    count = len(node)
    tall = mom.shape[0] // 2
    hbm = pl.BlockSpec(memory_space=pltpu.HBM)
    vmem = pl.BlockSpec(memory_space=pltpu.VMEM)
    wide = (rows, chans)
    dma = pltpu.SemaphoreType.DMA
    out = pl.pallas_call(
        functools.partial(kernel, n, tuple(float(v) for v in node)),
        name="mixer",
        out_shape=(
            pltpu.VMEM(wide, BF16),
            pltpu.VMEM(wide, BF16),
            pltpu.VMEM(wide, BF16),
            pltpu.VMEM((groups, rows), F32),
            pltpu.VMEM((modes, own), F32),
            pltpu.VMEM((modes, own), F32),
        ),
        in_specs=[hbm] * 12,
        out_specs=(vmem,) * 6,
        scratch_shapes=[
            pltpu.VMEM(wide, BF16),
            pltpu.VMEM((8, 128), F32),
            pltpu.VMEM((n, 8, 128), F32),
            pltpu.VMEM((2, tall, chans), BF16),
            pltpu.VMEM((n, tall, chans), BF16),
            pltpu.VMEM(wide, BF16),
            pltpu.VMEM(wide, BF16),
            pltpu.VMEM((n, tall, 128), BF16),
            pltpu.VMEM((n, tall, 128), BF16),
            pltpu.VMEM((groups, rows), BF16),
            pltpu.VMEM((n, groups, rows), BF16),
            pltpu.VMEM((modes, chans), F32),
            pltpu.VMEM((modes, chans), F32),
            pltpu.VMEM((count, modes, chans), F32),
            pltpu.VMEM((tall, chans), F32),
            pltpu.VMEM((count,) + wide, F32),
            pltpu.VMEM((tall, chans), F32),
            pltpu.VMEM(wide, F32),
            pltpu.VMEM((8 * count, chans), F32),
            pltpu.VMEM((tall, chans), F32),
            pltpu.VMEM(wide, F32),
            pltpu.VMEM(wide, F32),
            pltpu.VMEM((2 * rows, chans), F32),
            pltpu.VMEM((2 * rows, chans), F32),
            pltpu.VMEM(wide, BF16),
            pltpu.VMEM((4,) + wide, BF16),
            pltpu.VMEM((groups, rows), BF16),
            pltpu.VMEM((2, modes, own), F32),
            pltpu.VMEM((3, 2 * rows, 2 * rows), BF16),
            pltpu.VMEM(mom.shape, BF16),
            pltpu.VMEM(far.shape, BF16),
            pltpu.VMEM(up.shape, BF16),
            pltpu.VMEM(lo.shape, BF16),
            dma((9,)),
            dma((2,)), dma((2,)), dma((7,)), dma((n,)),
        ],
        compiler_params=pltpu.CompilerParams(
            collective_id=0, has_side_effects=True, vmem_limit_bytes=GRANT
        ),
    )(
        x, og, ig, oc, filt.T, res, rate,
        jnp.asarray(np.stack([fwd, inv, turn])), jnp.asarray(mom), jnp.asarray(far), jnp.asarray(up), jnp.asarray(lo),
    )
    xg, ogg, igg, fg, rg, tg = pl.pallas_call(
        store,
        name="store",
        out_shape=tuple(jax.ShapeDtypeStruct(o.shape, o.dtype) for o in out),
        in_specs=[vmem] * 6,
        out_specs=(hbm,) * 6,
        scratch_shapes=[dma((6,))],
        compiler_params=pltpu.CompilerParams(vmem_limit_bytes=GRANT),
    )(*[pltpu.with_memory_space_constraint(o, pltpu.VMEM) for o in out])
    return xg, ogg, igg, fg.T, rg, tg


def solution(mesh):
    tokens = P("ctx", "ch")
    shared = P(None, "ch")
    owned = P(None, ("ch", "ctx"))
    return jax.shard_map(
        local,
        mesh=mesh,
        in_specs=(tokens, tokens, tokens, tokens, shared, owned, owned),
        out_specs=(tokens, tokens, tokens, shared, owned, owned),
        check_vma=False,
    )
```

```python
import functools
import math

import jax
import jax.numpy as jnp
import numpy as np
from jax import lax
from jax.experimental import pallas as pl
from jax.experimental.pallas import tpu as pltpu
from jax.sharding import PartitionSpec as P

MESH = pl.DeviceIdType.MESH
F32, BF16 = jnp.float32, jnp.bfloat16
AXIS = "ctx"
GRANT = 60 * 1024 * 1024
RATE_MAX = 0.03


def pair(table):
    table = table.astype(np.float32)
    high = table.astype(BF16)
    return high, (table - high.astype(np.float32)).astype(BF16)


def dft_tables(half):
    size = 2 * half
    k = np.arange(half)[:, None]
    t = np.arange(half)[None, :]
    angle = 2.0 * np.pi * (k * t % size) / size
    real, imag = np.cos(angle), -np.sin(angle)
    imag[0] = np.cos(np.pi * np.arange(half))
    forward = np.concatenate([real, imag], axis=0)
    gain = np.full((size, 1), 2.0 / size)
    gain[0] = gain[half] = 1.0 / size
    inverse = (forward * gain).T
    return (
        np.concatenate(pair(forward), axis=1),
        np.concatenate(pair(inverse), axis=0),
        np.concatenate(pair(inverse.T), axis=1),
    )


def basis(rows):
    t = np.arange(rows)
    probe = np.linspace(0.0, RATE_MAX, 97)[None, :]
    count = 4
    while True:
        j = np.arange(count)
        node = (rows - 1) / 2 * (1.0 - np.cos((2 * j + 1) * np.pi / (2 * count)))
        base = np.ones((rows, count))
        for a in range(count):
            for b in range(count):
                if a != b:
                    base[:, a] *= (t - node[b]) / (node[a] - node[b])
        error = np.abs(base @ np.exp(-probe * node[:, None]) - np.exp(-probe * t[:, None])).max()
        if error < 2.0**-23:
            return node, base
        count += 2


def node_tables(rows):
    node, base = basis(rows)
    count = len(node)
    pad = -count % 16
    moment = np.pad(base.T, ((0, pad), (0, 0)))
    turned = np.pad(base[::-1].T, ((0, pad), (0, 0)))
    lag = np.arange(rows)[:, None] - np.arange(rows)[None, :]
    lower = np.where((lag >= 0)[None], base.T[:, np.abs(lag)], 0.0)
    upper = np.swapaxes(lower, 1, 2)
    wide = np.repeat(np.concatenate([base, base[::-1]]), 8, axis=1)
    high, low = pair(wide)
    far = np.concatenate([high, high * 0, high * 0], axis=1)
    far[:, 8 * count : 16 * count], far[:, 16 * count :] = low, high
    far = np.pad(far, ((0, 0), (0, 2 * rows - far.shape[1])))
    return (
        node,
        np.concatenate(pair(np.concatenate([moment, turned])), axis=1),
        np.concatenate(pair(upper.reshape(count * rows, rows)), axis=1),
        np.concatenate(pair(lower.reshape(count * rows, rows)), axis=1),
        far,
    )


def dot(left, right):
    return jnp.dot(left, right, preferred_element_type=F32)


def split(value):
    high = value.astype(BF16)
    return high, (value - high.astype(F32)).astype(BF16)


def product(left, right):
    return (left.astype(F32) * right.astype(F32)).astype(BF16)


def twice(value):
    return jnp.concatenate([value, value], axis=0)


def kernel(
    n, node, x_hbm, og_hbm, ig_hbm, oc_hbm, filt_hbm, res_hbm, rate_hbm, mom_hbm, tab_hbm, lo_hbm,
    xg_ref, ogg_ref, igg_ref, fg_ref, rg_ref, tg_ref,
    rim, rr_send, rr_all, du_send, du_all, dv, dv_rim, p_send, p_all, fg_send, fg_all,
    rates, resid, fold_ref, pf_ref, e_ref, h_ref, b_ref, row_ref, far_ref, pb_ref, g_ref,
    conv_ref, xs_ref, fs_ref, ds_ref, mr_ref, u_ref, back_ref,
    wide_ref, filt_ref, own_ref, mom_ref, tab_ref, lo_ref, unit_ref, in_sem,
    rim_sem, dv_sem, all_sem, du_recv,
):
    me = lax.axis_index(AXIS)
    barrier = pltpu.get_barrier_semaphore()

    def others(act):
        def step(k, carry):
            act(lax.rem(me + k, n))
            return carry

        lax.fori_loop(1, n, step, 0)

    def span(lo, hi, act):
        def step(j, carry):
            act(j)
            return carry

        lax.fori_loop(lo, hi, step, 0)

    others(lambda j: pl.semaphore_signal(barrier, inc=1, device_id={AXIS: j}, device_id_type=MESH))

    def load(src, dst, i):
        return pltpu.make_async_copy(src, dst, in_sem.at[i])

    load(rate_hbm, own_ref.at[0], 0).start()
    load(res_hbm, own_ref.at[1], 0).start()
    load(og_hbm, wide_ref.at[0], 1).start()
    load(oc_hbm, wide_ref.at[1], 1).start()
    load(mom_hbm, mom_ref, 2).start()
    load(tab_hbm, tab_ref, 3).start()
    load(x_hbm, wide_ref.at[2], 4).start()
    load(ig_hbm, wide_ref.at[3], 4).start()
    load(filt_hbm, filt_ref, 5).start()
    load(lo_hbm, lo_ref, 6).start()
    og_ref, oc_ref, x_ref, ig_ref = (wide_ref.at[i] for i in range(4))
    rate_ref, res_ref = own_ref.at[0], own_ref.at[1]

    rows, chans = x_hbm.shape
    modes, own = rate_hbm.shape
    groups = filt_hbm.shape[0]
    parts = modes // 8
    count = len(node)
    tall = mom_ref.shape[0] // 2
    size = 2 * rows
    sides = chans // 128
    crowd = n // sides

    def remote(src, dst, ssem, rsem, to):
        return pltpu.make_async_remote_copy(
            src_ref=src, dst_ref=dst, send_sem=ssem, recv_sem=rsem, device_id={AXIS: to}, device_id_type=MESH
        )

    def rr_copy(to):
        return remote(rr_send, rr_all.at[me], all_sem.at[0], all_sem.at[3 + me // crowd], to)

    def p_copy(to):
        return remote(p_send.at[to], p_all.at[me], all_sem.at[0], all_sem.at[1], to)

    def fg_copy(side, to):
        return remote(fg_send.at[side], fg_all.at[me, side], all_sem.at[0], all_sem.at[2], to)

    def du_copy(which, slot, to):
        return remote(du_send.at[which], du_all.at[slot], all_sem.at[0], du_recv.at[slot], to)

    def rim_copy(to):
        return remote(x_ref, rim, rim_sem.at[0], rim_sem.at[1], to)

    def dv_copy(to):
        return remote(dv, dv_rim, dv_sem.at[0], dv_sem.at[1], to)

    def take(ref, i, many):
        part = ref.at[pl.ds(0, many)]
        pltpu.make_async_copy(part, part, all_sem.at[i]).wait()

    p_send[...] = jnp.zeros_like(p_send)
    g_ref[...] = jnp.zeros_like(g_ref)
    load(own_ref, own_ref, 0).wait()
    for g in range(parts):
        rr_send[:, g * own : (g + 1) * own] = rate_ref[8 * g : 8 * g + 8, :]
        rr_send[:, (parts + g) * own : (parts + g + 1) * own] = res_ref[8 * g : 8 * g + 8, :]

    load(wide_ref.at[pl.ds(0, 2)], wide_ref.at[pl.ds(0, 2)], 1).wait()
    load(mom_ref, mom_ref, 2).wait()
    dz2 = twice(product(og_ref[...], oc_ref[...]))
    du_send[0] = dot(mom_ref[:tall, :], dz2).astype(BF16)
    load(wide_ref.at[pl.ds(2, 2)], wide_ref.at[pl.ds(2, 2)], 4).wait()
    pl.semaphore_wait(barrier, n - 1)
    others(lambda j: rr_copy(j).start())
    span(0, me, lambda j: du_copy(0, me, j).start())

    @pl.when(me < n - 1)
    def _():
        rim_copy(me + 1).start()

    rr_all[me] = rr_send[...]
    load(tab_hbm, tab_ref, 3).wait()
    far_at = 3 * size
    up_at = far_at + size
    for j in range(count):
        b_ref[j] = dot(tab_ref[up_at + j * rows : up_at + (j + 1) * rows, :], dz2)

    load(filt_hbm, filt_ref, 5).wait()
    fwd = tab_ref[:size, :]
    inv_hi = tab_ref[size : size + rows, :]
    inv_lo = tab_ref[size + rows : 2 * size, :]
    sign = (1 - 2 * lax.rem(lax.broadcasted_iota(jnp.int32, (size, chans), 0), 2)).astype(F32)

    def spectrum(value):
        return dot(fwd, twice(value))

    def signal(spec):
        high, low = split(spec)
        return dot(inv_hi, high) + dot(inv_hi, low) + dot(inv_lo, high)

    def times(a, b, conj):
        ar, ai, br, bi = a[:rows], a[rows:], b[:rows], b[rows:]
        first_row = lax.broadcasted_iota(jnp.int32, ai.shape, 0) == 0
        pure = ai * bi
        cross = jnp.where(first_row, 0.0, pure)
        if conj:
            return jnp.concatenate([ar * br + cross, jnp.where(first_row, pure, ar * bi - ai * br)], axis=0)
        return jnp.concatenate([ar * br - cross, jnp.where(first_row, pure, ar * bi + ai * br)], axis=0)

    member = (
        lax.broadcasted_iota(jnp.int32, (groups, chans), 1) // (chans // groups)
        == lax.broadcasted_iota(jnp.int32, (groups, chans), 0)
    ).astype(BF16)
    taps = lax.dot_general(
        filt_ref[...], member, (((0,), (0,)), ((), ())), preferred_element_type=F32
    ).astype(BF16)
    fs_ref[...] = spectrum(taps)
    xs_ref[...] = spectrum(x_ref[...])

    def mix():
        @pl.when(me == 0)
        def _():
            rim[...] = jnp.zeros_like(rim)

        @pl.when(me > 0)
        def _():
            rim_copy(me).wait_recv()

        xs = xs_ref[...] + sign * spectrum(rim[...])
        xs_ref[...] = xs
        mr = signal(times(fs_ref[...], xs, False)).astype(BF16)
        mr_ref[...] = mr
        u = product(ig_ref[...], mr)
        u_ref[...] = u
        u2 = twice(u)
        state = dot(mom_ref[tall:, :], u2).astype(BF16)
        du_send[1] = state
        span(me + 1, n, lambda j: du_copy(1, me, j).start())
        for j in range(count):
            total = jnp.zeros((8, chans), F32)
            for t in range(rows // 8):
                total += b_ref[j, 8 * t : 8 * t + 8, :] * u[8 * t : 8 * t + 8, :].astype(F32)
            g_ref[j : j + 1, :] = jnp.sum(total, axis=0, keepdims=True)
        lag = g_ref[...].astype(BF16)
        here = du_send[0]
        for j in range(n):
            at = slice(j * own, (j + 1) * own)
            p_send[j, :, :own] = state[:, at]
            p_send[j, :, own : 2 * own] = here[:, at]
            p_send[j, :, 2 * own : 3 * own] = lag[:, at]
        p_all[me] = p_send[me]
        others(lambda j: p_copy(j).start())

    mine = rate_ref[...]
    lanes = p_all.shape[2]
    fold = jnp.concatenate([mine] * (lanes // own), axis=1)
    for j in range(count):
        fold_ref[j] = jnp.exp(-float(node[j]) * fold)

    def gather(slot, carry, cols):
        row_ref[:, cols] = du_all[slot, :, cols].astype(F32)
        for j in range(count):
            carry += e_ref[j, :, cols] * row_ref[j : j + 1, cols]
        return carry

    def spread(state, which, cols):
        coef = resid[:, cols] * jnp.exp(-rates[:, cols]) * state
        for j in range(count):
            part = coef * e_ref[j, :, cols]
            total = part[:8]
            for g in range(1, parts):
                total += part[8 * g : 8 * g + 8]
            pb_ref[8 * j : 8 * j + 8, cols] = total
        high, low = split(pb_ref[:, cols])
        stack = [high, high, low]
        spare = size - 3 * high.shape[0]
        if spare:
            stack.append(jnp.zeros((spare, high.shape[1]), BF16))
        table = tab_ref[far_at + which * rows : far_at + (which + 1) * rows, :]
        far_ref[:, cols] = dot(table, jnp.concatenate(stack, axis=0))

    @pl.when(me == n - 1)
    def _():
        far_ref[...] = jnp.zeros_like(far_ref)

    nt = (((1,), (1,)), ((), ()))
    few = groups // sides
    turn = tab_ref[2 * size : 3 * size, :]
    def grad(side):
        cols = slice(128 * side, 128 * side + 128)

        @pl.when(me // crowd == side)
        def _(side=side):
            take(rr_all, 3 + side, crowd - 1)

        @pl.when(me // crowd != side)
        def _(side=side):
            take(rr_all, 3 + side, crowd)

        for j in range(side * crowd, (side + 1) * crowd):
            piece = rr_all[j]
            for g in range(parts):
                at = (slice(8 * g, 8 * g + 8), slice(j * own, (j + 1) * own))
                rates[at] = piece[:, g * own : (g + 1) * own]
                resid[at] = piece[:, (parts + g) * own : (parts + g + 1) * own]
        rate = rates[:, cols]
        weight = resid[:, cols] * jnp.sqrt(2.0 * rate / modes)
        resid[:, cols] = weight
        for j in range(count):
            e = jnp.exp(-float(node[j]) * rate)
            e_ref[j, :, cols] = e
            h_ref[j : j + 1, cols] = jnp.sum(weight * e, axis=0, keepdims=True)

        @pl.when(me < n - 1)
        def _(side=side, cols=cols):
            if side == sides - 1:
                span(me + 1, n, lambda j: du_copy(0, j, j).wait_recv())
            decay = jnp.exp(-rates[:, cols] * rows)
            start = jnp.zeros((modes, 128), F32)
            spread(
                lax.fori_loop(0, n - 1 - me, lambda i, q: gather(n - 1 - i, q * decay, cols), start), 1, cols
            )

        chunk = 32
        for at in range(0, rows, chunk):
            here = slice(at, at + chunk)
            total = far_ref[here, cols]
            for j in range(count):
                total += h_ref[j : j + 1, cols] * b_ref[j, here, cols]
            back = total.astype(BF16)
            back_ref[here, cols] = back
            dv[here, cols] = product(back, ig_ref[here, cols])

    def tap(side):
        cols = slice(128 * side, 128 * side + 128)
        spec = spectrum(dv[:, cols])
        ds_ref[:, cols] = spec
        cross = times(xs_ref[:, cols], spec, True).astype(BF16)
        sums = lax.dot_general(
            member[side * few : (side + 1) * few, cols], cross, nt, preferred_element_type=F32
        )
        both = dot(jnp.concatenate(split(sums), axis=0), turn)
        fg_send[side] = (both[:few, :rows] + both[few:, :rows] + both[:few, rows:]).astype(BF16)
        others(lambda j: fg_copy(side, j).start())

    def hand():
        @pl.when(me > 0)
        def _():
            dv_copy(me - 1).start()

    @pl.when(me >= n // 2)
    def _():
        mix()
        for side in reversed(range(sides)):
            grad(side)
            if side == 0:
                hand()
            tap(side)

    @pl.when(me < n // 2)
    def _():
        for side in reversed(range(sides)):
            grad(side)
        hand()
        mix()
        for side in reversed(range(sides)):
            tap(side)

    fg_all[me] = fg_send[...]
    igg_ref[...] = product(back_ref[...], mr_ref[...])
    u2 = twice(u_ref[...])

    load(lo_hbm, lo_ref, 6).wait()
    conv = jnp.zeros((rows, chans), F32)
    for j in range(count):
        conv += h_ref[j : j + 1, :] * dot(lo_ref[j * rows : (j + 1) * rows, :], u2)
    conv_ref[...] = conv

    @pl.when(me == 0)
    def _():
        far_ref[...] = jnp.zeros_like(far_ref)

    @pl.when(me > 0)
    def _():
        span(0, me, lambda j: du_copy(1, j, j).wait_recv())
        decay = jnp.exp(-rates[...] * rows)
        every = slice(0, chans)
        start = jnp.zeros((modes, chans), F32)
        spread(lax.fori_loop(0, me, lambda i, s: gather(i, s * decay, every), start), 0, every)

    conv = (conv_ref[...] + far_ref[...]).astype(BF16)
    ogg_ref[...] = product(oc_ref[...], conv)

    take(p_all, 1, n - 1)
    scale = 1.0 / math.sqrt(rows * n)
    hop = jnp.exp(-float(rows) * fold)

    for b in range(n):
        pf_ref[b] = p_all[b].astype(F32)

    def owner(b, carry):
        s, far, first, second, near0, near1 = carry
        zero = one = jnp.zeros((modes, lanes), F32)
        for j in range(count):
            part = fold_ref[j] * pf_ref[b, j : j + 1, :]
            zero += part
            one += float(node[j]) * part
        d0 = pltpu.roll(zero, lanes - own, 1)
        d1 = pltpu.roll(one, lanes - own, 1)
        first += d0 * s
        second += (d0 + d1) * s + d0 * far
        return s * hop + zero, (far + rows * s) * hop + one, first, second, near0 + zero, near1 + one

    empty = jnp.zeros((modes, lanes), F32)
    _, _, first, second, near0, near1 = lax.fori_loop(0, n, owner, (empty,) * 6, unroll=8 if n % 8 == 0 else 1)
    step = jnp.exp(-fold)
    first = (step * first + pltpu.roll(near0, lanes - 2 * own, 1))[:, :own]
    second = (step * second + pltpu.roll(near1, lanes - 2 * own, 1))[:, :own]
    gain = jnp.sqrt(2.0 * mine / modes)
    rg_ref[...] = gain * first * scale
    tg_ref[...] = res_ref[...] * gain * (0.5 * first - mine * second) * scale

    @pl.when(me == n - 1)
    def _():
        dv_rim[...] = jnp.zeros_like(dv_rim)

    @pl.when(me < n - 1)
    def _():
        dv_copy(me).wait_recv()

    ws = ds_ref[...] + sign * spectrum(dv_rim[...])
    xg_ref[...] = signal(times(fs_ref[...], ws, True)).astype(BF16)

    pltpu.make_async_copy(unit_ref, unit_ref, all_sem.at[0]).wait()

    @pl.when(me < n - 1)
    def _():
        rim_copy(me + 1).wait_send()

    @pl.when(me > 0)
    def _():
        dv_copy(me - 1).wait_send()

    take(fg_all, 2, n - 1)
    total = jnp.sum(fg_all[...].astype(F32), axis=0) * scale
    for side in range(sides):
        fg_ref[side * few : (side + 1) * few, :] = total[side]


def store(*refs):
    count = (len(refs) - 1) // 2
    gives = [pltpu.make_async_copy(refs[i], refs[count + i], refs[-1].at[i]) for i in range(count)]
    for give in gives:
        give.start()
    for give in gives:
        give.wait()


def local(x, og, ig, oc, filt, res, rate):
    n = lax.axis_size(AXIS)
    rows, chans = x.shape
    modes, own = rate.shape
    groups = filt.shape[1]
    assert rows == filt.shape[0] and modes % 8 == 0 and 2 * (modes // 8) * own <= 128 and 128 % own == 0
    assert chans % 128 == 0 and n % (chans // 128) == 0
    sides = chans // 128
    fwd, inv, turn = dft_tables(rows)
    node, mom, up, lo, far = node_tables(rows)
    count = len(node)
    tall = mom.shape[0] // 2
    tab = np.concatenate([fwd, inv, turn, far, up])
    sent = 4 * 8 * 128 + 2 * (tall * 128 + groups * rows + tall * chans)
    hbm = pl.BlockSpec(memory_space=pltpu.HBM)
    vmem = pl.BlockSpec(memory_space=pltpu.VMEM)
    wide = (rows, chans)
    dma = pltpu.SemaphoreType.DMA
    out = pl.pallas_call(
        functools.partial(kernel, n, tuple(float(v) for v in node)),
        name="mixer",
        out_shape=(
            pltpu.VMEM(wide, BF16),
            pltpu.VMEM(wide, BF16),
            pltpu.VMEM(wide, BF16),
            pltpu.VMEM((groups, rows), F32),
            pltpu.VMEM((modes, own), F32),
            pltpu.VMEM((modes, own), F32),
        ),
        in_specs=[hbm] * 10,
        out_specs=(vmem,) * 6,
        scratch_shapes=[
            pltpu.VMEM(wide, BF16),
            pltpu.VMEM((8, 128), F32),
            pltpu.VMEM((n, 8, 128), F32),
            pltpu.VMEM((2, tall, chans), BF16),
            pltpu.VMEM((n, tall, chans), BF16),
            pltpu.VMEM(wide, BF16),
            pltpu.VMEM(wide, BF16),
            pltpu.VMEM((n, tall, 128), BF16),
            pltpu.VMEM((n, tall, 128), BF16),
            pltpu.VMEM((sides, groups // sides, rows), BF16),
            pltpu.VMEM((n, sides, groups // sides, rows), BF16),
            pltpu.VMEM((modes, chans), F32),
            pltpu.VMEM((modes, chans), F32),
            pltpu.VMEM((count, modes, 128), F32),
            pltpu.VMEM((n, tall, 128), F32),
            pltpu.VMEM((count, modes, chans), F32),
            pltpu.VMEM((tall, chans), F32),
            pltpu.VMEM((count,) + wide, F32),
            pltpu.VMEM((tall, chans), F32),
            pltpu.VMEM(wide, F32),
            pltpu.VMEM((8 * count, chans), F32),
            pltpu.VMEM((tall, chans), F32),
            pltpu.VMEM(wide, F32),
            pltpu.VMEM((2 * rows, chans), F32),
            pltpu.VMEM((2 * rows, chans), F32),
            pltpu.VMEM((2 * rows, chans), F32),
            pltpu.VMEM(wide, BF16),
            pltpu.VMEM(wide, BF16),
            pltpu.VMEM(wide, BF16),
            pltpu.VMEM((4,) + wide, BF16),
            pltpu.VMEM((groups, rows), BF16),
            pltpu.VMEM((2, modes, own), F32),
            pltpu.VMEM(mom.shape, BF16),
            pltpu.VMEM(tab.shape, BF16),
            pltpu.VMEM(lo.shape, BF16),
            pltpu.VMEM((n - 1, sent // 512, 128), F32),
            dma((7,)),
            dma((2,)), dma((2,)), dma((3 + sides,)), dma((n,)),
        ],
        compiler_params=pltpu.CompilerParams(
            collective_id=0, has_side_effects=True, vmem_limit_bytes=GRANT
        ),
    )(
        x, og, ig, oc, filt.T, res, rate,
        jnp.asarray(mom), jnp.asarray(tab), jnp.asarray(lo),
    )
    xg, ogg, igg, fg, rg, tg = pl.pallas_call(
        store,
        name="store",
        out_shape=tuple(jax.ShapeDtypeStruct(o.shape, o.dtype) for o in out),
        in_specs=[vmem] * 6,
        out_specs=(hbm,) * 6,
        scratch_shapes=[dma((6,))],
        compiler_params=pltpu.CompilerParams(vmem_limit_bytes=GRANT),
    )(*[pltpu.with_memory_space_constraint(o, pltpu.VMEM) for o in out])
    return xg, ogg, igg, fg.T, rg, tg


def solution(mesh):
    tokens = P("ctx", "ch")
    shared = P(None, "ch")
    owned = P(None, ("ch", "ctx"))
    return jax.shard_map(
        local,
        mesh=mesh,
        in_specs=(tokens, tokens, tokens, tokens, shared, owned, owned),
        out_specs=(tokens, tokens, tokens, shared, owned, owned),
        check_vma=False,
    )
```

```python
import functools
import math

import jax
import jax.numpy as jnp
import numpy as np
from jax import lax
from jax.experimental import pallas as pl
from jax.experimental.pallas import tpu as pltpu
from jax.sharding import PartitionSpec as P

MESH = pl.DeviceIdType.MESH
F32, BF16 = jnp.float32, jnp.bfloat16
AXIS = "ctx"
GRANT = 60 * 1024 * 1024
RATE_MAX = 0.03


def pair(table):
    table = table.astype(np.float32)
    high = table.astype(BF16)
    return high, (table - high.astype(np.float32)).astype(BF16)


def dft_tables(half):
    size = 2 * half
    k = np.arange(half)[:, None]
    t = np.arange(half)[None, :]
    angle = 2.0 * np.pi * (k * t % size) / size
    real, imag = np.cos(angle), -np.sin(angle)
    imag[0] = np.cos(np.pi * np.arange(half))
    forward = np.concatenate([real, imag], axis=0)
    gain = np.full((size, 1), 2.0 / size)
    gain[0] = gain[half] = 1.0 / size
    inverse = (forward * gain).T
    return (
        np.concatenate(pair(forward), axis=1),
        np.concatenate(pair(inverse), axis=0),
        np.concatenate(pair(inverse.T), axis=1),
    )


def basis(rows):
    t = np.arange(rows)
    probe = np.linspace(0.0, RATE_MAX, 97)[None, :]
    count = 4
    while True:
        j = np.arange(count)
        node = (rows - 1) / 2 * (1.0 - np.cos((2 * j + 1) * np.pi / (2 * count)))
        base = np.ones((rows, count))
        for a in range(count):
            for b in range(count):
                if a != b:
                    base[:, a] *= (t - node[b]) / (node[a] - node[b])
        error = np.abs(base @ np.exp(-probe * node[:, None]) - np.exp(-probe * t[:, None])).max()
        if error < 2.0**-23:
            return node, base
        count += 2


def node_tables(rows):
    node, base = basis(rows)
    count = len(node)
    pad = -count % 16
    moment = np.pad(base.T, ((0, pad), (0, 0)))
    turned = np.pad(base[::-1].T, ((0, pad), (0, 0)))
    lag = np.arange(rows)[:, None] - np.arange(rows)[None, :]
    lower = np.where((lag >= 0)[None], base.T[:, np.abs(lag)], 0.0)
    upper = np.swapaxes(lower, 1, 2)
    wide = np.repeat(np.concatenate([base, base[::-1]]), 8, axis=1)
    high, low = pair(wide)
    far = np.concatenate([high, high * 0, high * 0], axis=1)
    far[:, 8 * count : 16 * count], far[:, 16 * count :] = low, high
    far = np.pad(far, ((0, 0), (0, 2 * rows - far.shape[1])))
    return (
        node,
        np.concatenate(pair(np.concatenate([moment, turned])), axis=1),
        np.concatenate(pair(upper.reshape(count * rows, rows)), axis=1),
        np.concatenate(pair(lower.reshape(count * rows, rows)), axis=1),
        far,
    )


def dot(left, right):
    return jnp.dot(left, right, preferred_element_type=F32)


def split(value):
    high = value.astype(BF16)
    return high, (value - high.astype(F32)).astype(BF16)


def product(left, right):
    return (left.astype(F32) * right.astype(F32)).astype(BF16)


def twice(value):
    return jnp.concatenate([value, value], axis=0)


def kernel(
    n, node, x_hbm, og_hbm, ig_hbm, oc_hbm, filt_hbm, res_hbm, rate_hbm, mom_hbm, tab_hbm, lo_hbm,
    xg_ref, ogg_ref, igg_ref, fg_ref, rg_ref, tg_ref,
    rim, rr_send, rr_all, du_send, du_all, dv, dv_rim, p_send, p_all, fg_send, fg_all,
    rates, resid, fold_ref, pf_ref, e_ref, h_ref, b_ref, row_ref, far_ref, pb_ref, g_ref,
    conv_ref, xs_ref, fs_ref, ds_ref, mr_ref, u_ref, back_ref,
    wide_ref, filt_ref, own_ref, mom_ref, tab_ref, lo_ref, unit_ref, in_sem,
    rim_sem, dv_sem, all_sem, du_recv,
):
    me = lax.axis_index(AXIS)
    barrier = pltpu.get_barrier_semaphore()

    def others(act):
        def step(k, carry):
            act(lax.rem(me + k, n))
            return carry

        lax.fori_loop(1, n, step, 0)

    def span(lo, hi, act):
        def step(j, carry):
            act(j)
            return carry

        lax.fori_loop(lo, hi, step, 0)

    others(lambda j: pl.semaphore_signal(barrier, inc=1, device_id={AXIS: j}, device_id_type=MESH))

    def load(src, dst, i):
        return pltpu.make_async_copy(src, dst, in_sem.at[i])

    load(rate_hbm, own_ref.at[0], 0).start()
    load(res_hbm, own_ref.at[1], 0).start()
    load(og_hbm, wide_ref.at[0], 1).start()
    load(oc_hbm, wide_ref.at[1], 1).start()
    load(mom_hbm, mom_ref, 2).start()
    load(tab_hbm, tab_ref, 3).start()
    load(x_hbm, wide_ref.at[2], 4).start()
    load(ig_hbm, wide_ref.at[3], 4).start()
    load(filt_hbm, filt_ref, 5).start()
    load(lo_hbm, lo_ref, 6).start()
    og_ref, oc_ref, x_ref, ig_ref = (wide_ref.at[i] for i in range(4))
    rate_ref, res_ref = own_ref.at[0], own_ref.at[1]

    rows, chans = x_hbm.shape
    modes, own = rate_hbm.shape
    groups = filt_hbm.shape[0]
    parts = modes // 8
    count = len(node)
    tall = mom_ref.shape[0] // 2
    size = 2 * rows
    sides = chans // 128
    crowd = n // sides

    def remote(src, dst, ssem, rsem, to):
        return pltpu.make_async_remote_copy(
            src_ref=src, dst_ref=dst, send_sem=ssem, recv_sem=rsem, device_id={AXIS: to}, device_id_type=MESH
        )

    def rr_copy(to):
        return remote(rr_send, rr_all.at[me], all_sem.at[0], all_sem.at[3 + me // crowd], to)

    def p_copy(to):
        return remote(p_send.at[to], p_all.at[me], all_sem.at[0], all_sem.at[1], to)

    def fg_copy(low, top, to):
        part = pl.ds(low, top - low)
        return remote(fg_send.at[part], fg_all.at[me, part], all_sem.at[0], all_sem.at[2], to)

    def du_copy(which, slot, to):
        return remote(du_send.at[which], du_all.at[slot], all_sem.at[0], du_recv.at[slot], to)

    def rim_copy(to):
        return remote(x_ref, rim, rim_sem.at[0], rim_sem.at[1], to)

    def dv_copy(to):
        return remote(dv, dv_rim, dv_sem.at[0], dv_sem.at[1], to)

    def take(ref, i, many):
        part = ref.at[pl.ds(0, many)]
        pltpu.make_async_copy(part, part, all_sem.at[i]).wait()

    p_send[...] = jnp.zeros_like(p_send)
    g_ref[...] = jnp.zeros_like(g_ref)
    load(own_ref, own_ref, 0).wait()
    for g in range(parts):
        rr_send[:, g * own : (g + 1) * own] = rate_ref[8 * g : 8 * g + 8, :]
        rr_send[:, (parts + g) * own : (parts + g + 1) * own] = res_ref[8 * g : 8 * g + 8, :]

    load(wide_ref.at[pl.ds(0, 2)], wide_ref.at[pl.ds(0, 2)], 1).wait()
    load(mom_ref, mom_ref, 2).wait()
    dz2 = twice(product(og_ref[...], oc_ref[...]))
    du_send[0] = dot(mom_ref[:tall, :], dz2).astype(BF16)
    load(wide_ref.at[pl.ds(2, 2)], wide_ref.at[pl.ds(2, 2)], 4).wait()
    pl.semaphore_wait(barrier, n - 1)
    others(lambda j: rr_copy(j).start())
    span(0, me, lambda j: du_copy(0, me, j).start())

    rr_all[me] = rr_send[...]
    load(tab_hbm, tab_ref, 3).wait()
    far_at = 3 * size
    up_at = far_at + size
    for j in range(count):
        b_ref[j] = dot(tab_ref[up_at + j * rows : up_at + (j + 1) * rows, :], dz2)

    @pl.when(me < n - 1)
    def _():
        rim_copy(me + 1).start()

    load(filt_hbm, filt_ref, 5).wait()
    fwd = tab_ref[:size, :]
    inv_hi = tab_ref[size : size + rows, :]
    sign = (1 - 2 * lax.rem(lax.broadcasted_iota(jnp.int32, (size, chans), 0), 2)).astype(F32)

    def spectrum(value):
        return dot(fwd, twice(value))

    def signal(spec):
        return dot(inv_hi, spec.astype(BF16))

    def times(a, b, conj):
        ar, ai, br, bi = a[:rows], a[rows:], b[:rows], b[rows:]
        first_row = lax.broadcasted_iota(jnp.int32, ai.shape, 0) == 0
        pure = ai * bi
        cross = jnp.where(first_row, 0.0, pure)
        if conj:
            return jnp.concatenate([ar * br + cross, jnp.where(first_row, pure, ar * bi - ai * br)], axis=0)
        return jnp.concatenate([ar * br - cross, jnp.where(first_row, pure, ar * bi + ai * br)], axis=0)

    member = (
        lax.broadcasted_iota(jnp.int32, (groups, chans), 1) // (chans // groups)
        == lax.broadcasted_iota(jnp.int32, (groups, chans), 0)
    ).astype(BF16)
    taps = lax.dot_general(
        filt_ref[...], member, (((0,), (0,)), ((), ())), preferred_element_type=F32
    ).astype(BF16)
    fs_ref[...] = spectrum(taps)
    xs_ref[...] = spectrum(x_ref[...])

    def mix():
        @pl.when(me == 0)
        def _():
            rim[...] = jnp.zeros_like(rim)

        @pl.when(me > 0)
        def _():
            rim_copy(me).wait_recv()

        xs = xs_ref[...] + sign * spectrum(rim[...])
        xs_ref[...] = xs
        mr = signal(times(fs_ref[...], xs, False)).astype(BF16)
        mr_ref[...] = mr
        u = product(ig_ref[...], mr)
        u_ref[...] = u
        u2 = twice(u)
        state = dot(mom_ref[tall:, :], u2).astype(BF16)
        du_send[1] = state
        span(me + 1, n, lambda j: du_copy(1, me, j).start())
        for j in range(count):
            total = jnp.zeros((8, chans), F32)
            for t in range(rows // 8):
                total += b_ref[j, 8 * t : 8 * t + 8, :] * u[8 * t : 8 * t + 8, :].astype(F32)
            g_ref[j : j + 1, :] = jnp.sum(total, axis=0, keepdims=True)
        lag = g_ref[...].astype(BF16)
        here = du_send[0]
        for j in range(n):
            at = slice(j * own, (j + 1) * own)
            p_send[j, :, :own] = state[:, at]
            p_send[j, :, own : 2 * own] = here[:, at]
            p_send[j, :, 2 * own : 3 * own] = lag[:, at]
        p_all[me] = p_send[me]
        others(lambda j: p_copy(j).start())

    mine = rate_ref[...]
    lanes = p_all.shape[2]
    fold = jnp.concatenate([mine] * (lanes // own), axis=1)
    for j in range(count):
        fold_ref[j] = jnp.exp(-float(node[j]) * fold)

    def gather(slot, carry, cols):
        row_ref[:, cols] = du_all[slot, :, cols].astype(F32)
        for j in range(count):
            carry += e_ref[j, :, cols] * row_ref[j : j + 1, cols]
        return carry

    def spread(state, which, cols):
        coef = resid[:, cols] * jnp.exp(-rates[:, cols]) * state
        for j in range(count):
            part = coef * e_ref[j, :, cols]
            total = part[:8]
            for g in range(1, parts):
                total += part[8 * g : 8 * g + 8]
            pb_ref[8 * j : 8 * j + 8, cols] = total
        high, low = split(pb_ref[:, cols])
        stack = [high, high, low]
        spare = size - 3 * high.shape[0]
        if spare:
            stack.append(jnp.zeros((spare, high.shape[1]), BF16))
        table = tab_ref[far_at + which * rows : far_at + (which + 1) * rows, :]
        far_ref[:, cols] = dot(table, jnp.concatenate(stack, axis=0))

    @pl.when(me == n - 1)
    def _():
        far_ref[...] = jnp.zeros_like(far_ref)

    nt = (((1,), (1,)), ((), ()))
    few = groups // sides
    turn = tab_ref[2 * size : 3 * size, :]
    def grad(low, top):
        cols = slice(128 * low, 128 * top)

        for side in reversed(range(low, top)):

            @pl.when(me // crowd == side)
            def _(side=side):
                take(rr_all, 3 + side, crowd - 1)

            @pl.when(me // crowd != side)
            def _(side=side):
                take(rr_all, 3 + side, crowd)

        for j in range(low * crowd, top * crowd):
            piece = rr_all[j]
            for g in range(parts):
                at = (slice(8 * g, 8 * g + 8), slice(j * own, (j + 1) * own))
                rates[at] = piece[:, g * own : (g + 1) * own]
                resid[at] = piece[:, (parts + g) * own : (parts + g + 1) * own]
        rate = rates[:, cols]
        weight = resid[:, cols] * jnp.sqrt(2.0 * rate / modes)
        resid[:, cols] = weight
        for j in range(count):
            e = jnp.exp(-float(node[j]) * rate)
            e_ref[j, :, cols] = e
            h_ref[j : j + 1, cols] = jnp.sum(weight * e, axis=0, keepdims=True)

        @pl.when(me < n - 1)
        def _():
            if top == sides:
                span(me + 1, n, lambda j: du_copy(0, j, j).wait_recv())
            decay = jnp.exp(-rates[:, cols] * rows)
            start = jnp.zeros((modes, 128 * (top - low)), F32)
            spread(
                lax.fori_loop(0, n - 1 - me, lambda i, q: gather(n - 1 - i, q * decay, cols), start), 1, cols
            )

        chunk = 32
        for at in range(0, rows, chunk):
            here = slice(at, at + chunk)
            total = far_ref[here, cols]
            for j in range(count):
                total += h_ref[j : j + 1, cols] * b_ref[j, here, cols]
            back = total.astype(BF16)
            back_ref[here, cols] = back
            dv[here, cols] = product(back, ig_ref[here, cols])

    def tap(low, top):
        cols = slice(128 * low, 128 * top)
        spec = spectrum(dv[:, cols])
        ds_ref[:, cols] = spec
        cross = times(xs_ref[:, cols], spec, True).astype(BF16)
        sums = lax.dot_general(member[low * few : top * few, cols], cross, nt, preferred_element_type=F32)
        both = dot(jnp.concatenate(split(sums), axis=0), turn)
        many = (top - low) * few
        part = (both[:many, :rows] + both[many:, :rows] + both[:many, rows:]).astype(BF16)
        for side in range(low, top):
            fg_send[side] = part[(side - low) * few : (side - low + 1) * few]
        others(lambda j: fg_copy(low, top, j).start())

    def hand():
        @pl.when(me > 0)
        def _():
            dv_copy(me - 1).start()

    @pl.when(me == n - 1)
    def _():
        mix()
        for side in reversed(range(sides)):
            grad(side, side + 1)
            if side == 0:
                hand()
            tap(side, side + 1)

    @pl.when((me >= n // 2) & (me < n - 1))
    def _():
        mix()
        grad(0, sides)
        hand()
        tap(0, sides)

    @pl.when(me < n // 2)
    def _():
        grad(0, sides)
        hand()
        mix()
        tap(0, sides)

    fg_all[me] = fg_send[...]
    igg_ref[...] = product(back_ref[...], mr_ref[...])
    u2 = twice(u_ref[...])

    load(lo_hbm, lo_ref, 6).wait()
    conv = jnp.zeros((rows, chans), F32)
    for j in range(count):
        conv += h_ref[j : j + 1, :] * dot(lo_ref[j * rows : (j + 1) * rows, :], u2)
    conv_ref[...] = conv

    @pl.when(me == 0)
    def _():
        far_ref[...] = jnp.zeros_like(far_ref)

    @pl.when(me > 0)
    def _():
        span(0, me, lambda j: du_copy(1, j, j).wait_recv())
        decay = jnp.exp(-rates[...] * rows)
        every = slice(0, chans)
        start = jnp.zeros((modes, chans), F32)
        spread(lax.fori_loop(0, me, lambda i, s: gather(i, s * decay, every), start), 0, every)

    conv = (conv_ref[...] + far_ref[...]).astype(BF16)
    ogg_ref[...] = product(oc_ref[...], conv)

    take(p_all, 1, n - 1)
    scale = 1.0 / math.sqrt(rows * n)
    hop = jnp.exp(-float(rows) * fold)

    for b in range(n):
        pf_ref[b] = p_all[b].astype(F32)

    def owner(b, carry):
        s, far, first, second, near0, near1 = carry
        zero = one = jnp.zeros((modes, lanes), F32)
        for j in range(count):
            part = fold_ref[j] * pf_ref[b, j : j + 1, :]
            zero += part
            one += float(node[j]) * part
        d0 = pltpu.roll(zero, lanes - own, 1)
        d1 = pltpu.roll(one, lanes - own, 1)
        first += d0 * s
        second += (d0 + d1) * s + d0 * far
        return s * hop + zero, (far + rows * s) * hop + one, first, second, near0 + zero, near1 + one

    empty = jnp.zeros((modes, lanes), F32)
    _, _, first, second, near0, near1 = lax.fori_loop(0, n, owner, (empty,) * 6, unroll=8 if n % 8 == 0 else 1)
    step = jnp.exp(-fold)
    first = (step * first + pltpu.roll(near0, lanes - 2 * own, 1))[:, :own]
    second = (step * second + pltpu.roll(near1, lanes - 2 * own, 1))[:, :own]
    gain = jnp.sqrt(2.0 * mine / modes)
    rg_ref[...] = gain * first * scale
    tg_ref[...] = res_ref[...] * gain * (0.5 * first - mine * second) * scale

    @pl.when(me == n - 1)
    def _():
        dv_rim[...] = jnp.zeros_like(dv_rim)

    @pl.when(me < n - 1)
    def _():
        dv_copy(me).wait_recv()

    ws = ds_ref[...] + sign * spectrum(dv_rim[...])
    xg_ref[...] = signal(times(fs_ref[...], ws, True)).astype(BF16)

    pltpu.make_async_copy(unit_ref, unit_ref, all_sem.at[0]).wait()

    @pl.when(me < n - 1)
    def _():
        rim_copy(me + 1).wait_send()

    @pl.when(me > 0)
    def _():
        dv_copy(me - 1).wait_send()

    take(fg_all, 2, n - 1)
    total = jnp.sum(fg_all[...].astype(F32), axis=0) * scale
    for side in range(sides):
        fg_ref[side * few : (side + 1) * few, :] = total[side]


def store(*refs):
    count = (len(refs) - 1) // 2
    gives = [pltpu.make_async_copy(refs[i], refs[count + i], refs[-1].at[i]) for i in range(count)]
    for give in gives:
        give.start()
    for give in gives:
        give.wait()


def local(x, og, ig, oc, filt, res, rate):
    n = lax.axis_size(AXIS)
    rows, chans = x.shape
    modes, own = rate.shape
    groups = filt.shape[1]
    assert rows == filt.shape[0] and modes % 8 == 0 and 2 * (modes // 8) * own <= 128 and 128 % own == 0
    assert chans % 128 == 0 and n % (chans // 128) == 0
    sides = chans // 128
    fwd, inv, turn = dft_tables(rows)
    node, mom, up, lo, far = node_tables(rows)
    count = len(node)
    tall = mom.shape[0] // 2
    tab = np.concatenate([fwd, inv, turn, far, up])
    sent = 4 * 8 * 128 + 2 * (tall * 128 + groups * rows + tall * chans)
    hbm = pl.BlockSpec(memory_space=pltpu.HBM)
    vmem = pl.BlockSpec(memory_space=pltpu.VMEM)
    wide = (rows, chans)
    dma = pltpu.SemaphoreType.DMA
    out = pl.pallas_call(
        functools.partial(kernel, n, tuple(float(v) for v in node)),
        name="mixer",
        out_shape=(
            pltpu.VMEM(wide, BF16),
            pltpu.VMEM(wide, BF16),
            pltpu.VMEM(wide, BF16),
            pltpu.VMEM((groups, rows), F32),
            pltpu.VMEM((modes, own), F32),
            pltpu.VMEM((modes, own), F32),
        ),
        in_specs=[hbm] * 10,
        out_specs=(vmem,) * 6,
        scratch_shapes=[
            pltpu.VMEM(wide, BF16),
            pltpu.VMEM((8, 128), F32),
            pltpu.VMEM((n, 8, 128), F32),
            pltpu.VMEM((2, tall, chans), BF16),
            pltpu.VMEM((n, tall, chans), BF16),
            pltpu.VMEM(wide, BF16),
            pltpu.VMEM(wide, BF16),
            pltpu.VMEM((n, tall, 128), BF16),
            pltpu.VMEM((n, tall, 128), BF16),
            pltpu.VMEM((sides, groups // sides, rows), BF16),
            pltpu.VMEM((n, sides, groups // sides, rows), BF16),
            pltpu.VMEM((modes, chans), F32),
            pltpu.VMEM((modes, chans), F32),
            pltpu.VMEM((count, modes, 128), F32),
            pltpu.VMEM((n, tall, 128), F32),
            pltpu.VMEM((count, modes, chans), F32),
            pltpu.VMEM((tall, chans), F32),
            pltpu.VMEM((count,) + wide, F32),
            pltpu.VMEM((tall, chans), F32),
            pltpu.VMEM(wide, F32),
            pltpu.VMEM((8 * count, chans), F32),
            pltpu.VMEM((tall, chans), F32),
            pltpu.VMEM(wide, F32),
            pltpu.VMEM((2 * rows, chans), F32),
            pltpu.VMEM((2 * rows, chans), F32),
            pltpu.VMEM((2 * rows, chans), F32),
            pltpu.VMEM(wide, BF16),
            pltpu.VMEM(wide, BF16),
            pltpu.VMEM(wide, BF16),
            pltpu.VMEM((4,) + wide, BF16),
            pltpu.VMEM((groups, rows), BF16),
            pltpu.VMEM((2, modes, own), F32),
            pltpu.VMEM(mom.shape, BF16),
            pltpu.VMEM(tab.shape, BF16),
            pltpu.VMEM(lo.shape, BF16),
            pltpu.VMEM((n - 1, sent // 512, 128), F32),
            dma((7,)),
            dma((2,)), dma((2,)), dma((3 + sides,)), dma((n,)),
        ],
        compiler_params=pltpu.CompilerParams(
            collective_id=0, has_side_effects=True, vmem_limit_bytes=GRANT
        ),
    )(
        x, og, ig, oc, filt.T, res, rate,
        jnp.asarray(mom), jnp.asarray(tab), jnp.asarray(lo),
    )
    xg, ogg, igg, fg, rg, tg = pl.pallas_call(
        store,
        name="store",
        out_shape=tuple(jax.ShapeDtypeStruct(o.shape, o.dtype) for o in out),
        in_specs=[vmem] * 6,
        out_specs=(hbm,) * 6,
        scratch_shapes=[dma((6,))],
        compiler_params=pltpu.CompilerParams(vmem_limit_bytes=GRANT),
    )(*[pltpu.with_memory_space_constraint(o, pltpu.VMEM) for o in out])
    return xg, ogg, igg, fg.T, rg, tg


def solution(mesh):
    tokens = P("ctx", "ch")
    shared = P(None, "ch")
    owned = P(None, ("ch", "ctx"))
    return jax.shard_map(
        local,
        mesh=mesh,
        in_specs=(tokens, tokens, tokens, tokens, shared, owned, owned),
        out_specs=(tokens, tokens, tokens, shared, owned, owned),
        check_vma=False,
    )
```

```python
import functools
import math

import jax
import jax.numpy as jnp
import numpy as np
from jax import lax
from jax.experimental import pallas as pl
from jax.experimental.pallas import tpu as pltpu
from jax.sharding import PartitionSpec as P

MESH = pl.DeviceIdType.MESH
F32, BF16 = jnp.float32, jnp.bfloat16
AXIS = "ctx"
GRANT = 60 * 1024 * 1024
RATE_MAX = 0.03


def pair(table):
    table = table.astype(np.float32)
    high = table.astype(BF16)
    return high, (table - high.astype(np.float32)).astype(BF16)


def dft_tables(half):
    size = 2 * half
    k = np.arange(half)[:, None]
    t = np.arange(half)[None, :]
    angle = 2.0 * np.pi * (k * t % size) / size
    real, imag = np.cos(angle), -np.sin(angle)
    imag[0] = np.cos(np.pi * np.arange(half))
    forward = np.concatenate([real, imag], axis=0)
    gain = np.full((size, 1), 2.0 / size)
    gain[0] = gain[half] = 1.0 / size
    inverse = (forward * gain).T
    return (
        np.concatenate(pair(forward), axis=1),
        np.concatenate(pair(inverse), axis=0),
        np.concatenate(pair(inverse.T), axis=1),
    )


def basis(rows):
    t = np.arange(rows)
    probe = np.linspace(0.0, RATE_MAX, 97)[None, :]
    count = 4
    while True:
        j = np.arange(count)
        node = (rows - 1) / 2 * (1.0 - np.cos((2 * j + 1) * np.pi / (2 * count)))
        base = np.ones((rows, count))
        for a in range(count):
            for b in range(count):
                if a != b:
                    base[:, a] *= (t - node[b]) / (node[a] - node[b])
        error = np.abs(base @ np.exp(-probe * node[:, None]) - np.exp(-probe * t[:, None])).max()
        if error < 2.0**-23:
            return node, base
        count += 2


def node_tables(rows):
    node, base = basis(rows)
    count = len(node)
    pad = -count % 16
    moment = np.pad(base.T, ((0, pad), (0, 0)))
    turned = np.pad(base[::-1].T, ((0, pad), (0, 0)))
    lag = np.arange(rows)[:, None] - np.arange(rows)[None, :]
    lower = np.where((lag >= 0)[None], base.T[:, np.abs(lag)], 0.0)
    upper = np.swapaxes(lower, 1, 2)
    wide = np.repeat(np.concatenate([base, base[::-1]]), 8, axis=1)
    high, low = pair(wide)
    far = np.concatenate([high, high * 0, high * 0], axis=1)
    far[:, 8 * count : 16 * count], far[:, 16 * count :] = low, high
    far = np.pad(far, ((0, 0), (0, 2 * rows - far.shape[1])))
    return (
        node,
        np.concatenate(pair(np.concatenate([moment, turned])), axis=1),
        np.concatenate(pair(upper.reshape(count * rows, rows)), axis=1),
        np.concatenate(pair(lower.reshape(count * rows, rows)), axis=1),
        far,
    )


def dot(left, right):
    return jnp.dot(left, right, preferred_element_type=F32)


def split(value):
    high = value.astype(BF16)
    return high, (value - high.astype(F32)).astype(BF16)


def product(left, right):
    return (left.astype(F32) * right.astype(F32)).astype(BF16)


def twice(value):
    return jnp.concatenate([value, value], axis=0)


def kernel(
    n, node, x_hbm, og_hbm, ig_hbm, oc_hbm, filt_hbm, res_hbm, rate_hbm, mom_hbm, tab_hbm, lo_hbm,
    xg_ref, ogg_ref, igg_ref, fg_ref, rg_ref, tg_ref,
    rim, rr_send, rr_all, du_send, du_all, dv, dv_rim, p_send, p_all, fg_send, fg_all,
    rates, resid, fold_ref, pf_ref, e_ref, h_ref, b_ref, row_ref, far_ref, pb_ref, g_ref,
    conv_ref, xs_ref, fs_ref, ds_ref, mr_ref, u_ref, back_ref,
    wide_ref, filt_ref, own_ref, tab_ref, unit_ref, in_sem,
    rim_sem, dv_sem, all_sem, du_recv,
):
    me = lax.axis_index(AXIS)
    barrier = pltpu.get_barrier_semaphore()

    def others(act):
        def step(k, carry):
            act(lax.rem(me + jnp.where(me < n // 2, n - k, k), n))
            return carry

        lax.fori_loop(1, n, step, 0)

    def span(lo, hi, act):
        def step(j, carry):
            act(j)
            return carry

        lax.fori_loop(lo, hi, step, 0)

    others(lambda j: pl.semaphore_signal(barrier, inc=1, device_id={AXIS: j}, device_id_type=MESH))

    def load(src, dst, i):
        return pltpu.make_async_copy(src, dst, in_sem.at[i])

    rows, chans = x_hbm.shape
    wide = [wide_ref.at[pl.ds(i * rows, rows)] for i in range(4)]
    og_ref, oc_ref, x_ref, ig_ref = wide
    mom_ref = wide_ref.at[pl.ds(4 * rows, mom_hbm.shape[0])]
    head = tab_hbm.shape[0]
    load(rate_hbm, own_ref.at[0], 0).start()
    load(res_hbm, own_ref.at[1], 0).start()
    for src, dst in zip((og_hbm, oc_hbm, x_hbm, ig_hbm, mom_hbm), wide + [mom_ref]):
        load(src, dst, 1).start()
    load(tab_hbm, tab_ref.at[pl.ds(0, head)], 2).start()
    load(lo_hbm, tab_ref.at[pl.ds(head, lo_hbm.shape[0])], 2).start()
    load(filt_hbm, filt_ref, 3).start()
    rate_ref, res_ref = own_ref.at[0], own_ref.at[1]

    modes, own = rate_hbm.shape
    groups = filt_hbm.shape[0]
    parts = modes // 8
    count = len(node)
    tall = mom_hbm.shape[0] // 2
    size = 2 * rows
    sides = chans // 128
    crowd = n // sides

    def remote(src, dst, ssem, rsem, to):
        return pltpu.make_async_remote_copy(
            src_ref=src, dst_ref=dst, send_sem=ssem, recv_sem=rsem, device_id={AXIS: to}, device_id_type=MESH
        )

    def rr_copy(to):
        return remote(rr_send, rr_all.at[me], all_sem.at[0], all_sem.at[3 + me // crowd], to)

    def p_copy(to):
        return remote(p_send.at[to], p_all.at[me], all_sem.at[0], all_sem.at[1], to)

    def fg_copy(low, top, to):
        part = pl.ds(low, top - low)
        return remote(fg_send.at[part], fg_all.at[me, part], all_sem.at[0], all_sem.at[2], to)

    def du_copy(which, slot, to):
        return remote(du_send.at[which], du_all.at[slot], all_sem.at[0], du_recv.at[which], to)

    def rim_copy(to):
        return remote(x_ref, rim, all_sem.at[0], rim_sem.at[0], to)

    def dv_copy(to):
        return remote(dv, dv_rim, all_sem.at[0], dv_sem.at[0], to)

    def take(ref, i, many):
        part = ref.at[pl.ds(0, many)]
        pltpu.make_async_copy(part, part, all_sem.at[i]).wait()

    def arrive(which, many):
        for exact in range(1, n):

            @pl.when(many == exact)
            def _(exact=exact):
                part = du_all.at[pl.ds(0, exact)]
                pltpu.make_async_copy(part, part, du_recv.at[which]).wait()

    p_send[...] = jnp.zeros_like(p_send)
    g_ref[...] = jnp.zeros_like(g_ref)
    load(own_ref, own_ref, 0).wait()
    for g in range(parts):
        rr_send[:, g * own : (g + 1) * own] = rate_ref[8 * g : 8 * g + 8, :]
        gain = jnp.sqrt(2.0 * rate_ref[8 * g : 8 * g + 8, :] / modes)
        rr_send[:, (parts + g) * own : (parts + g + 1) * own] = res_ref[8 * g : 8 * g + 8, :] * gain

    load(wide_ref, wide_ref, 1).wait()
    dz2 = twice(product(og_ref[...], oc_ref[...]))
    du_send[0] = dot(mom_ref[:tall, :], dz2).astype(BF16)
    pl.semaphore_wait(barrier, n - 1)
    others(lambda j: rr_copy(j).start())

    @pl.when((me >= n // 2 - 1) & (me < n - 1))
    def _():
        rim_copy(me + 1).start()

    span(0, me, lambda j: du_copy(0, me, j).start())

    rr_all[me] = rr_send[...]
    load(tab_ref, tab_ref, 2).wait()
    far_at = 3 * size
    up_at = far_at + size
    for j in range(count):
        b_ref[j] = dot(tab_ref[up_at + j * rows : up_at + (j + 1) * rows, :], dz2)

    @pl.when(me < n // 2 - 1)
    def _():
        rim_copy(me + 1).start()

    load(filt_hbm, filt_ref, 3).wait()
    fwd = tab_ref[:size, :]
    inv_hi = tab_ref[size : size + rows, :]
    sign = (1 - 2 * lax.rem(lax.broadcasted_iota(jnp.int32, (size, chans), 0), 2)).astype(F32)

    def spectrum(value):
        return dot(fwd, twice(value))

    def signal(spec):
        return dot(inv_hi, spec.astype(BF16))

    def times(a, b, conj):
        ar, ai, br, bi = a[:rows], a[rows:], b[:rows], b[rows:]
        first_row = lax.broadcasted_iota(jnp.int32, ai.shape, 0) == 0
        pure = ai * bi
        cross = jnp.where(first_row, 0.0, pure)
        if conj:
            return jnp.concatenate([ar * br + cross, jnp.where(first_row, pure, ar * bi - ai * br)], axis=0)
        return jnp.concatenate([ar * br - cross, jnp.where(first_row, pure, ar * bi + ai * br)], axis=0)

    member = (
        lax.broadcasted_iota(jnp.int32, (groups, chans), 1) // (chans // groups)
        == lax.broadcasted_iota(jnp.int32, (groups, chans), 0)
    ).astype(BF16)
    taps = lax.dot_general(
        filt_ref[...], member, (((0,), (0,)), ((), ())), preferred_element_type=F32
    ).astype(BF16)
    fs_ref[...] = spectrum(taps)
    xs_ref[...] = spectrum(x_ref[...])

    def mix():
        @pl.when(me == 0)
        def _():
            rim[...] = jnp.zeros_like(rim)

        @pl.when(me > 0)
        def _():
            rim_copy(me).wait_recv()

        xs = xs_ref[...] + sign * spectrum(rim[...])
        xs_ref[...] = xs
        mr = signal(times(fs_ref[...], xs, False)).astype(BF16)
        mr_ref[...] = mr
        u = product(ig_ref[...], mr)
        u_ref[...] = u
        u2 = twice(u)
        state = dot(mom_ref[tall:, :], u2).astype(BF16)
        du_send[1] = state
        span(me + 1, n, lambda j: du_copy(1, me, j).start())
        for j in range(count):
            total = jnp.zeros((8, chans), F32)
            for t in range(rows // 8):
                total += b_ref[j, 8 * t : 8 * t + 8, :] * u[8 * t : 8 * t + 8, :].astype(F32)
            g_ref[j : j + 1, :] = jnp.sum(total, axis=0, keepdims=True)
        lag = g_ref[...].astype(BF16)
        here = du_send[0]
        for j in range(n):
            at = slice(j * own, (j + 1) * own)
            p_send[j, :, :own] = state[:, at]
            p_send[j, :, own : 2 * own] = here[:, at]
            p_send[j, :, 2 * own : 3 * own] = lag[:, at]
        p_all[me] = p_send[me]
        others(lambda j: p_copy(j).start())

    mine = rate_ref[...]
    lanes = p_all.shape[2]
    fold = jnp.concatenate([mine] * (lanes // own), axis=1)
    for j in range(count):
        fold_ref[j] = jnp.exp(-float(node[j]) * fold)

    def gather(slot, carry, cols):
        row_ref[:, cols] = du_all[slot, :, cols].astype(F32)
        for j in range(count):
            carry += e_ref[j, :, cols] * row_ref[j : j + 1, cols]
        return carry

    def spread(state, which, cols):
        coef = resid[:, cols] * jnp.exp(-rates[:, cols]) * state
        for j in range(count):
            part = coef * e_ref[j, :, cols]
            total = part[:8]
            for g in range(1, parts):
                total += part[8 * g : 8 * g + 8]
            pb_ref[8 * j : 8 * j + 8, cols] = total
        high, low = split(pb_ref[:, cols])
        stack = [high, high, low]
        spare = size - 3 * high.shape[0]
        if spare:
            stack.append(jnp.zeros((spare, high.shape[1]), BF16))
        table = tab_ref[far_at + which * rows : far_at + (which + 1) * rows, :]
        far_ref[:, cols] = dot(table, jnp.concatenate(stack, axis=0))

    @pl.when(me == n - 1)
    def _():
        far_ref[...] = jnp.zeros_like(far_ref)

    nt = (((1,), (1,)), ((), ()))
    few = groups // sides
    turn = tab_ref[2 * size : 3 * size, :rows]
    def grad(low, top):
        cols = slice(128 * low, 128 * top)

        for side in reversed(range(low, top)):

            @pl.when(me // crowd == side)
            def _(side=side):
                take(rr_all, 3 + side, crowd - 1)

            @pl.when(me // crowd != side)
            def _(side=side):
                take(rr_all, 3 + side, crowd)

        for j in range(low * crowd, top * crowd):
            piece = rr_all[j]
            for g in range(parts):
                at = (slice(8 * g, 8 * g + 8), slice(j * own, (j + 1) * own))
                rates[at] = piece[:, g * own : (g + 1) * own]
                resid[at] = piece[:, (parts + g) * own : (parts + g + 1) * own]
        rate = rates[:, cols]
        weight = resid[:, cols]
        for j in range(count):
            e = jnp.exp(-float(node[j]) * rate)
            e_ref[j, :, cols] = e
            h_ref[j : j + 1, cols] = jnp.sum(weight * e, axis=0, keepdims=True)

        @pl.when(me < n - 1)
        def _():
            if top == sides:
                arrive(0, n - 1 - me)
            decay = jnp.exp(-rates[:, cols] * rows)
            start = jnp.zeros((modes, 128 * (top - low)), F32)
            spread(
                lax.fori_loop(0, n - 1 - me, lambda i, q: gather(n - 1 - i, q * decay, cols), start), 1, cols
            )

        chunk = 32
        for at in range(0, rows, chunk):
            here = slice(at, at + chunk)
            total = far_ref[here, cols]
            for j in range(count):
                total += h_ref[j : j + 1, cols] * b_ref[j, here, cols]
            back = total.astype(BF16)
            back_ref[here, cols] = back
            dv[here, cols] = product(back, ig_ref[here, cols])

    def tap(low, top):
        cols = slice(128 * low, 128 * top)
        spec = spectrum(dv[:, cols])
        ds_ref[:, cols] = spec
        cross = times(xs_ref[:, cols], spec, True).astype(BF16)
        sums = lax.dot_general(member[low * few : top * few, cols], cross, nt, preferred_element_type=F32)
        part = dot(sums.astype(BF16), turn).astype(BF16)
        for side in range(low, top):
            fg_send[side] = part[(side - low) * few : (side - low + 1) * few]
        others(lambda j: fg_copy(low, top, j).start())

    def hand():
        @pl.when(me > 0)
        def _():
            dv_copy(me - 1).start()

    @pl.when(me == n - 1)
    def _():
        mix()
        for side in reversed(range(sides)):
            grad(side, side + 1)
            if side == 0:
                hand()
            tap(side, side + 1)

    @pl.when((me > n // 2) & (me < n - 1))
    def _():
        mix()
        grad(0, sides)
        hand()
        tap(0, sides)

    @pl.when(me <= n // 2)
    def _():
        grad(0, sides)
        hand()
        mix()
        tap(0, sides)

    fg_all[me] = fg_send[...]
    igg_ref[...] = product(back_ref[...], mr_ref[...])
    u2 = twice(u_ref[...])

    conv = jnp.zeros((rows, chans), F32)
    for j in range(count):
        conv += h_ref[j : j + 1, :] * dot(tab_ref[head + j * rows : head + (j + 1) * rows, :], u2)
    conv_ref[...] = conv

    @pl.when(me == 0)
    def _():
        far_ref[...] = jnp.zeros_like(far_ref)

    @pl.when(me > 0)
    def _():
        arrive(1, me)
        decay = jnp.exp(-rates[...] * rows)
        every = slice(0, chans)
        start = jnp.zeros((modes, chans), F32)
        spread(lax.fori_loop(0, me, lambda i, s: gather(i, s * decay, every), start), 0, every)

    conv = (conv_ref[...] + far_ref[...]).astype(BF16)
    ogg_ref[...] = product(oc_ref[...], conv)

    take(p_all, 1, n - 1)
    scale = 1.0 / math.sqrt(rows * n)
    hop = jnp.exp(-float(rows) * fold)

    for b in range(n):
        pf_ref[b] = p_all[b].astype(F32)

    def owner(b, carry):
        s, far, first, second, near0, near1 = carry
        zero = one = jnp.zeros((modes, lanes), F32)
        for j in range(count):
            part = fold_ref[j] * pf_ref[b, j : j + 1, :]
            zero += part
            one += float(node[j]) * part
        d0 = pltpu.roll(zero, lanes - own, 1)
        d1 = pltpu.roll(one, lanes - own, 1)
        first += d0 * s
        second += (d0 + d1) * s + d0 * far
        return s * hop + zero, (far + rows * s) * hop + one, first, second, near0 + zero, near1 + one

    empty = jnp.zeros((modes, lanes), F32)
    _, _, first, second, near0, near1 = lax.fori_loop(0, n, owner, (empty,) * 6, unroll=8 if n % 8 == 0 else 1)
    step = jnp.exp(-fold)
    first = (step * first + pltpu.roll(near0, lanes - 2 * own, 1))[:, :own]
    second = (step * second + pltpu.roll(near1, lanes - 2 * own, 1))[:, :own]
    gain = jnp.sqrt(2.0 * mine / modes)
    rg_ref[...] = gain * first * scale
    tg_ref[...] = res_ref[...] * gain * (0.5 * first - mine * second) * scale

    @pl.when(me == n - 1)
    def _():
        dv_rim[...] = jnp.zeros_like(dv_rim)

    @pl.when(me < n - 1)
    def _():
        dv_copy(me).wait_recv()

    ws = ds_ref[...] + sign * spectrum(dv_rim[...])
    xg_ref[...] = signal(times(fs_ref[...], ws, True)).astype(BF16)

    edge = (me == 0) | (me == n - 1)
    most = unit_ref.shape[0]

    @pl.when(edge)
    def _():
        part = unit_ref.at[pl.ds(0, most - rows * chans // 256)]
        pltpu.make_async_copy(part, part, all_sem.at[0]).wait()

    @pl.when(jnp.logical_not(edge))
    def _():
        pltpu.make_async_copy(unit_ref, unit_ref, all_sem.at[0]).wait()

    take(fg_all, 2, n - 1)
    total = jnp.sum(fg_all[...].astype(F32), axis=0) * scale
    for side in range(sides):
        fg_ref[side * few : (side + 1) * few, :] = total[side]


def store(*refs):
    count = (len(refs) - 1) // 2
    gives = [pltpu.make_async_copy(refs[i], refs[count + i], refs[-1].at[i]) for i in range(count)]
    for give in gives:
        give.start()
    for give in gives:
        give.wait()


def local(x, og, ig, oc, filt, res, rate):
    n = lax.axis_size(AXIS)
    rows, chans = x.shape
    modes, own = rate.shape
    groups = filt.shape[1]
    assert rows == filt.shape[0] and modes % 8 == 0 and 2 * (modes // 8) * own <= 128 and 128 % own == 0
    assert chans == 2 * rows and chans % 128 == 0 and n % (chans // 128) == 0
    sides = chans // 128
    fwd, inv, turn = dft_tables(rows)
    node, mom, up, lo, far = node_tables(rows)
    count = len(node)
    tall = mom.shape[0] // 2
    tab = np.concatenate([fwd, inv, turn, far, up])
    sent = 4 * 8 * 128 + 2 * (tall * 128 + groups * rows + tall * chans)
    hbm = pl.BlockSpec(memory_space=pltpu.HBM)
    vmem = pl.BlockSpec(memory_space=pltpu.VMEM)
    wide = (rows, chans)
    dma = pltpu.SemaphoreType.DMA
    out = pl.pallas_call(
        functools.partial(kernel, n, tuple(float(v) for v in node)),
        name="mixer",
        out_shape=(
            pltpu.VMEM(wide, BF16),
            pltpu.VMEM(wide, BF16),
            pltpu.VMEM(wide, BF16),
            pltpu.VMEM((groups, rows), F32),
            pltpu.VMEM((modes, own), F32),
            pltpu.VMEM((modes, own), F32),
        ),
        in_specs=[hbm] * 10,
        out_specs=(vmem,) * 6,
        scratch_shapes=[
            pltpu.VMEM(wide, BF16),
            pltpu.VMEM((8, 128), F32),
            pltpu.VMEM((n, 8, 128), F32),
            pltpu.VMEM((2, tall, chans), BF16),
            pltpu.VMEM((n, tall, chans), BF16),
            pltpu.VMEM(wide, BF16),
            pltpu.VMEM(wide, BF16),
            pltpu.VMEM((n, tall, 128), BF16),
            pltpu.VMEM((n, tall, 128), BF16),
            pltpu.VMEM((sides, groups // sides, rows), BF16),
            pltpu.VMEM((n, sides, groups // sides, rows), BF16),
            pltpu.VMEM((modes, chans), F32),
            pltpu.VMEM((modes, chans), F32),
            pltpu.VMEM((count, modes, 128), F32),
            pltpu.VMEM((n, tall, 128), F32),
            pltpu.VMEM((count, modes, chans), F32),
            pltpu.VMEM((tall, chans), F32),
            pltpu.VMEM((count,) + wide, F32),
            pltpu.VMEM((tall, chans), F32),
            pltpu.VMEM(wide, F32),
            pltpu.VMEM((8 * count, chans), F32),
            pltpu.VMEM((tall, chans), F32),
            pltpu.VMEM(wide, F32),
            pltpu.VMEM((2 * rows, chans), F32),
            pltpu.VMEM((2 * rows, chans), F32),
            pltpu.VMEM((2 * rows, chans), F32),
            pltpu.VMEM(wide, BF16),
            pltpu.VMEM(wide, BF16),
            pltpu.VMEM(wide, BF16),
            pltpu.VMEM((4 * rows + mom.shape[0], chans), BF16),
            pltpu.VMEM((groups, rows), BF16),
            pltpu.VMEM((2, modes, own), F32),
            pltpu.VMEM((tab.shape[0] + lo.shape[0], 2 * rows), BF16),
            pltpu.VMEM(((n - 1) * (sent // 512) + rows * chans // 128, 128), F32),
            dma((4,)),
            dma((1,)), dma((1,)), dma((3 + sides,)), dma((2,)),
        ],
        compiler_params=pltpu.CompilerParams(
            collective_id=0, has_side_effects=True, vmem_limit_bytes=GRANT
        ),
    )(
        x, og, ig, oc, filt.T, res, rate,
        jnp.asarray(mom), jnp.asarray(tab), jnp.asarray(lo),
    )
    xg, ogg, igg, fg, rg, tg = pl.pallas_call(
        store,
        name="store",
        out_shape=tuple(jax.ShapeDtypeStruct(o.shape, o.dtype) for o in out),
        in_specs=[vmem] * 6,
        out_specs=(hbm,) * 6,
        scratch_shapes=[dma((6,))],
        compiler_params=pltpu.CompilerParams(vmem_limit_bytes=GRANT),
    )(*[pltpu.with_memory_space_constraint(o, pltpu.VMEM) for o in out])
    return xg, ogg, igg, fg.T, rg, tg


def solution(mesh):
    tokens = P("ctx", "ch")
    shared = P(None, "ch")
    owned = P(None, ("ch", "ctx"))
    return jax.shard_map(
        local,
        mesh=mesh,
        in_specs=(tokens, tokens, tokens, tokens, shared, owned, owned),
        out_specs=(tokens, tokens, tokens, shared, owned, owned),
        check_vma=False,
    )
```

```python
import functools
import math

import jax
import jax.numpy as jnp
import numpy as np
from jax import lax
from jax.experimental import pallas as pl
from jax.experimental.pallas import tpu as pltpu
from jax.sharding import PartitionSpec as P

MESH = pl.DeviceIdType.MESH
F32, BF16 = jnp.float32, jnp.bfloat16
AXIS = "ctx"
GRANT = 60 * 1024 * 1024
RATE_MAX = 0.03


def pair(table):
    table = table.astype(np.float32)
    high = table.astype(BF16)
    return high, (table - high.astype(np.float32)).astype(BF16)


def dft_tables(half):
    size = 2 * half
    k = np.arange(half)[:, None]
    t = np.arange(half)[None, :]
    angle = 2.0 * np.pi * (k * t % size) / size
    real, imag = np.cos(angle), -np.sin(angle)
    imag[0] = np.cos(np.pi * np.arange(half))
    forward = np.concatenate([real, imag], axis=0)
    gain = np.full((size, 1), 2.0 / size)
    gain[0] = gain[half] = 1.0 / size
    inverse = (forward * gain).T
    return (
        np.concatenate(pair(forward), axis=1),
        np.concatenate(pair(inverse), axis=0),
        np.concatenate(pair(inverse.T), axis=1),
    )


def basis(rows):
    t = np.arange(rows)
    probe = np.linspace(0.0, RATE_MAX, 97)[None, :]
    count = 4
    while True:
        j = np.arange(count)
        node = (rows - 1) / 2 * (1.0 - np.cos((2 * j + 1) * np.pi / (2 * count)))
        base = np.ones((rows, count))
        for a in range(count):
            for b in range(count):
                if a != b:
                    base[:, a] *= (t - node[b]) / (node[a] - node[b])
        error = np.abs(base @ np.exp(-probe * node[:, None]) - np.exp(-probe * t[:, None])).max()
        if error < 2.0**-23:
            return node, base
        count += 2


def node_tables(rows):
    node, base = basis(rows)
    count = len(node)
    pad = -count % 16
    moment = np.pad(base.T, ((0, pad), (0, 0)))
    turned = np.pad(base[::-1].T, ((0, pad), (0, 0)))
    lag = np.arange(rows)[:, None] - np.arange(rows)[None, :]
    lower = np.where((lag >= 0)[None], base.T[:, np.abs(lag)], 0.0)
    upper = np.swapaxes(lower, 1, 2)
    wide = np.repeat(np.concatenate([base, base[::-1]]), 8, axis=1)
    high, low = pair(wide)
    far = np.concatenate([high, high * 0, high * 0], axis=1)
    far[:, 8 * count : 16 * count], far[:, 16 * count :] = low, high
    far = np.pad(far, ((0, 0), (0, 2 * rows - far.shape[1])))
    return (
        node,
        np.concatenate(pair(np.concatenate([moment, turned])), axis=1),
        np.concatenate(pair(upper.reshape(count * rows, rows)), axis=1),
        np.concatenate(pair(lower.reshape(count * rows, rows)), axis=1),
        far,
    )


def dot(left, right):
    return jnp.dot(left, right, preferred_element_type=F32)


def split(value):
    high = value.astype(BF16)
    return high, (value - high.astype(F32)).astype(BF16)


def product(left, right):
    return (left.astype(F32) * right.astype(F32)).astype(BF16)


def twice(value):
    return jnp.concatenate([value, value], axis=0)


def kernel(
    n, node, x_hbm, og_hbm, ig_hbm, oc_hbm, filt_hbm, res_hbm, rate_hbm, mom_hbm, tab_hbm, lo_hbm,
    xg_ref, ogg_ref, igg_ref, fg_ref, rg_ref, tg_ref,
    rim, rr_send, rr_all, du_send, du_all, dv, dv_rim, p_send, p_all, fg_send, fg_all,
    rates, resid, fold_ref, pf_ref, e_ref, h_ref, b_ref, row_ref, far_ref, pb_ref, g_ref,
    conv_ref, xs_ref, fs_ref, ds_ref, mr_ref, u_ref, back_ref,
    wide_ref, filt_ref, own_ref, tab_ref, unit_ref, in_sem,
    rim_sem, dv_sem, all_sem, du_recv,
):
    me = lax.axis_index(AXIS)
    barrier = pltpu.get_barrier_semaphore()

    def others(act):
        def step(k, carry):
            act(lax.rem(me + jnp.where(me < n // 2, n - k, k), n))
            return carry

        lax.fori_loop(1, n, step, 0)

    def span(lo, hi, act):
        def step(j, carry):
            act(j)
            return carry

        lax.fori_loop(lo, hi, step, 0)

    others(lambda j: pl.semaphore_signal(barrier, inc=1, device_id={AXIS: j}, device_id_type=MESH))

    def load(src, dst, i):
        return pltpu.make_async_copy(src, dst, in_sem.at[i])

    rows, chans = x_hbm.shape
    wide = [wide_ref.at[pl.ds(i * rows, rows)] for i in range(4)]
    og_ref, oc_ref, x_ref, ig_ref = wide
    mom_ref = wide_ref.at[pl.ds(4 * rows, mom_hbm.shape[0])]
    head = tab_hbm.shape[0]
    load(rate_hbm, own_ref.at[0], 0).start()
    load(res_hbm, own_ref.at[1], 0).start()
    for src, dst in zip((og_hbm, oc_hbm, x_hbm, ig_hbm, mom_hbm), wide + [mom_ref]):
        load(src, dst, 1).start()
    load(tab_hbm, tab_ref.at[pl.ds(0, head)], 2).start()
    load(lo_hbm, tab_ref.at[pl.ds(head, lo_hbm.shape[0])], 2).start()
    load(filt_hbm, filt_ref, 3).start()
    rate_ref, res_ref = own_ref.at[0], own_ref.at[1]

    modes, own = rate_hbm.shape
    groups = filt_hbm.shape[0]
    parts = modes // 8
    count = len(node)
    tall = mom_hbm.shape[0] // 2
    size = 2 * rows
    sides = chans // 128
    crowd = n // sides

    def remote(src, dst, ssem, rsem, to):
        return pltpu.make_async_remote_copy(
            src_ref=src, dst_ref=dst, send_sem=ssem, recv_sem=rsem, device_id={AXIS: to}, device_id_type=MESH
        )

    def rr_copy(to):
        return remote(rr_send, rr_all.at[me], all_sem.at[0], all_sem.at[3 + me // crowd], to)

    def p_copy(to):
        return remote(p_send.at[to], p_all.at[me], all_sem.at[0], all_sem.at[1], to)

    def fg_copy(low, top, to):
        part = pl.ds(low, top - low)
        return remote(fg_send.at[part], fg_all.at[me, part], all_sem.at[0], all_sem.at[2], to)

    def du_copy(which, slot, to):
        return remote(du_send.at[which], du_all.at[slot], all_sem.at[0], du_recv.at[which], to)

    def rim_copy(to):
        return remote(x_ref, rim, all_sem.at[0], rim_sem.at[0], to)

    def dv_copy(to):
        return remote(dv, dv_rim, all_sem.at[0], dv_sem.at[0], to)

    def take(ref, i, many):
        part = ref.at[pl.ds(0, many)]
        pltpu.make_async_copy(part, part, all_sem.at[i]).wait()

    def arrive(which, many):
        for exact in range(1, n):

            @pl.when(many == exact)
            def _(exact=exact):
                part = du_all.at[pl.ds(0, exact)]
                pltpu.make_async_copy(part, part, du_recv.at[which]).wait()

    p_send[...] = jnp.zeros_like(p_send)
    g_ref[...] = jnp.zeros_like(g_ref)
    load(own_ref, own_ref, 0).wait()
    for g in range(parts):
        rr_send[:, g * own : (g + 1) * own] = rate_ref[8 * g : 8 * g + 8, :]
        gain = jnp.sqrt(2.0 * rate_ref[8 * g : 8 * g + 8, :] / modes)
        rr_send[:, (parts + g) * own : (parts + g + 1) * own] = res_ref[8 * g : 8 * g + 8, :] * gain

    load(wide_ref, wide_ref, 1).wait()
    dz2 = twice(product(og_ref[...], oc_ref[...]))
    du_send[0] = dot(mom_ref[:tall, :], dz2).astype(BF16)
    pl.semaphore_wait(barrier, n - 1)
    others(lambda j: rr_copy(j).start())

    @pl.when((me >= n // 2 - 1) & (me < n - 1))
    def _():
        rim_copy(me + 1).start()

    span(0, me, lambda j: du_copy(0, me, j).start())

    rr_all[me] = rr_send[...]
    load(tab_ref, tab_ref, 2).wait()
    far_at = 3 * size
    up_at = far_at + size
    for j in range(count):
        b_ref[j] = dot(tab_ref[up_at + j * rows : up_at + (j + 1) * rows, :], dz2)

    @pl.when(me < n // 2 - 1)
    def _():
        rim_copy(me + 1).start()

    load(filt_hbm, filt_ref, 3).wait()
    fwd = tab_ref[:size, :]
    inv_hi = tab_ref[size : size + rows, :]
    sign = (1 - 2 * lax.rem(lax.broadcasted_iota(jnp.int32, (size, chans), 0), 2)).astype(F32)

    def spectrum(value):
        return dot(fwd, twice(value))

    def signal(spec):
        return dot(inv_hi, spec.astype(BF16))

    def times(a, b, conj):
        ar, ai, br, bi = a[:rows], a[rows:], b[:rows], b[rows:]
        first_row = lax.broadcasted_iota(jnp.int32, ai.shape, 0) == 0
        pure = ai * bi
        cross = jnp.where(first_row, 0.0, pure)
        if conj:
            return jnp.concatenate([ar * br + cross, jnp.where(first_row, pure, ar * bi - ai * br)], axis=0)
        return jnp.concatenate([ar * br - cross, jnp.where(first_row, pure, ar * bi + ai * br)], axis=0)

    member = (
        lax.broadcasted_iota(jnp.int32, (groups, chans), 1) // (chans // groups)
        == lax.broadcasted_iota(jnp.int32, (groups, chans), 0)
    ).astype(BF16)
    taps = lax.dot_general(
        filt_ref[...], member, (((0,), (0,)), ((), ())), preferred_element_type=F32
    ).astype(BF16)
    fs_ref[...] = spectrum(taps)
    xs_ref[...] = spectrum(x_ref[...])

    def mix():
        @pl.when(me == 0)
        def _():
            rim[...] = jnp.zeros_like(rim)

        @pl.when(me > 0)
        def _():
            rim_copy(me).wait_recv()

        xs = xs_ref[...] + sign * spectrum(rim[...])
        xs_ref[...] = xs
        mr = signal(times(fs_ref[...], xs, False)).astype(BF16)
        mr_ref[...] = mr
        u = product(ig_ref[...], mr)
        u_ref[...] = u
        u2 = twice(u)
        state = dot(mom_ref[tall:, :], u2).astype(BF16)
        du_send[1] = state
        span(me + 1, n, lambda j: du_copy(1, me, j).start())
        for j in range(count):
            total = jnp.zeros((8, chans), F32)
            for t in range(rows // 8):
                total += b_ref[j, 8 * t : 8 * t + 8, :] * u[8 * t : 8 * t + 8, :].astype(F32)
            g_ref[j : j + 1, :] = jnp.sum(total, axis=0, keepdims=True)
        lag = g_ref[...].astype(BF16)
        here = du_send[0]
        for j in range(n):
            at = slice(j * own, (j + 1) * own)
            p_send[j, :, :own] = state[:, at]
            p_send[j, :, own : 2 * own] = here[:, at]
            p_send[j, :, 2 * own : 3 * own] = lag[:, at]
        p_all[me] = p_send[me]
        others(lambda j: p_copy(j).start())

    mine = rate_ref[...]
    lanes = p_all.shape[2]
    fold = jnp.concatenate([mine] * (lanes // own), axis=1)
    for j in range(count):
        fold_ref[j] = jnp.exp(-float(node[j]) * fold)

    def gather(slot, carry, cols):
        row_ref[:, cols] = du_all[slot, :, cols].astype(F32)
        for j in range(count):
            carry += e_ref[j, :, cols] * row_ref[j : j + 1, cols]
        return carry

    def spread(state, which, cols):
        coef = resid[:, cols] * jnp.exp(-rates[:, cols]) * state
        for j in range(count):
            part = coef * e_ref[j, :, cols]
            total = part[:8]
            for g in range(1, parts):
                total += part[8 * g : 8 * g + 8]
            pb_ref[8 * j : 8 * j + 8, cols] = total
        high, low = split(pb_ref[:, cols])
        stack = [high, high, low]
        spare = size - 3 * high.shape[0]
        if spare:
            stack.append(jnp.zeros((spare, high.shape[1]), BF16))
        table = tab_ref[far_at + which * rows : far_at + (which + 1) * rows, :]
        far_ref[:, cols] = dot(table, jnp.concatenate(stack, axis=0))

    @pl.when(me == n - 1)
    def _():
        far_ref[...] = jnp.zeros_like(far_ref)

    nt = (((1,), (1,)), ((), ()))
    few = groups // sides
    turn = tab_ref[2 * size : 3 * size, :rows]
    def grad(low, top):
        cols = slice(128 * low, 128 * top)

        for side in reversed(range(low, top)):

            @pl.when(me // crowd == side)
            def _(side=side):
                take(rr_all, 3 + side, crowd - 1)

            @pl.when(me // crowd != side)
            def _(side=side):
                take(rr_all, 3 + side, crowd)

        for j in range(low * crowd, top * crowd):
            piece = rr_all[j]
            for g in range(parts):
                at = (slice(8 * g, 8 * g + 8), slice(j * own, (j + 1) * own))
                rates[at] = piece[:, g * own : (g + 1) * own]
                resid[at] = piece[:, (parts + g) * own : (parts + g + 1) * own]
        rate = rates[:, cols]
        weight = resid[:, cols]
        for j in range(count):
            e = jnp.exp(-float(node[j]) * rate)
            e_ref[j, :, cols] = e
            h_ref[j : j + 1, cols] = jnp.sum(weight * e, axis=0, keepdims=True)

        @pl.when(me < n - 1)
        def _():
            if top == sides:
                arrive(0, n - 1 - me)
            decay = jnp.exp(-rates[:, cols] * rows)
            start = jnp.zeros((modes, 128 * (top - low)), F32)
            spread(
                lax.fori_loop(0, n - 1 - me, lambda i, q: gather(n - 1 - i, q * decay, cols), start), 1, cols
            )

        chunk = 32
        for at in range(0, rows, chunk):
            here = slice(at, at + chunk)
            total = far_ref[here, cols]
            for j in range(count):
                total += h_ref[j : j + 1, cols] * b_ref[j, here, cols]
            back = total.astype(BF16)
            back_ref[here, cols] = back
            dv[here, cols] = product(back, ig_ref[here, cols])

    def tap(low, top):
        cols = slice(128 * low, 128 * top)
        spec = spectrum(dv[:, cols])
        ds_ref[:, cols] = spec
        cross = times(xs_ref[:, cols], spec, True).astype(BF16)
        sums = lax.dot_general(member[low * few : top * few, cols], cross, nt, preferred_element_type=F32)
        part = dot(sums.astype(BF16), turn).astype(BF16)
        for side in range(low, top):
            fg_send[side] = part[(side - low) * few : (side - low + 1) * few]
        others(lambda j: fg_copy(low, top, j).start())

    def hand():
        @pl.when(me > 0)
        def _():
            dv_copy(me - 1).start()

    @pl.when(me == n - 1)
    def _():
        mix()
        for side in reversed(range(sides)):
            grad(side, side + 1)
            if side == 0:
                hand()
            tap(side, side + 1)

    @pl.when((me > n // 2) & (me < n - 1))
    def _():
        mix()
        grad(0, sides)
        hand()
        tap(0, sides)

    @pl.when(me <= n // 2)
    def _():
        grad(0, sides)
        hand()
        mix()
        tap(0, sides)

    fg_all[me] = fg_send[...]
    igg_ref[...] = product(back_ref[...], mr_ref[...])
    u2 = twice(u_ref[...])

    conv = jnp.zeros((rows, chans), F32)
    for j in range(count):
        conv += h_ref[j : j + 1, :] * dot(tab_ref[head + j * rows : head + (j + 1) * rows, :], u2)
    conv_ref[...] = conv

    @pl.when(me == 0)
    def _():
        far_ref[...] = jnp.zeros_like(far_ref)

    @pl.when(me > 0)
    def _():
        arrive(1, me)
        decay = jnp.exp(-rates[...] * rows)
        every = slice(0, chans)
        start = jnp.zeros((modes, chans), F32)
        spread(lax.fori_loop(0, me, lambda i, s: gather(i, s * decay, every), start), 0, every)

    conv = (conv_ref[...] + far_ref[...]).astype(BF16)
    ogg_ref[...] = product(oc_ref[...], conv)

    @pl.when(me == n - 1)
    def _():
        dv_rim[...] = jnp.zeros_like(dv_rim)

    @pl.when(me < n - 1)
    def _():
        dv_copy(me).wait_recv()

    ws = ds_ref[...] + sign * spectrum(dv_rim[...])
    xg_ref[...] = signal(times(fs_ref[...], ws, True)).astype(BF16)

    take(p_all, 1, n - 1)
    scale = 1.0 / math.sqrt(rows * n)
    hop = jnp.exp(-float(rows) * fold)

    for b in range(n):
        pf_ref[b] = p_all[b].astype(F32)

    def owner(b, carry):
        s, far, first, second, near0, near1 = carry
        zero = one = jnp.zeros((modes, lanes), F32)
        for j in range(count):
            part = fold_ref[j] * pf_ref[b, j : j + 1, :]
            zero += part
            one += float(node[j]) * part
        d0 = pltpu.roll(zero, lanes - own, 1)
        d1 = pltpu.roll(one, lanes - own, 1)
        first += d0 * s
        second += (d0 + d1) * s + d0 * far
        return s * hop + zero, (far + rows * s) * hop + one, first, second, near0 + zero, near1 + one

    empty = jnp.zeros((modes, lanes), F32)
    _, _, first, second, near0, near1 = lax.fori_loop(0, n, owner, (empty,) * 6, unroll=8 if n % 8 == 0 else 1)
    step = jnp.exp(-fold)
    first = (step * first + pltpu.roll(near0, lanes - 2 * own, 1))[:, :own]
    second = (step * second + pltpu.roll(near1, lanes - 2 * own, 1))[:, :own]
    gain = jnp.sqrt(2.0 * mine / modes)
    rg_ref[...] = gain * first * scale
    tg_ref[...] = res_ref[...] * gain * (0.5 * first - mine * second) * scale

    edge = (me == 0) | (me == n - 1)
    most = unit_ref.shape[0]

    @pl.when(edge)
    def _():
        part = unit_ref.at[pl.ds(0, most - rows * chans // 256)]
        pltpu.make_async_copy(part, part, all_sem.at[0]).wait()

    @pl.when(jnp.logical_not(edge))
    def _():
        pltpu.make_async_copy(unit_ref, unit_ref, all_sem.at[0]).wait()

    take(fg_all, 2, n - 1)
    total = jnp.sum(fg_all[...].astype(F32), axis=0) * scale
    for side in range(sides):
        fg_ref[side * few : (side + 1) * few, :] = total[side]


def store(*refs):
    count = (len(refs) - 1) // 2
    gives = [pltpu.make_async_copy(refs[i], refs[count + i], refs[-1].at[i]) for i in range(count)]
    for give in gives:
        give.start()
    for give in gives:
        give.wait()


def local(x, og, ig, oc, filt, res, rate):
    n = lax.axis_size(AXIS)
    rows, chans = x.shape
    modes, own = rate.shape
    groups = filt.shape[1]
    assert rows == filt.shape[0] and modes % 8 == 0 and 2 * (modes // 8) * own <= 128 and 128 % own == 0
    assert chans == 2 * rows and chans % 128 == 0 and n % (chans // 128) == 0
    sides = chans // 128
    fwd, inv, turn = dft_tables(rows)
    node, mom, up, lo, far = node_tables(rows)
    count = len(node)
    tall = mom.shape[0] // 2
    tab = np.concatenate([fwd, inv, turn, far, up])
    sent = 4 * 8 * 128 + 2 * (tall * 128 + groups * rows + tall * chans)
    hbm = pl.BlockSpec(memory_space=pltpu.HBM)
    vmem = pl.BlockSpec(memory_space=pltpu.VMEM)
    wide = (rows, chans)
    dma = pltpu.SemaphoreType.DMA
    out = pl.pallas_call(
        functools.partial(kernel, n, tuple(float(v) for v in node)),
        name="mixer",
        out_shape=(
            pltpu.VMEM(wide, BF16),
            pltpu.VMEM(wide, BF16),
            pltpu.VMEM(wide, BF16),
            pltpu.VMEM((groups, rows), F32),
            pltpu.VMEM((modes, own), F32),
            pltpu.VMEM((modes, own), F32),
        ),
        in_specs=[hbm] * 10,
        out_specs=(vmem,) * 6,
        scratch_shapes=[
            pltpu.VMEM(wide, BF16),
            pltpu.VMEM((8, 128), F32),
            pltpu.VMEM((n, 8, 128), F32),
            pltpu.VMEM((2, tall, chans), BF16),
            pltpu.VMEM((n, tall, chans), BF16),
            pltpu.VMEM(wide, BF16),
            pltpu.VMEM(wide, BF16),
            pltpu.VMEM((n, tall, 128), BF16),
            pltpu.VMEM((n, tall, 128), BF16),
            pltpu.VMEM((sides, groups // sides, rows), BF16),
            pltpu.VMEM((n, sides, groups // sides, rows), BF16),
            pltpu.VMEM((modes, chans), F32),
            pltpu.VMEM((modes, chans), F32),
            pltpu.VMEM((count, modes, 128), F32),
            pltpu.VMEM((n, tall, 128), F32),
            pltpu.VMEM((count, modes, chans), F32),
            pltpu.VMEM((tall, chans), F32),
            pltpu.VMEM((count,) + wide, F32),
            pltpu.VMEM((tall, chans), F32),
            pltpu.VMEM(wide, F32),
            pltpu.VMEM((8 * count, chans), F32),
            pltpu.VMEM((tall, chans), F32),
            pltpu.VMEM(wide, F32),
            pltpu.VMEM((2 * rows, chans), F32),
            pltpu.VMEM((2 * rows, chans), F32),
            pltpu.VMEM((2 * rows, chans), F32),
            pltpu.VMEM(wide, BF16),
            pltpu.VMEM(wide, BF16),
            pltpu.VMEM(wide, BF16),
            pltpu.VMEM((4 * rows + mom.shape[0], chans), BF16),
            pltpu.VMEM((groups, rows), BF16),
            pltpu.VMEM((2, modes, own), F32),
            pltpu.VMEM((tab.shape[0] + lo.shape[0], 2 * rows), BF16),
            pltpu.VMEM(((n - 1) * (sent // 512) + rows * chans // 128, 128), F32),
            dma((4,)),
            dma((1,)), dma((1,)), dma((3 + sides,)), dma((2,)),
        ],
        compiler_params=pltpu.CompilerParams(
            collective_id=0, has_side_effects=True, vmem_limit_bytes=GRANT
        ),
    )(
        x, og, ig, oc, filt.T, res, rate,
        jnp.asarray(mom), jnp.asarray(tab), jnp.asarray(lo),
    )
    xg, ogg, igg, fg, rg, tg = pl.pallas_call(
        store,
        name="store",
        out_shape=tuple(jax.ShapeDtypeStruct(o.shape, o.dtype) for o in out),
        in_specs=[vmem] * 6,
        out_specs=(hbm,) * 6,
        scratch_shapes=[dma((6,))],
        compiler_params=pltpu.CompilerParams(vmem_limit_bytes=GRANT),
    )(*[pltpu.with_memory_space_constraint(o, pltpu.VMEM) for o in out])
    return xg, ogg, igg, fg.T, rg, tg


def solution(mesh):
    tokens = P("ctx", "ch")
    shared = P(None, "ch")
    owned = P(None, ("ch", "ctx"))
    return jax.shard_map(
        local,
        mesh=mesh,
        in_specs=(tokens, tokens, tokens, tokens, shared, owned, owned),
        out_specs=(tokens, tokens, tokens, shared, owned, owned),
        check_vma=False,
    )
```

```python
import functools
import math

import jax
import jax.numpy as jnp
import numpy as np
from jax import lax
from jax.experimental import pallas as pl
from jax.experimental.pallas import tpu as pltpu
from jax.sharding import PartitionSpec as P

MESH = pl.DeviceIdType.MESH
F32, BF16 = jnp.float32, jnp.bfloat16
AXIS = "ctx"
GRANT = 60 * 1024 * 1024
RATE_MAX = 0.03


def pair(table):
    table = table.astype(np.float32)
    high = table.astype(BF16)
    return high, (table - high.astype(np.float32)).astype(BF16)


def dft_tables(half):
    size = 2 * half
    k = np.arange(half)[:, None]
    t = np.arange(half)[None, :]
    angle = 2.0 * np.pi * (k * t % size) / size
    real, imag = np.cos(angle), -np.sin(angle)
    imag[0] = np.cos(np.pi * np.arange(half))
    forward = np.concatenate([real, imag], axis=0)
    gain = np.full((size, 1), 2.0 / size)
    gain[0] = gain[half] = 1.0 / size
    inverse = (forward * gain).T
    return (
        np.concatenate(pair(forward), axis=1),
        np.concatenate(pair(inverse), axis=0),
        np.concatenate(pair(inverse.T), axis=1),
    )


def basis(rows):
    t = np.arange(rows)
    probe = np.linspace(0.0, RATE_MAX, 97)[None, :]
    count = 4
    while True:
        j = np.arange(count)
        node = (rows - 1) / 2 * (1.0 - np.cos((2 * j + 1) * np.pi / (2 * count)))
        base = np.ones((rows, count))
        for a in range(count):
            for b in range(count):
                if a != b:
                    base[:, a] *= (t - node[b]) / (node[a] - node[b])
        error = np.abs(base @ np.exp(-probe * node[:, None]) - np.exp(-probe * t[:, None])).max()
        if error < 2.0**-23:
            return node, base
        count += 2


def node_tables(rows):
    node, base = basis(rows)
    count = len(node)
    pad = -count % 16
    moment = np.pad(base.T, ((0, pad), (0, 0)))
    turned = np.pad(base[::-1].T, ((0, pad), (0, 0)))
    lag = np.arange(rows)[:, None] - np.arange(rows)[None, :]
    lower = np.where((lag >= 0)[None], base.T[:, np.abs(lag)], 0.0)
    upper = np.swapaxes(lower, 1, 2)
    wide = np.repeat(np.concatenate([base, base[::-1]]), 8, axis=1)
    high, low = pair(wide)
    far = np.concatenate([high, high * 0, high * 0], axis=1)
    far[:, 8 * count : 16 * count], far[:, 16 * count :] = low, high
    far = np.pad(far, ((0, 0), (0, 2 * rows - far.shape[1])))
    return (
        node,
        np.concatenate(pair(np.concatenate([moment, turned])), axis=1),
        np.concatenate(pair(upper.reshape(count * rows, rows)), axis=1),
        np.concatenate(pair(lower.reshape(count * rows, rows)), axis=1),
        far,
    )


def dot(left, right):
    return jnp.dot(left, right, preferred_element_type=F32)


def split(value):
    high = value.astype(BF16)
    return high, (value - high.astype(F32)).astype(BF16)


def product(left, right):
    return (left.astype(F32) * right.astype(F32)).astype(BF16)


def twice(value):
    return jnp.concatenate([value, value], axis=0)


def kernel(
    n, node, x_hbm, og_hbm, ig_hbm, oc_hbm, filt_hbm, res_hbm, rate_hbm, mom_hbm, tab_hbm, lo_hbm,
    xg_ref, ogg_ref, igg_ref, fg_ref, rg_ref, tg_ref,
    rim, rr_send, rr_all, du_send, du_all, dv, dv_rim, p_send, p_all, fg_send, fg_all,
    rates, resid, fold_ref, pf_ref, e_ref, h_ref, b_ref, row_ref, far_ref, pb_ref, g_ref,
    conv_ref, xs_ref, fs_ref, ds_ref, mr_ref, u_ref, back_ref,
    wide_ref, filt_ref, own_ref, tab_ref, unit_ref, in_sem,
    rim_sem, dv_sem, all_sem, du_recv,
):
    me = lax.axis_index(AXIS)
    barrier = pltpu.get_barrier_semaphore()

    def others(act):
        def step(k, carry):
            act(lax.rem(me + jnp.where(me < n // 2, n - k, k), n))
            return carry

        lax.fori_loop(1, n, step, 0)

    def span(lo, hi, act):
        def step(j, carry):
            act(j)
            return carry

        lax.fori_loop(lo, hi, step, 0)

    others(lambda j: pl.semaphore_signal(barrier, inc=1, device_id={AXIS: j}, device_id_type=MESH))

    def load(src, dst, i):
        return pltpu.make_async_copy(src, dst, in_sem.at[i])

    rows, chans = x_hbm.shape
    wide = [wide_ref.at[pl.ds(i * rows, rows)] for i in range(4)]
    og_ref, oc_ref, x_ref, ig_ref = wide
    mom_ref = wide_ref.at[pl.ds(4 * rows, mom_hbm.shape[0])]
    head = tab_hbm.shape[0]
    load(rate_hbm, own_ref.at[0], 0).start()
    load(res_hbm, own_ref.at[1], 0).start()
    for src, dst in zip((og_hbm, oc_hbm, x_hbm, ig_hbm, mom_hbm), wide + [mom_ref]):
        load(src, dst, 1).start()
    load(tab_hbm, tab_ref.at[pl.ds(0, head)], 2).start()
    load(lo_hbm, tab_ref.at[pl.ds(head, lo_hbm.shape[0])], 2).start()
    load(filt_hbm, filt_ref, 3).start()
    rate_ref, res_ref = own_ref.at[0], own_ref.at[1]

    modes, own = rate_hbm.shape
    groups = filt_hbm.shape[0]
    parts = modes // 8
    count = len(node)
    tall = mom_hbm.shape[0] // 2
    size = 2 * rows
    sides = chans // 128
    crowd = n // sides

    def remote(src, dst, ssem, rsem, to):
        return pltpu.make_async_remote_copy(
            src_ref=src, dst_ref=dst, send_sem=ssem, recv_sem=rsem, device_id={AXIS: to}, device_id_type=MESH
        )

    def rr_copy(to):
        return remote(rr_send, rr_all.at[me], all_sem.at[0], all_sem.at[3 + me // crowd], to)

    def p_copy(to):
        return remote(p_send.at[to], p_all.at[me], all_sem.at[0], all_sem.at[1], to)

    def fg_copy(low, top, to):
        part = pl.ds(low, top - low)
        return remote(fg_send.at[part], fg_all.at[me, part], all_sem.at[0], all_sem.at[2], to)

    def du_copy(which, slot, to):
        return remote(du_send.at[which], du_all.at[slot], all_sem.at[0], du_recv.at[which], to)

    def rim_copy(to):
        return remote(x_ref, rim, all_sem.at[0], rim_sem.at[0], to)

    def dv_copy(to):
        return remote(dv, dv_rim, all_sem.at[0], dv_sem.at[0], to)

    def take(ref, i, many):
        part = ref.at[pl.ds(0, many)]
        pltpu.make_async_copy(part, part, all_sem.at[i]).wait()

    def arrive(which, many):
        for exact in range(1, n):

            @pl.when(many == exact)
            def _(exact=exact):
                part = du_all.at[pl.ds(0, exact)]
                pltpu.make_async_copy(part, part, du_recv.at[which]).wait()

    p_send[...] = jnp.zeros_like(p_send)
    g_ref[...] = jnp.zeros_like(g_ref)
    load(own_ref, own_ref, 0).wait()
    for g in range(parts):
        rr_send[:, g * own : (g + 1) * own] = rate_ref[8 * g : 8 * g + 8, :]
        gain = jnp.sqrt(2.0 * rate_ref[8 * g : 8 * g + 8, :] / modes)
        rr_send[:, (parts + g) * own : (parts + g + 1) * own] = res_ref[8 * g : 8 * g + 8, :] * gain

    load(wide_ref, wide_ref, 1).wait()
    dz2 = twice(product(og_ref[...], oc_ref[...]))
    du_send[0] = dot(mom_ref[:tall, :], dz2).astype(BF16)
    pl.semaphore_wait(barrier, n - 1)
    others(lambda j: rr_copy(j).start())

    @pl.when((me >= n // 2 - 1) & (me < n - 1))
    def _():
        rim_copy(me + 1).start()

    span(0, me, lambda j: du_copy(0, me, j).start())

    rr_all[me] = rr_send[...]
    load(tab_ref, tab_ref, 2).wait()
    far_at = 3 * size
    up_at = far_at + size
    for j in range(count):
        b_ref[j] = dot(tab_ref[up_at + j * rows : up_at + (j + 1) * rows, :], dz2)

    @pl.when(me < n // 2 - 1)
    def _():
        rim_copy(me + 1).start()

    load(filt_hbm, filt_ref, 3).wait()
    fwd = tab_ref[:size, :]
    inv_hi = tab_ref[size : size + rows, :]
    sign = (1 - 2 * lax.rem(lax.broadcasted_iota(jnp.int32, (size, chans), 0), 2)).astype(F32)

    def spectrum(value):
        return dot(fwd, twice(value))

    def signal(spec):
        return dot(inv_hi, spec.astype(BF16))

    def times(a, b, conj):
        ar, ai, br, bi = a[:rows], a[rows:], b[:rows], b[rows:]
        first_row = lax.broadcasted_iota(jnp.int32, ai.shape, 0) == 0
        pure = ai * bi
        cross = jnp.where(first_row, 0.0, pure)
        if conj:
            return jnp.concatenate([ar * br + cross, jnp.where(first_row, pure, ar * bi - ai * br)], axis=0)
        return jnp.concatenate([ar * br - cross, jnp.where(first_row, pure, ar * bi + ai * br)], axis=0)

    member = (
        lax.broadcasted_iota(jnp.int32, (groups, chans), 1) // (chans // groups)
        == lax.broadcasted_iota(jnp.int32, (groups, chans), 0)
    ).astype(BF16)
    taps = lax.dot_general(
        filt_ref[...], member, (((0,), (0,)), ((), ())), preferred_element_type=F32
    ).astype(BF16)
    fs_ref[...] = spectrum(taps)
    xs_ref[...] = spectrum(x_ref[...])

    def mix():
        @pl.when(me == 0)
        def _():
            rim[...] = jnp.zeros_like(rim)

        @pl.when(me > 0)
        def _():
            rim_copy(me).wait_recv()

        xs = xs_ref[...] + sign * spectrum(rim[...])
        xs_ref[...] = xs
        mr = signal(times(fs_ref[...], xs, False)).astype(BF16)
        mr_ref[...] = mr
        u = product(ig_ref[...], mr)
        u_ref[...] = u
        u2 = twice(u)
        state = dot(mom_ref[tall:, :], u2).astype(BF16)
        du_send[1] = state
        span(me + 1, n, lambda j: du_copy(1, me, j).start())

    def share():
        u = u_ref[...]
        state = du_send[1]
        for j in range(count):
            total = jnp.zeros((8, chans), F32)
            for t in range(rows // 8):
                total += b_ref[j, 8 * t : 8 * t + 8, :] * u[8 * t : 8 * t + 8, :].astype(F32)
            g_ref[j : j + 1, :] = jnp.sum(total, axis=0, keepdims=True)
        lag = g_ref[...].astype(BF16)
        here = du_send[0]
        for j in range(n):
            at = slice(j * own, (j + 1) * own)
            p_send[j, :, :own] = state[:, at]
            p_send[j, :, own : 2 * own] = here[:, at]
            p_send[j, :, 2 * own : 3 * own] = lag[:, at]
        p_all[me] = p_send[me]
        others(lambda j: p_copy(j).start())

    mine = rate_ref[...]
    lanes = p_all.shape[2]
    fold = jnp.concatenate([mine] * (lanes // own), axis=1)
    for j in range(count):
        fold_ref[j] = jnp.exp(-float(node[j]) * fold)

    def gather(slot, carry, cols):
        row_ref[:, cols] = du_all[slot, :, cols].astype(F32)
        for j in range(count):
            carry += e_ref[j, :, cols] * row_ref[j : j + 1, cols]
        return carry

    def spread(state, which, cols):
        coef = resid[:, cols] * jnp.exp(-rates[:, cols]) * state
        for j in range(count):
            part = coef * e_ref[j, :, cols]
            total = part[:8]
            for g in range(1, parts):
                total += part[8 * g : 8 * g + 8]
            pb_ref[8 * j : 8 * j + 8, cols] = total
        high, low = split(pb_ref[:, cols])
        stack = [high, high, low]
        spare = size - 3 * high.shape[0]
        if spare:
            stack.append(jnp.zeros((spare, high.shape[1]), BF16))
        table = tab_ref[far_at + which * rows : far_at + (which + 1) * rows, :]
        far_ref[:, cols] = dot(table, jnp.concatenate(stack, axis=0))

    @pl.when(me == n - 1)
    def _():
        far_ref[...] = jnp.zeros_like(far_ref)

    nt = (((1,), (1,)), ((), ()))
    few = groups // sides
    turn = tab_ref[2 * size : 3 * size, :rows]
    def grad(low, top):
        cols = slice(128 * low, 128 * top)

        for side in reversed(range(low, top)):

            @pl.when(me // crowd == side)
            def _(side=side):
                take(rr_all, 3 + side, crowd - 1)

            @pl.when(me // crowd != side)
            def _(side=side):
                take(rr_all, 3 + side, crowd)

        for j in range(low * crowd, top * crowd):
            piece = rr_all[j]
            for g in range(parts):
                at = (slice(8 * g, 8 * g + 8), slice(j * own, (j + 1) * own))
                rates[at] = piece[:, g * own : (g + 1) * own]
                resid[at] = piece[:, (parts + g) * own : (parts + g + 1) * own]
        rate = rates[:, cols]
        weight = resid[:, cols]
        for j in range(count):
            e = jnp.exp(-float(node[j]) * rate)
            e_ref[j, :, cols] = e
            h_ref[j : j + 1, cols] = jnp.sum(weight * e, axis=0, keepdims=True)

        @pl.when(me < n - 1)
        def _():
            if top == sides:
                arrive(0, n - 1 - me)
            decay = jnp.exp(-rates[:, cols] * rows)
            start = jnp.zeros((modes, 128 * (top - low)), F32)
            spread(
                lax.fori_loop(0, n - 1 - me, lambda i, q: gather(n - 1 - i, q * decay, cols), start), 1, cols
            )

        chunk = 32
        for at in range(0, rows, chunk):
            here = slice(at, at + chunk)
            total = far_ref[here, cols]
            for j in range(count):
                total += h_ref[j : j + 1, cols] * b_ref[j, here, cols]
            back = total.astype(BF16)
            back_ref[here, cols] = back
            dv[here, cols] = product(back, ig_ref[here, cols])

    def tap(low, top):
        cols = slice(128 * low, 128 * top)
        spec = spectrum(dv[:, cols])
        ds_ref[:, cols] = spec
        cross = times(xs_ref[:, cols], spec, True).astype(BF16)
        sums = lax.dot_general(member[low * few : top * few, cols], cross, nt, preferred_element_type=F32)
        part = dot(sums.astype(BF16), turn).astype(BF16)
        for side in range(low, top):
            fg_send[side] = part[(side - low) * few : (side - low + 1) * few]
        others(lambda j: fg_copy(low, top, j).start())

    def hand():
        @pl.when(me > 0)
        def _():
            dv_copy(me - 1).start()

    @pl.when(me == n - 1)
    def _():
        mix()
        share()
        for side in reversed(range(sides)):
            grad(side, side + 1)
            if side == 0:
                hand()
            tap(side, side + 1)

    @pl.when(me == n - 2)
    def _():
        mix()
        share()
        grad(0, sides)
        hand()
        tap(0, sides)

    @pl.when((me > n // 2) & (me < n - 2))
    def _():
        mix()
        share()
        grad(0, sides)
        hand()
        tap(0, sides)

    @pl.when((me == n // 2) & (me < n - 2))
    def _():
        grad(0, sides)
        hand()
        mix()
        share()
        tap(0, sides)

    @pl.when((me < n // 2) & (me < n - 2))
    def _():
        grad(0, sides)
        hand()
        mix()
        tap(0, sides)
        share()

    fg_all[me] = fg_send[...]
    igg_ref[...] = product(back_ref[...], mr_ref[...])
    u2 = twice(u_ref[...])

    conv = jnp.zeros((rows, chans), F32)
    for j in range(count):
        conv += h_ref[j : j + 1, :] * dot(tab_ref[head + j * rows : head + (j + 1) * rows, :], u2)
    conv_ref[...] = conv

    @pl.when(me == 0)
    def _():
        far_ref[...] = jnp.zeros_like(far_ref)

    @pl.when(me > 0)
    def _():
        arrive(1, me)
        decay = jnp.exp(-rates[...] * rows)
        every = slice(0, chans)
        start = jnp.zeros((modes, chans), F32)
        spread(lax.fori_loop(0, me, lambda i, s: gather(i, s * decay, every), start), 0, every)

    conv = (conv_ref[...] + far_ref[...]).astype(BF16)
    ogg_ref[...] = product(oc_ref[...], conv)

    @pl.when(me == n - 1)
    def _():
        dv_rim[...] = jnp.zeros_like(dv_rim)

    @pl.when(me < n - 1)
    def _():
        dv_copy(me).wait_recv()

    ws = ds_ref[...] + sign * spectrum(dv_rim[...])
    xg_ref[...] = signal(times(fs_ref[...], ws, True)).astype(BF16)

    take(p_all, 1, n - 1)
    scale = 1.0 / math.sqrt(rows * n)
    hop = jnp.exp(-float(rows) * fold)

    for b in range(n):
        pf_ref[b] = p_all[b].astype(F32)

    def owner(b, carry):
        s, far, first, second, near0, near1 = carry
        zero = one = jnp.zeros((modes, lanes), F32)
        for j in range(count):
            part = fold_ref[j] * pf_ref[b, j : j + 1, :]
            zero += part
            one += float(node[j]) * part
        d0 = pltpu.roll(zero, lanes - own, 1)
        d1 = pltpu.roll(one, lanes - own, 1)
        first += d0 * s
        second += (d0 + d1) * s + d0 * far
        return s * hop + zero, (far + rows * s) * hop + one, first, second, near0 + zero, near1 + one

    empty = jnp.zeros((modes, lanes), F32)
    _, _, first, second, near0, near1 = lax.fori_loop(0, n, owner, (empty,) * 6, unroll=8 if n % 8 == 0 else 1)
    step = jnp.exp(-fold)
    first = (step * first + pltpu.roll(near0, lanes - 2 * own, 1))[:, :own]
    second = (step * second + pltpu.roll(near1, lanes - 2 * own, 1))[:, :own]
    gain = jnp.sqrt(2.0 * mine / modes)
    rg_ref[...] = gain * first * scale
    tg_ref[...] = res_ref[...] * gain * (0.5 * first - mine * second) * scale

    edge = (me == 0) | (me == n - 1)
    most = unit_ref.shape[0]

    @pl.when(edge)
    def _():
        part = unit_ref.at[pl.ds(0, most - rows * chans // 256)]
        pltpu.make_async_copy(part, part, all_sem.at[0]).wait()

    @pl.when(jnp.logical_not(edge))
    def _():
        pltpu.make_async_copy(unit_ref, unit_ref, all_sem.at[0]).wait()

    take(fg_all, 2, n - 1)
    total = jnp.sum(fg_all[...].astype(F32), axis=0) * scale
    for side in range(sides):
        fg_ref[side * few : (side + 1) * few, :] = total[side]


def store(*refs):
    sources, targets, (wide, small, sem) = refs[:6], refs[6:12], refs[12:]
    for source, target, which in zip(sources, targets, (0, 0, 0, 1, 2, 2)):
        pltpu.make_async_copy(source, target, sem.at[which]).start()
    pltpu.make_async_copy(wide, wide, sem.at[0]).wait()
    pltpu.make_async_copy(sources[3], targets[3], sem.at[1]).wait()
    pltpu.make_async_copy(small, small, sem.at[2]).wait()


def local(x, og, ig, oc, filt, res, rate):
    n = lax.axis_size(AXIS)
    rows, chans = x.shape
    modes, own = rate.shape
    groups = filt.shape[1]
    assert rows == filt.shape[0] and modes % 8 == 0 and 2 * (modes // 8) * own <= 128 and 128 % own == 0
    assert chans == 2 * rows and chans % 128 == 0 and n % (chans // 128) == 0
    sides = chans // 128
    fwd, inv, turn = dft_tables(rows)
    node, mom, up, lo, far = node_tables(rows)
    count = len(node)
    tall = mom.shape[0] // 2
    tab = np.concatenate([fwd, inv, turn, far, up])
    sent = 4 * 8 * 128 + 2 * (tall * 128 + groups * rows + tall * chans)
    hbm = pl.BlockSpec(memory_space=pltpu.HBM)
    vmem = pl.BlockSpec(memory_space=pltpu.VMEM)
    wide = (rows, chans)
    dma = pltpu.SemaphoreType.DMA
    out = pl.pallas_call(
        functools.partial(kernel, n, tuple(float(v) for v in node)),
        name="mixer",
        out_shape=(
            pltpu.VMEM(wide, BF16),
            pltpu.VMEM(wide, BF16),
            pltpu.VMEM(wide, BF16),
            pltpu.VMEM((groups, rows), F32),
            pltpu.VMEM((modes, own), F32),
            pltpu.VMEM((modes, own), F32),
        ),
        in_specs=[hbm] * 10,
        out_specs=(vmem,) * 6,
        scratch_shapes=[
            pltpu.VMEM(wide, BF16),
            pltpu.VMEM((8, 128), F32),
            pltpu.VMEM((n, 8, 128), F32),
            pltpu.VMEM((2, tall, chans), BF16),
            pltpu.VMEM((n, tall, chans), BF16),
            pltpu.VMEM(wide, BF16),
            pltpu.VMEM(wide, BF16),
            pltpu.VMEM((n, tall, 128), BF16),
            pltpu.VMEM((n, tall, 128), BF16),
            pltpu.VMEM((sides, groups // sides, rows), BF16),
            pltpu.VMEM((n, sides, groups // sides, rows), BF16),
            pltpu.VMEM((modes, chans), F32),
            pltpu.VMEM((modes, chans), F32),
            pltpu.VMEM((count, modes, 128), F32),
            pltpu.VMEM((n, tall, 128), F32),
            pltpu.VMEM((count, modes, chans), F32),
            pltpu.VMEM((tall, chans), F32),
            pltpu.VMEM((count,) + wide, F32),
            pltpu.VMEM((tall, chans), F32),
            pltpu.VMEM(wide, F32),
            pltpu.VMEM((8 * count, chans), F32),
            pltpu.VMEM((tall, chans), F32),
            pltpu.VMEM(wide, F32),
            pltpu.VMEM((2 * rows, chans), F32),
            pltpu.VMEM((2 * rows, chans), F32),
            pltpu.VMEM((2 * rows, chans), F32),
            pltpu.VMEM(wide, BF16),
            pltpu.VMEM(wide, BF16),
            pltpu.VMEM(wide, BF16),
            pltpu.VMEM((4 * rows + mom.shape[0], chans), BF16),
            pltpu.VMEM((groups, rows), BF16),
            pltpu.VMEM((2, modes, own), F32),
            pltpu.VMEM((tab.shape[0] + lo.shape[0], 2 * rows), BF16),
            pltpu.VMEM(((n - 1) * (sent // 512) + rows * chans // 128, 128), F32),
            dma((4,)),
            dma((1,)), dma((1,)), dma((3 + sides,)), dma((2,)),
        ],
        compiler_params=pltpu.CompilerParams(
            collective_id=0, has_side_effects=True, vmem_limit_bytes=GRANT
        ),
    )(
        x, og, ig, oc, filt.T, res, rate,
        jnp.asarray(mom), jnp.asarray(tab), jnp.asarray(lo),
    )
    xg, ogg, igg, fg, rg, tg = pl.pallas_call(
        store,
        name="store",
        out_shape=tuple(jax.ShapeDtypeStruct(o.shape, o.dtype) for o in out),
        in_specs=[vmem] * 6,
        out_specs=(hbm,) * 6,
        scratch_shapes=[pltpu.VMEM((3,) + wide, BF16), pltpu.VMEM((2, modes, own), F32), dma((3,))],
        compiler_params=pltpu.CompilerParams(vmem_limit_bytes=GRANT),
    )(*[pltpu.with_memory_space_constraint(o, pltpu.VMEM) for o in out])
    return xg, ogg, igg, fg.T, rg, tg


def solution(mesh):
    tokens = P("ctx", "ch")
    shared = P(None, "ch")
    owned = P(None, ("ch", "ctx"))
    return jax.shard_map(
        local,
        mesh=mesh,
        in_specs=(tokens, tokens, tokens, tokens, shared, owned, owned),
        out_specs=(tokens, tokens, tokens, shared, owned, owned),
        check_vma=False,
    )
```

```python
import functools
import math

import jax
import jax.numpy as jnp
import numpy as np
from jax import lax
from jax.experimental import pallas as pl
from jax.experimental.pallas import tpu as pltpu
from jax.sharding import PartitionSpec as P

MESH = pl.DeviceIdType.MESH
F32, BF16 = jnp.float32, jnp.bfloat16
AXIS = "ctx"
GRANT = 60 * 1024 * 1024
RATE_MAX = 0.03


def pair(table):
    table = table.astype(np.float32)
    high = table.astype(BF16)
    return high, (table - high.astype(np.float32)).astype(BF16)


def dft_tables(half):
    size = 2 * half
    k = np.arange(half)[:, None]
    t = np.arange(half)[None, :]
    angle = 2.0 * np.pi * (k * t % size) / size
    real, imag = np.cos(angle), -np.sin(angle)
    imag[0] = np.cos(np.pi * np.arange(half))
    forward = np.concatenate([real, imag], axis=0)
    gain = np.full((size, 1), 2.0 / size)
    gain[0] = gain[half] = 1.0 / size
    inverse = (forward * gain).T
    return (
        np.concatenate(pair(forward), axis=1),
        np.concatenate(pair(inverse), axis=0),
        np.concatenate(pair(inverse.T), axis=1),
    )


def basis(rows):
    t = np.arange(rows)
    probe = np.linspace(0.0, RATE_MAX, 97)[None, :]
    count = 4
    while True:
        j = np.arange(count)
        node = (rows - 1) / 2 * (1.0 - np.cos((2 * j + 1) * np.pi / (2 * count)))
        base = np.ones((rows, count))
        for a in range(count):
            for b in range(count):
                if a != b:
                    base[:, a] *= (t - node[b]) / (node[a] - node[b])
        error = np.abs(base @ np.exp(-probe * node[:, None]) - np.exp(-probe * t[:, None])).max()
        if error < 2.0**-23:
            return node, base
        count += 2


def node_tables(rows):
    node, base = basis(rows)
    count = len(node)
    pad = -count % 16
    moment = np.pad(base.T, ((0, pad), (0, 0)))
    turned = np.pad(base[::-1].T, ((0, pad), (0, 0)))
    lag = np.arange(rows)[:, None] - np.arange(rows)[None, :]
    lower = np.where((lag >= 0)[None], base.T[:, np.abs(lag)], 0.0)
    upper = np.swapaxes(lower, 1, 2)
    wide = np.repeat(np.concatenate([base, base[::-1]]), 8, axis=1)
    high, low = pair(wide)
    far = np.concatenate([high, high * 0, high * 0], axis=1)
    far[:, 8 * count : 16 * count], far[:, 16 * count :] = low, high
    far = np.pad(far, ((0, 0), (0, 2 * rows - far.shape[1])))
    return (
        node,
        np.concatenate(pair(np.concatenate([moment, turned])), axis=1),
        np.concatenate(pair(upper.reshape(count * rows, rows)), axis=1),
        np.concatenate(pair(lower.reshape(count * rows, rows)), axis=1),
        far,
    )


def dot(left, right):
    return jnp.dot(left, right, preferred_element_type=F32)


def split(value):
    high = value.astype(BF16)
    return high, (value - high.astype(F32)).astype(BF16)


def product(left, right):
    return (left.astype(F32) * right.astype(F32)).astype(BF16)


def twice(value):
    return jnp.concatenate([value, value], axis=0)


def kernel(
    n, node, x_hbm, og_hbm, ig_hbm, oc_hbm, filt_hbm, res_hbm, rate_hbm, mom_hbm, tab_hbm, lo_hbm,
    xg_ref, ogg_ref, igg_ref, fg_ref, rg_ref, tg_ref,
    rim, rr_send, rr_all, du_send, du_all, dv, dv_rim, p_send, p_all, fg_send, fg_all,
    rates, resid, fold_ref, pf_ref, e_ref, h_ref, b_ref, row_ref, far_ref, pb_ref, g_ref,
    conv_ref, xs_ref, fs_ref, ds_ref, mr_ref, u_ref, back_ref,
    wide_ref, filt_ref, own_ref, tab_ref, unit_ref, in_sem,
    rim_sem, dv_sem, all_sem, du_recv,
):
    me = lax.axis_index(AXIS)
    barrier = pltpu.get_barrier_semaphore()

    def others(act):
        def step(k, carry):
            act(lax.rem(me + jnp.where(me < n // 2, n - k, k), n))
            return carry

        lax.fori_loop(1, n, step, 0)

    def span(lo, hi, act):
        def step(j, carry):
            act(j)
            return carry

        lax.fori_loop(lo, hi, step, 0)

    others(lambda j: pl.semaphore_signal(barrier, inc=1, device_id={AXIS: j}, device_id_type=MESH))

    def load(src, dst, i):
        return pltpu.make_async_copy(src, dst, in_sem.at[i])

    rows, chans = x_hbm.shape
    wide = [wide_ref.at[pl.ds(i * rows, rows)] for i in range(4)]
    og_ref, oc_ref, x_ref, ig_ref = wide
    mom_ref = wide_ref.at[pl.ds(4 * rows, mom_hbm.shape[0])]
    head = tab_hbm.shape[0]
    load(rate_hbm, own_ref.at[0], 0).start()
    load(res_hbm, own_ref.at[1], 0).start()
    for src, dst in zip((og_hbm, oc_hbm, x_hbm, ig_hbm, mom_hbm), wide + [mom_ref]):
        load(src, dst, 1).start()
    load(tab_hbm, tab_ref.at[pl.ds(0, head)], 2).start()
    load(lo_hbm, tab_ref.at[pl.ds(head, lo_hbm.shape[0])], 2).start()
    load(filt_hbm, filt_ref, 3).start()
    rate_ref, res_ref = own_ref.at[0], own_ref.at[1]

    modes, own = rate_hbm.shape
    groups = filt_hbm.shape[0]
    parts = modes // 8
    count = len(node)
    tall = mom_hbm.shape[0] // 2
    size = 2 * rows
    sides = chans // 128
    crowd = n // sides

    def remote(src, dst, ssem, rsem, to):
        return pltpu.make_async_remote_copy(
            src_ref=src, dst_ref=dst, send_sem=ssem, recv_sem=rsem, device_id={AXIS: to}, device_id_type=MESH
        )

    def rr_copy(to):
        return remote(rr_send, rr_all.at[me], all_sem.at[0], all_sem.at[3 + me // crowd], to)

    def p_copy(to):
        return remote(p_send.at[to], p_all.at[me], all_sem.at[0], all_sem.at[1], to)

    def fg_copy(low, top, to):
        part = pl.ds(low, top - low)
        return remote(fg_send.at[part], fg_all.at[me, part], all_sem.at[0], all_sem.at[2], to)

    def du_copy(which, slot, to):
        return remote(du_send.at[which], du_all.at[slot], all_sem.at[0], du_recv.at[which], to)

    def rim_copy(to):
        return remote(x_ref, rim, all_sem.at[0], rim_sem.at[0], to)

    def dv_copy(to):
        return remote(dv, dv_rim, all_sem.at[0], dv_sem.at[0], to)

    def take(ref, i, many):
        part = ref.at[pl.ds(0, many)]
        pltpu.make_async_copy(part, part, all_sem.at[i]).wait()

    def arrive(which, many):
        for exact in range(1, n):

            @pl.when(many == exact)
            def _(exact=exact):
                part = du_all.at[pl.ds(0, exact)]
                pltpu.make_async_copy(part, part, du_recv.at[which]).wait()

    p_send[...] = jnp.zeros_like(p_send)
    g_ref[...] = jnp.zeros_like(g_ref)
    load(own_ref, own_ref, 0).wait()
    for g in range(parts):
        rr_send[:, g * own : (g + 1) * own] = rate_ref[8 * g : 8 * g + 8, :]
        gain = jnp.sqrt(2.0 * rate_ref[8 * g : 8 * g + 8, :] / modes)
        rr_send[:, (parts + g) * own : (parts + g + 1) * own] = res_ref[8 * g : 8 * g + 8, :] * gain

    load(wide_ref, wide_ref, 1).wait()
    dz2 = twice(product(og_ref[...], oc_ref[...]))
    du_send[0] = dot(mom_ref[:tall, :], dz2).astype(BF16)
    pl.semaphore_wait(barrier, n - 1)
    others(lambda j: rr_copy(j).start())

    @pl.when((me >= n // 2 - 1) & (me < n - 1))
    def _():
        rim_copy(me + 1).start()

    span(0, me, lambda j: du_copy(0, me, j).start())

    rr_all[me] = rr_send[...]
    load(tab_ref, tab_ref, 2).wait()
    far_at = 3 * size
    up_at = far_at + size
    for j in range(count):
        b_ref[j] = dot(tab_ref[up_at + j * rows : up_at + (j + 1) * rows, :], dz2)

    @pl.when(me < n // 2 - 1)
    def _():
        rim_copy(me + 1).start()

    load(filt_hbm, filt_ref, 3).wait()
    fwd = tab_ref[:size, :]
    inv_hi = tab_ref[size : size + rows, :]
    sign = (1 - 2 * lax.rem(lax.broadcasted_iota(jnp.int32, (size, chans), 0), 2)).astype(F32)

    def spectrum(value):
        return dot(fwd[:, :rows], value)

    def signal(spec):
        return dot(inv_hi, spec.astype(BF16))

    def times(a, b, conj):
        ar, ai, br, bi = a[:rows], a[rows:], b[:rows], b[rows:]
        first_row = lax.broadcasted_iota(jnp.int32, ai.shape, 0) == 0
        pure = ai * bi
        cross = jnp.where(first_row, 0.0, pure)
        if conj:
            return jnp.concatenate([ar * br + cross, jnp.where(first_row, pure, ar * bi - ai * br)], axis=0)
        return jnp.concatenate([ar * br - cross, jnp.where(first_row, pure, ar * bi + ai * br)], axis=0)

    member = (
        lax.broadcasted_iota(jnp.int32, (groups, chans), 1) // (chans // groups)
        == lax.broadcasted_iota(jnp.int32, (groups, chans), 0)
    ).astype(BF16)
    taps = lax.dot_general(
        filt_ref[...], member, (((0,), (0,)), ((), ())), preferred_element_type=F32
    ).astype(BF16)
    fs_ref[...] = spectrum(taps)
    xs_ref[...] = spectrum(x_ref[...])

    def mix():
        @pl.when(me == 0)
        def _():
            rim[...] = jnp.zeros_like(rim)

        @pl.when(me > 0)
        def _():
            rim_copy(me).wait_recv()

        xs = xs_ref[...] + sign * spectrum(rim[...])
        xs_ref[...] = xs
        mr = signal(times(fs_ref[...], xs, False)).astype(BF16)
        mr_ref[...] = mr
        u = product(ig_ref[...], mr)
        u_ref[...] = u
        u2 = twice(u)
        state = dot(mom_ref[tall:, :], u2).astype(BF16)
        du_send[1] = state
        span(me + 1, n, lambda j: du_copy(1, me, j).start())

    def share():
        u = u_ref[...]
        state = du_send[1]
        for j in range(count):
            total = jnp.zeros((8, chans), F32)
            for t in range(rows // 8):
                total += b_ref[j, 8 * t : 8 * t + 8, :] * u[8 * t : 8 * t + 8, :].astype(F32)
            g_ref[j : j + 1, :] = jnp.sum(total, axis=0, keepdims=True)
        lag = g_ref[...].astype(BF16)
        here = du_send[0]
        for j in range(n):
            at = slice(j * own, (j + 1) * own)
            p_send[j, :, :own] = state[:, at]
            p_send[j, :, own : 2 * own] = here[:, at]
            p_send[j, :, 2 * own : 3 * own] = lag[:, at]
        p_all[me] = p_send[me]
        others(lambda j: p_copy(j).start())

    mine = rate_ref[...]
    lanes = p_all.shape[2]
    fold = jnp.concatenate([mine] * (lanes // own), axis=1)
    for j in range(count):
        fold_ref[j] = jnp.exp(-float(node[j]) * fold)

    def gather(slot, carry, cols):
        row_ref[:, cols] = du_all[slot, :, cols].astype(F32)
        for j in range(count):
            carry += e_ref[j, :, cols] * row_ref[j : j + 1, cols]
        return carry

    def spread(state, which, cols):
        coef = resid[:, cols] * jnp.exp(-rates[:, cols]) * state
        for j in range(count):
            part = coef * e_ref[j, :, cols]
            total = part[:8]
            for g in range(1, parts):
                total += part[8 * g : 8 * g + 8]
            pb_ref[8 * j : 8 * j + 8, cols] = total
        high, low = split(pb_ref[:, cols])
        stack = [high, high, low]
        spare = size - 3 * high.shape[0]
        if spare:
            stack.append(jnp.zeros((spare, high.shape[1]), BF16))
        table = tab_ref[far_at + which * rows : far_at + (which + 1) * rows, :]
        far_ref[:, cols] = dot(table, jnp.concatenate(stack, axis=0))

    @pl.when(me == n - 1)
    def _():
        far_ref[...] = jnp.zeros_like(far_ref)

    nt = (((1,), (1,)), ((), ()))
    few = groups // sides
    turn = tab_ref[2 * size : 3 * size, :rows]
    def grad(low, top):
        cols = slice(128 * low, 128 * top)

        for side in reversed(range(low, top)):

            @pl.when(me // crowd == side)
            def _(side=side):
                take(rr_all, 3 + side, crowd - 1)

            @pl.when(me // crowd != side)
            def _(side=side):
                take(rr_all, 3 + side, crowd)

        for j in range(low * crowd, top * crowd):
            piece = rr_all[j]
            for g in range(parts):
                at = (slice(8 * g, 8 * g + 8), slice(j * own, (j + 1) * own))
                rates[at] = piece[:, g * own : (g + 1) * own]
                resid[at] = piece[:, (parts + g) * own : (parts + g + 1) * own]
        rate = rates[:, cols]
        weight = resid[:, cols]
        for j in range(count):
            e = jnp.exp(-float(node[j]) * rate)
            e_ref[j, :, cols] = e
            h_ref[j : j + 1, cols] = jnp.sum(weight * e, axis=0, keepdims=True)

        @pl.when(me < n - 1)
        def _():
            if top == sides:
                arrive(0, n - 1 - me)
            decay = jnp.exp(-rates[:, cols] * rows)
            start = jnp.zeros((modes, 128 * (top - low)), F32)
            spread(
                lax.fori_loop(0, n - 1 - me, lambda i, q: gather(n - 1 - i, q * decay, cols), start), 1, cols
            )

        chunk = 32
        for at in range(0, rows, chunk):
            here = slice(at, at + chunk)
            total = far_ref[here, cols]
            for j in range(count):
                total += h_ref[j : j + 1, cols] * b_ref[j, here, cols]
            back = total.astype(BF16)
            back_ref[here, cols] = back
            dv[here, cols] = product(back, ig_ref[here, cols])

    def tap(low, top):
        cols = slice(128 * low, 128 * top)
        spec = spectrum(dv[:, cols])
        ds_ref[:, cols] = spec
        cross = times(xs_ref[:, cols], spec, True).astype(BF16)
        sums = lax.dot_general(member[low * few : top * few, cols], cross, nt, preferred_element_type=F32)
        part = dot(sums.astype(BF16), turn).astype(BF16)
        for side in range(low, top):
            fg_send[side] = part[(side - low) * few : (side - low + 1) * few]
        others(lambda j: fg_copy(low, top, j).start())

    def hand():
        @pl.when(me > 0)
        def _():
            dv_copy(me - 1).start()

    @pl.when(me == n - 1)
    def _():
        mix()
        share()
        for side in reversed(range(sides)):
            grad(side, side + 1)
            tap(side, side + 1)
        hand()

    @pl.when(me == n - 2)
    def _():
        mix()
        share()
        grad(0, sides)
        tap(0, sides)
        hand()

    @pl.when((me > n // 2) & (me < n - 2))
    def _():
        mix()
        share()
        grad(0, sides)
        tap(0, sides)
        hand()

    @pl.when((me == n // 2) & (me < n - 2))
    def _():
        grad(0, sides)
        hand()
        mix()
        share()
        tap(0, sides)

    @pl.when((me < n // 2) & (me < n - 2))
    def _():
        grad(0, sides)
        hand()
        mix()
        tap(0, sides)
        share()

    fg_all[me] = fg_send[...]
    igg_ref[...] = product(back_ref[...], mr_ref[...])
    u2 = twice(u_ref[...])

    conv = jnp.zeros((rows, chans), F32)
    for j in range(count):
        conv += h_ref[j : j + 1, :] * dot(tab_ref[head + j * rows : head + (j + 1) * rows, :], u2)
    conv_ref[...] = conv

    @pl.when(me == 0)
    def _():
        far_ref[...] = jnp.zeros_like(far_ref)

    @pl.when(me > 0)
    def _():
        arrive(1, me)
        decay = jnp.exp(-rates[...] * rows)
        every = slice(0, chans)
        start = jnp.zeros((modes, chans), F32)
        spread(lax.fori_loop(0, me, lambda i, s: gather(i, s * decay, every), start), 0, every)

    conv = (conv_ref[...] + far_ref[...]).astype(BF16)
    ogg_ref[...] = product(oc_ref[...], conv)

    @pl.when(me == n - 1)
    def _():
        dv_rim[...] = jnp.zeros_like(dv_rim)

    @pl.when(me < n - 1)
    def _():
        dv_copy(me).wait_recv()

    ws = ds_ref[...] + sign * spectrum(dv_rim[...])
    xg_ref[...] = signal(times(fs_ref[...], ws, True)).astype(BF16)

    take(p_all, 1, n - 1)
    scale = 1.0 / math.sqrt(rows * n)
    hop = jnp.exp(-float(rows) * fold)

    for b in range(n):
        pf_ref[b] = p_all[b].astype(F32)

    def owner(b, carry):
        s, far, first, second, near0, near1 = carry
        zero = one = jnp.zeros((modes, lanes), F32)
        for j in range(count):
            part = fold_ref[j] * pf_ref[b, j : j + 1, :]
            zero += part
            one += float(node[j]) * part
        d0 = pltpu.roll(zero, lanes - own, 1)
        d1 = pltpu.roll(one, lanes - own, 1)
        first += d0 * s
        second += (d0 + d1) * s + d0 * far
        return s * hop + zero, (far + rows * s) * hop + one, first, second, near0 + zero, near1 + one

    empty = jnp.zeros((modes, lanes), F32)
    _, _, first, second, near0, near1 = lax.fori_loop(0, n, owner, (empty,) * 6, unroll=8 if n % 8 == 0 else 1)
    step = jnp.exp(-fold)
    first = (step * first + pltpu.roll(near0, lanes - 2 * own, 1))[:, :own]
    second = (step * second + pltpu.roll(near1, lanes - 2 * own, 1))[:, :own]
    gain = jnp.sqrt(2.0 * mine / modes)
    rg_ref[...] = gain * first * scale
    tg_ref[...] = res_ref[...] * gain * (0.5 * first - mine * second) * scale

    edge = (me == 0) | (me == n - 1)
    most = unit_ref.shape[0]

    @pl.when(edge)
    def _():
        part = unit_ref.at[pl.ds(0, most - rows * chans // 256)]
        pltpu.make_async_copy(part, part, all_sem.at[0]).wait()

    @pl.when(jnp.logical_not(edge))
    def _():
        pltpu.make_async_copy(unit_ref, unit_ref, all_sem.at[0]).wait()

    take(fg_all, 2, n - 1)
    total = jnp.sum(fg_all[...].astype(F32), axis=0) * scale
    for side in range(sides):
        fg_ref[side * few : (side + 1) * few, :] = total[side]


def store(*refs):
    sources, targets, (wide, small, sem) = refs[:6], refs[6:12], refs[12:]
    for source, target, which in zip(sources, targets, (0, 0, 0, 1, 2, 2)):
        pltpu.make_async_copy(source, target, sem.at[which]).start()
    pltpu.make_async_copy(wide, wide, sem.at[0]).wait()
    pltpu.make_async_copy(sources[3], targets[3], sem.at[1]).wait()
    pltpu.make_async_copy(small, small, sem.at[2]).wait()


def local(x, og, ig, oc, filt, res, rate):
    n = lax.axis_size(AXIS)
    rows, chans = x.shape
    modes, own = rate.shape
    groups = filt.shape[1]
    assert rows == filt.shape[0] and modes % 8 == 0 and 2 * (modes // 8) * own <= 128 and 128 % own == 0
    assert chans == 2 * rows and chans % 128 == 0 and n % (chans // 128) == 0
    sides = chans // 128
    fwd, inv, turn = dft_tables(rows)
    node, mom, up, lo, far = node_tables(rows)
    count = len(node)
    tall = mom.shape[0] // 2
    tab = np.concatenate([fwd, inv, turn, far, up])
    sent = 4 * 8 * 128 + 2 * (tall * 128 + groups * rows + tall * chans)
    hbm = pl.BlockSpec(memory_space=pltpu.HBM)
    vmem = pl.BlockSpec(memory_space=pltpu.VMEM)
    wide = (rows, chans)
    dma = pltpu.SemaphoreType.DMA
    out = pl.pallas_call(
        functools.partial(kernel, n, tuple(float(v) for v in node)),
        name="mixer",
        out_shape=(
            pltpu.VMEM(wide, BF16),
            pltpu.VMEM(wide, BF16),
            pltpu.VMEM(wide, BF16),
            pltpu.VMEM((groups, rows), F32),
            pltpu.VMEM((modes, own), F32),
            pltpu.VMEM((modes, own), F32),
        ),
        in_specs=[hbm] * 10,
        out_specs=(vmem,) * 6,
        scratch_shapes=[
            pltpu.VMEM(wide, BF16),
            pltpu.VMEM((8, 128), F32),
            pltpu.VMEM((n, 8, 128), F32),
            pltpu.VMEM((2, tall, chans), BF16),
            pltpu.VMEM((n, tall, chans), BF16),
            pltpu.VMEM(wide, BF16),
            pltpu.VMEM(wide, BF16),
            pltpu.VMEM((n, tall, 128), BF16),
            pltpu.VMEM((n, tall, 128), BF16),
            pltpu.VMEM((sides, groups // sides, rows), BF16),
            pltpu.VMEM((n, sides, groups // sides, rows), BF16),
            pltpu.VMEM((modes, chans), F32),
            pltpu.VMEM((modes, chans), F32),
            pltpu.VMEM((count, modes, 128), F32),
            pltpu.VMEM((n, tall, 128), F32),
            pltpu.VMEM((count, modes, chans), F32),
            pltpu.VMEM((tall, chans), F32),
            pltpu.VMEM((count,) + wide, F32),
            pltpu.VMEM((tall, chans), F32),
            pltpu.VMEM(wide, F32),
            pltpu.VMEM((8 * count, chans), F32),
            pltpu.VMEM((tall, chans), F32),
            pltpu.VMEM(wide, F32),
            pltpu.VMEM((2 * rows, chans), F32),
            pltpu.VMEM((2 * rows, chans), F32),
            pltpu.VMEM((2 * rows, chans), F32),
            pltpu.VMEM(wide, BF16),
            pltpu.VMEM(wide, BF16),
            pltpu.VMEM(wide, BF16),
            pltpu.VMEM((4 * rows + mom.shape[0], chans), BF16),
            pltpu.VMEM((groups, rows), BF16),
            pltpu.VMEM((2, modes, own), F32),
            pltpu.VMEM((tab.shape[0] + lo.shape[0], 2 * rows), BF16),
            pltpu.VMEM(((n - 1) * (sent // 512) + rows * chans // 128, 128), F32),
            dma((4,)),
            dma((1,)), dma((1,)), dma((3 + sides,)), dma((2,)),
        ],
        compiler_params=pltpu.CompilerParams(
            collective_id=0, has_side_effects=True, vmem_limit_bytes=GRANT
        ),
    )(
        x, og, ig, oc, filt.T, res, rate,
        jnp.asarray(mom), jnp.asarray(tab), jnp.asarray(lo),
    )
    xg, ogg, igg, fg, rg, tg = pl.pallas_call(
        store,
        name="store",
        out_shape=tuple(jax.ShapeDtypeStruct(o.shape, o.dtype) for o in out),
        in_specs=[vmem] * 6,
        out_specs=(hbm,) * 6,
        scratch_shapes=[pltpu.VMEM((3,) + wide, BF16), pltpu.VMEM((2, modes, own), F32), dma((3,))],
        compiler_params=pltpu.CompilerParams(vmem_limit_bytes=GRANT),
    )(*[pltpu.with_memory_space_constraint(o, pltpu.VMEM) for o in out])
    return xg, ogg, igg, fg.T, rg, tg


def solution(mesh):
    tokens = P("ctx", "ch")
    shared = P(None, "ch")
    owned = P(None, ("ch", "ctx"))
    return jax.shard_map(
        local,
        mesh=mesh,
        in_specs=(tokens, tokens, tokens, tokens, shared, owned, owned),
        out_specs=(tokens, tokens, tokens, shared, owned, owned),
        check_vma=False,
    )
```

```python
import functools
import math

import jax
import jax.numpy as jnp
import numpy as np
from jax import lax
from jax.experimental import pallas as pl
from jax.experimental.pallas import tpu as pltpu
from jax.sharding import PartitionSpec as P

MESH = pl.DeviceIdType.MESH
F32, BF16 = jnp.float32, jnp.bfloat16
AXIS = "ctx"
GRANT = 60 * 1024 * 1024
RATE_MAX = 0.03


def pair(table):
    table = table.astype(np.float32)
    high = table.astype(BF16)
    return high, (table - high.astype(np.float32)).astype(BF16)


def dft_tables(half):
    size = 2 * half
    k = np.arange(half)[:, None]
    t = np.arange(half)[None, :]
    angle = 2.0 * np.pi * (k * t % size) / size
    real, imag = np.cos(angle), -np.sin(angle)
    imag[0] = np.cos(np.pi * np.arange(half))
    forward = np.concatenate([real, imag], axis=0)
    gain = np.full((size, 1), 2.0 / size)
    gain[0] = gain[half] = 1.0 / size
    inverse = (forward * gain).T
    return (
        np.concatenate(pair(forward), axis=1),
        np.concatenate(pair(inverse), axis=0),
        np.concatenate(pair(inverse.T), axis=1),
    )


def basis(rows):
    t = np.arange(rows)
    probe = np.linspace(0.0, RATE_MAX, 97)[None, :]
    count = 4
    while True:
        j = np.arange(count)
        node = (rows - 1) / 2 * (1.0 - np.cos((2 * j + 1) * np.pi / (2 * count)))
        base = np.ones((rows, count))
        for a in range(count):
            for b in range(count):
                if a != b:
                    base[:, a] *= (t - node[b]) / (node[a] - node[b])
        error = np.abs(base @ np.exp(-probe * node[:, None]) - np.exp(-probe * t[:, None])).max()
        if error < 2.0**-23:
            return node, base
        count += 2


def node_tables(rows):
    node, base = basis(rows)
    count = len(node)
    pad = -count % 16
    moment = np.pad(base.T, ((0, pad), (0, 0)))
    turned = np.pad(base[::-1].T, ((0, pad), (0, 0)))
    lag = np.arange(rows)[:, None] - np.arange(rows)[None, :]
    lower = np.where((lag >= 0)[None], base.T[:, np.abs(lag)], 0.0)
    upper = np.swapaxes(lower, 1, 2)
    wide = np.repeat(np.concatenate([base, base[::-1]]), 8, axis=1)
    high, low = pair(wide)
    far = np.concatenate([high, high * 0, high * 0], axis=1)
    far[:, 8 * count : 16 * count], far[:, 16 * count :] = low, high
    far = np.pad(far, ((0, 0), (0, 2 * rows - far.shape[1])))
    return (
        node,
        np.concatenate(pair(np.concatenate([moment, turned])), axis=1),
        np.concatenate(pair(upper.reshape(count * rows, rows)), axis=1),
        np.concatenate(pair(lower.reshape(count * rows, rows)), axis=1),
        far,
    )


def dot(left, right):
    return jnp.dot(left, right, preferred_element_type=F32)


def split(value):
    high = value.astype(BF16)
    return high, (value - high.astype(F32)).astype(BF16)


def product(left, right):
    return (left.astype(F32) * right.astype(F32)).astype(BF16)


def twice(value):
    return jnp.concatenate([value, value], axis=0)


def kernel(
    n, node, x_hbm, og_hbm, ig_hbm, oc_hbm, filt_hbm, res_hbm, rate_hbm, mom_hbm, tab_hbm, lo_hbm,
    xg_ref, ogg_ref, igg_ref, fg_ref, rg_ref, tg_ref,
    rim, rr_send, rr_all, du_send, du_all, dv, dv_rim, p_send, p_all, fg_send, fg_all,
    rates, resid, fold_ref, pf_ref, e_ref, h_ref, b_ref, row_ref, far_ref, pb_ref, g_ref,
    conv_ref, xs_ref, fs_ref, ds_ref, mr_ref, u_ref, back_ref,
    wide_ref, filt_ref, own_ref, tab_ref, unit_ref, in_sem,
    rim_sem, dv_sem, all_sem, du_recv,
):
    me = lax.axis_index(AXIS)
    barrier = pltpu.get_barrier_semaphore()

    def others(act):
        def step(k, carry):
            act(lax.rem(me + jnp.where(me < n // 2, n - k, k), n))
            return carry

        lax.fori_loop(1, n, step, 0)

    def span(lo, hi, act):
        def step(j, carry):
            act(j)
            return carry

        lax.fori_loop(lo, hi, step, 0)

    others(lambda j: pl.semaphore_signal(barrier, inc=1, device_id={AXIS: j}, device_id_type=MESH))

    def load(src, dst, i):
        return pltpu.make_async_copy(src, dst, in_sem.at[i])

    rows, chans = x_hbm.shape
    wide = [wide_ref.at[pl.ds(i * rows, rows)] for i in range(4)]
    og_ref, oc_ref, x_ref, ig_ref = wide
    mom_ref = wide_ref.at[pl.ds(4 * rows, mom_hbm.shape[0])]
    head = tab_hbm.shape[0]
    load(rate_hbm, own_ref.at[0], 0).start()
    load(res_hbm, own_ref.at[1], 0).start()
    for src, dst in zip((og_hbm, oc_hbm, x_hbm, ig_hbm, mom_hbm), wide + [mom_ref]):
        load(src, dst, 1).start()
    load(tab_hbm, tab_ref.at[pl.ds(0, head)], 2).start()
    load(lo_hbm, tab_ref.at[pl.ds(head, lo_hbm.shape[0])], 2).start()
    load(filt_hbm, filt_ref, 3).start()
    rate_ref, res_ref = own_ref.at[0], own_ref.at[1]

    modes, own = rate_hbm.shape
    groups = filt_hbm.shape[0]
    parts = modes // 8
    count = len(node)
    tall = mom_hbm.shape[0] // 2
    size = 2 * rows
    sides = chans // 128
    crowd = n // sides

    def remote(src, dst, ssem, rsem, to):
        return pltpu.make_async_remote_copy(
            src_ref=src, dst_ref=dst, send_sem=ssem, recv_sem=rsem, device_id={AXIS: to}, device_id_type=MESH
        )

    def rr_copy(to):
        return remote(rr_send, rr_all.at[me], all_sem.at[0], all_sem.at[3 + me // crowd], to)

    def p_copy(to):
        return remote(p_send.at[to], p_all.at[me], all_sem.at[0], all_sem.at[1], to)

    def fg_copy(low, top, to):
        part = pl.ds(low, top - low)
        return remote(fg_send.at[part], fg_all.at[me, part], all_sem.at[0], all_sem.at[2], to)

    def du_copy(which, slot, to):
        return remote(du_send.at[which], du_all.at[slot], all_sem.at[0], du_recv.at[which], to)

    def rim_copy(to):
        return remote(x_ref, rim, all_sem.at[0], rim_sem.at[0], to)

    def dv_copy(to):
        return remote(dv, dv_rim, all_sem.at[0], dv_sem.at[0], to)

    def take(ref, i, many):
        part = ref.at[pl.ds(0, many)]
        pltpu.make_async_copy(part, part, all_sem.at[i]).wait()

    def arrive(which, many):
        for exact in range(1, n):

            @pl.when(many == exact)
            def _(exact=exact):
                part = du_all.at[pl.ds(0, exact)]
                pltpu.make_async_copy(part, part, du_recv.at[which]).wait()

    p_send[...] = jnp.zeros_like(p_send)
    g_ref[...] = jnp.zeros_like(g_ref)
    load(own_ref, own_ref, 0).wait()
    for g in range(parts):
        rr_send[:, g * own : (g + 1) * own] = rate_ref[8 * g : 8 * g + 8, :]
        gain = jnp.sqrt(2.0 * rate_ref[8 * g : 8 * g + 8, :] / modes)
        rr_send[:, (parts + g) * own : (parts + g + 1) * own] = res_ref[8 * g : 8 * g + 8, :] * gain

    load(wide_ref, wide_ref, 1).wait()
    dz2 = twice(product(og_ref[...], oc_ref[...]))
    du_send[0] = dot(mom_ref[:tall, :], dz2).astype(BF16)
    pl.semaphore_wait(barrier, n - 1)
    others(lambda j: rr_copy(j).start())

    @pl.when((me >= n // 2 - 1) & (me < n - 1))
    def _():
        rim_copy(me + 1).start()

    span(0, me, lambda j: du_copy(0, me, j).start())

    rr_all[me] = rr_send[...]
    load(tab_ref, tab_ref, 2).wait()
    far_at = 3 * size
    up_at = far_at + size
    for j in range(count):
        b_ref[j] = dot(tab_ref[up_at + j * rows : up_at + (j + 1) * rows, :], dz2)

    @pl.when(me < n // 2 - 1)
    def _():
        rim_copy(me + 1).start()

    load(filt_hbm, filt_ref, 3).wait()
    fwd = tab_ref[:size, :]
    inv_hi = tab_ref[size : size + rows, :]
    sign = (1 - 2 * lax.rem(lax.broadcasted_iota(jnp.int32, (size, chans), 0), 2)).astype(F32)

    def spectrum(value):
        return dot(fwd[:, :rows], value)

    def signal(spec):
        return dot(inv_hi, spec.astype(BF16))

    def times(a, b, conj):
        ar, ai, br, bi = a[:rows], a[rows:], b[:rows], b[rows:]
        first_row = lax.broadcasted_iota(jnp.int32, ai.shape, 0) == 0
        pure = ai * bi
        cross = jnp.where(first_row, 0.0, pure)
        if conj:
            return jnp.concatenate([ar * br + cross, jnp.where(first_row, pure, ar * bi - ai * br)], axis=0)
        return jnp.concatenate([ar * br - cross, jnp.where(first_row, pure, ar * bi + ai * br)], axis=0)

    member = (
        lax.broadcasted_iota(jnp.int32, (groups, chans), 1) // (chans // groups)
        == lax.broadcasted_iota(jnp.int32, (groups, chans), 0)
    ).astype(BF16)
    taps = lax.dot_general(
        filt_ref[...], member, (((0,), (0,)), ((), ())), preferred_element_type=F32
    ).astype(BF16)
    fs_ref[...] = spectrum(taps)
    xs_ref[...] = spectrum(x_ref[...])

    def mix():
        @pl.when(me == 0)
        def _():
            rim[...] = jnp.zeros_like(rim)

        @pl.when(me > 0)
        def _():
            rim_copy(me).wait_recv()

        xs = xs_ref[...] + sign * spectrum(rim[...])
        xs_ref[...] = xs
        mr = signal(times(fs_ref[...], xs, False)).astype(BF16)
        mr_ref[...] = mr
        u = product(ig_ref[...], mr)
        u_ref[...] = u
        u2 = twice(u)
        state = dot(mom_ref[tall:, :], u2).astype(BF16)
        du_send[1] = state
        span(me + 1, n, lambda j: du_copy(1, me, j).start())

    def share():
        u = u_ref[...]
        state = du_send[1]
        for j in range(count):
            total = jnp.zeros((8, chans), F32)
            for t in range(rows // 8):
                total += b_ref[j, 8 * t : 8 * t + 8, :] * u[8 * t : 8 * t + 8, :].astype(F32)
            g_ref[j : j + 1, :] = jnp.sum(total, axis=0, keepdims=True)
        lag = g_ref[...].astype(BF16)
        here = du_send[0]
        for j in range(n):
            at = slice(j * own, (j + 1) * own)
            p_send[j, :, :own] = state[:, at]
            p_send[j, :, own : 2 * own] = here[:, at]
            p_send[j, :, 2 * own : 3 * own] = lag[:, at]
        p_all[me] = p_send[me]
        others(lambda j: p_copy(j).start())

    mine = rate_ref[...]
    lanes = p_all.shape[2]
    fold = jnp.concatenate([mine] * (lanes // own), axis=1)
    for j in range(count):
        fold_ref[j] = jnp.exp(-float(node[j]) * fold)

    def gather(slot, carry, cols):
        row_ref[:, cols] = du_all[slot, :, cols].astype(F32)
        for j in range(count):
            carry += e_ref[j, :, cols] * row_ref[j : j + 1, cols]
        return carry

    def spread(state, which, cols):
        coef = resid[:, cols] * jnp.exp(-rates[:, cols]) * state
        for j in range(count):
            part = coef * e_ref[j, :, cols]
            total = part[:8]
            for g in range(1, parts):
                total += part[8 * g : 8 * g + 8]
            pb_ref[8 * j : 8 * j + 8, cols] = total
        high, low = split(pb_ref[:, cols])
        stack = [high, high, low]
        spare = size - 3 * high.shape[0]
        if spare:
            stack.append(jnp.zeros((spare, high.shape[1]), BF16))
        table = tab_ref[far_at + which * rows : far_at + (which + 1) * rows, :]
        far_ref[:, cols] = dot(table, jnp.concatenate(stack, axis=0))

    @pl.when(me == n - 1)
    def _():
        far_ref[...] = jnp.zeros_like(far_ref)

    nt = (((1,), (1,)), ((), ()))
    few = groups // sides
    turn = tab_ref[2 * size : 3 * size, :rows]
    def grad(low, top):
        cols = slice(128 * low, 128 * top)

        for side in reversed(range(low, top)):

            @pl.when(me // crowd == side)
            def _(side=side):
                take(rr_all, 3 + side, crowd - 1)

            @pl.when(me // crowd != side)
            def _(side=side):
                take(rr_all, 3 + side, crowd)

        for j in range(low * crowd, top * crowd):
            piece = rr_all[j]
            for g in range(parts):
                at = (slice(8 * g, 8 * g + 8), slice(j * own, (j + 1) * own))
                rates[at] = piece[:, g * own : (g + 1) * own]
                resid[at] = piece[:, (parts + g) * own : (parts + g + 1) * own]
        rate = rates[:, cols]
        weight = resid[:, cols]
        for j in range(count):
            e = jnp.exp(-float(node[j]) * rate)
            e_ref[j, :, cols] = e
            h_ref[j : j + 1, cols] = jnp.sum(weight * e, axis=0, keepdims=True)

        @pl.when(me < n - 1)
        def _():
            if top == sides:
                arrive(0, n - 1 - me)
            decay = jnp.exp(-rates[:, cols] * rows)
            start = jnp.zeros((modes, 128 * (top - low)), F32)
            spread(
                lax.fori_loop(0, n - 1 - me, lambda i, q: gather(n - 1 - i, q * decay, cols), start), 1, cols
            )

        chunk = 32
        for at in range(0, rows, chunk):
            here = slice(at, at + chunk)
            total = far_ref[here, cols]
            for j in range(count):
                total += h_ref[j : j + 1, cols] * b_ref[j, here, cols]
            back = total.astype(BF16)
            back_ref[here, cols] = back
            dv[here, cols] = product(back, ig_ref[here, cols])

    def tap(low, top):
        cols = slice(128 * low, 128 * top)
        spec = spectrum(dv[:, cols])
        ds_ref[:, cols] = spec
        cross = times(xs_ref[:, cols], spec, True).astype(BF16)
        sums = lax.dot_general(member[low * few : top * few, cols], cross, nt, preferred_element_type=F32)
        part = dot(sums.astype(BF16), turn).astype(BF16)
        for side in range(low, top):
            fg_send[side] = part[(side - low) * few : (side - low + 1) * few]
        others(lambda j: fg_copy(low, top, j).start())

    def hand():
        @pl.when(me > 0)
        def _():
            dv_copy(me - 1).start()

    @pl.when(me == n - 1)
    def _():
        mix()
        share()
        for side in reversed(range(sides)):
            grad(side, side + 1)
            tap(side, side + 1)
        hand()

    @pl.when(me == n - 2)
    def _():
        mix()
        share()
        grad(0, sides)
        tap(0, sides)
        hand()

    @pl.when((me > n // 2) & (me < n - 2))
    def _():
        mix()
        share()
        grad(0, sides)
        tap(0, sides)
        hand()

    @pl.when((me == n // 2) & (me < n - 2))
    def _():
        grad(0, sides)
        mix()
        share()
        tap(0, sides)
        hand()

    @pl.when((me < n // 2) & (me < n - 2))
    def _():
        grad(0, sides)
        hand()
        mix()
        tap(0, sides)
        share()

    fg_all[me] = fg_send[...]
    igg_ref[...] = product(back_ref[...], mr_ref[...])
    u2 = twice(u_ref[...])

    conv = jnp.zeros((rows, chans), F32)
    for j in range(count):
        conv += h_ref[j : j + 1, :] * dot(tab_ref[head + j * rows : head + (j + 1) * rows, :], u2)
    conv_ref[...] = conv

    @pl.when(me == 0)
    def _():
        far_ref[...] = jnp.zeros_like(far_ref)

    @pl.when(me > 0)
    def _():
        arrive(1, me)
        decay = jnp.exp(-rates[...] * rows)
        every = slice(0, chans)
        start = jnp.zeros((modes, chans), F32)
        spread(lax.fori_loop(0, me, lambda i, s: gather(i, s * decay, every), start), 0, every)

    conv = (conv_ref[...] + far_ref[...]).astype(BF16)
    ogg_ref[...] = product(oc_ref[...], conv)

    @pl.when(me == n - 1)
    def _():
        dv_rim[...] = jnp.zeros_like(dv_rim)

    @pl.when(me < n - 1)
    def _():
        dv_copy(me).wait_recv()

    ws = ds_ref[...] + sign * spectrum(dv_rim[...])
    xg_ref[...] = signal(times(fs_ref[...], ws, True)).astype(BF16)

    take(p_all, 1, n - 1)
    scale = 1.0 / math.sqrt(rows * n)
    hop = jnp.exp(-float(rows) * fold)

    for b in range(n):
        pf_ref[b] = p_all[b].astype(F32)

    def owner(b, carry):
        s, far, first, second, near0, near1 = carry
        zero = one = jnp.zeros((modes, lanes), F32)
        for j in range(count):
            part = fold_ref[j] * pf_ref[b, j : j + 1, :]
            zero += part
            one += float(node[j]) * part
        d0 = pltpu.roll(zero, lanes - own, 1)
        d1 = pltpu.roll(one, lanes - own, 1)
        first += d0 * s
        second += (d0 + d1) * s + d0 * far
        return s * hop + zero, (far + rows * s) * hop + one, first, second, near0 + zero, near1 + one

    empty = jnp.zeros((modes, lanes), F32)
    _, _, first, second, near0, near1 = lax.fori_loop(0, n, owner, (empty,) * 6, unroll=8 if n % 8 == 0 else 1)
    step = jnp.exp(-fold)
    first = (step * first + pltpu.roll(near0, lanes - 2 * own, 1))[:, :own]
    second = (step * second + pltpu.roll(near1, lanes - 2 * own, 1))[:, :own]
    gain = jnp.sqrt(2.0 * mine / modes)
    rg_ref[...] = gain * first * scale
    tg_ref[...] = res_ref[...] * gain * (0.5 * first - mine * second) * scale

    edge = (me == 0) | (me == n - 1)
    most = unit_ref.shape[0]

    @pl.when(edge)
    def _():
        part = unit_ref.at[pl.ds(0, most - rows * chans // 256)]
        pltpu.make_async_copy(part, part, all_sem.at[0]).wait()

    @pl.when(jnp.logical_not(edge))
    def _():
        pltpu.make_async_copy(unit_ref, unit_ref, all_sem.at[0]).wait()

    take(fg_all, 2, n - 1)
    total = jnp.sum(fg_all[...].astype(F32), axis=0) * scale
    for side in range(sides):
        fg_ref[side * few : (side + 1) * few, :] = total[side]


def store(*refs):
    sources, targets, (wide, small, sem) = refs[:6], refs[6:12], refs[12:]
    for source, target, which in zip(sources, targets, (0, 0, 0, 1, 2, 2)):
        pltpu.make_async_copy(source, target, sem.at[which]).start()
    pltpu.make_async_copy(wide, wide, sem.at[0]).wait()
    pltpu.make_async_copy(sources[3], targets[3], sem.at[1]).wait()
    pltpu.make_async_copy(small, small, sem.at[2]).wait()


def local(x, og, ig, oc, filt, res, rate):
    n = lax.axis_size(AXIS)
    rows, chans = x.shape
    modes, own = rate.shape
    groups = filt.shape[1]
    assert rows == filt.shape[0] and modes % 8 == 0 and 2 * (modes // 8) * own <= 128 and 128 % own == 0
    assert chans == 2 * rows and chans % 128 == 0 and n % (chans // 128) == 0
    sides = chans // 128
    fwd, inv, turn = dft_tables(rows)
    node, mom, up, lo, far = node_tables(rows)
    count = len(node)
    tall = mom.shape[0] // 2
    tab = np.concatenate([fwd, inv, turn, far, up])
    sent = 4 * 8 * 128 + 2 * (tall * 128 + groups * rows + tall * chans)
    hbm = pl.BlockSpec(memory_space=pltpu.HBM)
    vmem = pl.BlockSpec(memory_space=pltpu.VMEM)
    wide = (rows, chans)
    dma = pltpu.SemaphoreType.DMA
    out = pl.pallas_call(
        functools.partial(kernel, n, tuple(float(v) for v in node)),
        name="mixer",
        out_shape=(
            pltpu.VMEM(wide, BF16),
            pltpu.VMEM(wide, BF16),
            pltpu.VMEM(wide, BF16),
            pltpu.VMEM((groups, rows), F32),
            pltpu.VMEM((modes, own), F32),
            pltpu.VMEM((modes, own), F32),
        ),
        in_specs=[hbm] * 10,
        out_specs=(vmem,) * 6,
        scratch_shapes=[
            pltpu.VMEM(wide, BF16),
            pltpu.VMEM((8, 128), F32),
            pltpu.VMEM((n, 8, 128), F32),
            pltpu.VMEM((2, tall, chans), BF16),
            pltpu.VMEM((n, tall, chans), BF16),
            pltpu.VMEM(wide, BF16),
            pltpu.VMEM(wide, BF16),
            pltpu.VMEM((n, tall, 128), BF16),
            pltpu.VMEM((n, tall, 128), BF16),
            pltpu.VMEM((sides, groups // sides, rows), BF16),
            pltpu.VMEM((n, sides, groups // sides, rows), BF16),
            pltpu.VMEM((modes, chans), F32),
            pltpu.VMEM((modes, chans), F32),
            pltpu.VMEM((count, modes, 128), F32),
            pltpu.VMEM((n, tall, 128), F32),
            pltpu.VMEM((count, modes, chans), F32),
            pltpu.VMEM((tall, chans), F32),
            pltpu.VMEM((count,) + wide, F32),
            pltpu.VMEM((tall, chans), F32),
            pltpu.VMEM(wide, F32),
            pltpu.VMEM((8 * count, chans), F32),
            pltpu.VMEM((tall, chans), F32),
            pltpu.VMEM(wide, F32),
            pltpu.VMEM((2 * rows, chans), F32),
            pltpu.VMEM((2 * rows, chans), F32),
            pltpu.VMEM((2 * rows, chans), F32),
            pltpu.VMEM(wide, BF16),
            pltpu.VMEM(wide, BF16),
            pltpu.VMEM(wide, BF16),
            pltpu.VMEM((4 * rows + mom.shape[0], chans), BF16),
            pltpu.VMEM((groups, rows), BF16),
            pltpu.VMEM((2, modes, own), F32),
            pltpu.VMEM((tab.shape[0] + lo.shape[0], 2 * rows), BF16),
            pltpu.VMEM(((n - 1) * (sent // 512) + rows * chans // 128, 128), F32),
            dma((4,)),
            dma((1,)), dma((1,)), dma((3 + sides,)), dma((2,)),
        ],
        compiler_params=pltpu.CompilerParams(
            collective_id=0, has_side_effects=True, vmem_limit_bytes=GRANT
        ),
    )(
        x, og, ig, oc, filt.T, res, rate,
        jnp.asarray(mom), jnp.asarray(tab), jnp.asarray(lo),
    )
    xg, ogg, igg, fg, rg, tg = pl.pallas_call(
        store,
        name="store",
        out_shape=tuple(jax.ShapeDtypeStruct(o.shape, o.dtype) for o in out),
        in_specs=[vmem] * 6,
        out_specs=(hbm,) * 6,
        scratch_shapes=[pltpu.VMEM((3,) + wide, BF16), pltpu.VMEM((2, modes, own), F32), dma((3,))],
        compiler_params=pltpu.CompilerParams(vmem_limit_bytes=GRANT),
    )(*[pltpu.with_memory_space_constraint(o, pltpu.VMEM) for o in out])
    return xg, ogg, igg, fg.T, rg, tg


def solution(mesh):
    tokens = P("ctx", "ch")
    shared = P(None, "ch")
    owned = P(None, ("ch", "ctx"))
    return jax.shard_map(
        local,
        mesh=mesh,
        in_specs=(tokens, tokens, tokens, tokens, shared, owned, owned),
        out_specs=(tokens, tokens, tokens, shared, owned, owned),
        check_vma=False,
    )
```
